32 devices in a mesh: dp: 8 (over z, x), tensor: 4 (over y, core).
Axes of the slice: x: 2, y: 2, z: 4, core: 2. Of those that a mesh axis runs over, the one named last changes fastest.
Arguments:
- layer_in: bfloat16 [1024, 8, 1024], P('tensor', 'dp'), may hold values from -6 to 6
- out_grad: bfloat16 [1024, 8, 1024], P('tensor', 'dp'), may hold values from -6 to 6
- lengths: int32 [8], P('dp'), may hold values from 512 to 1024, as said below
- mamba_x: float32 [1024, 1536], P('dp', 'tensor'), may hold values from -0.1875 to 0.1875
- mamba_z: float32 [1024, 1536], P('dp', 'tensor'), may hold values from -0.1875 to 0.1875
- mamba_step: float32 [1024, 24], P('dp', 'tensor'), may hold values from -0.1875 to 0.1875
- query_proj: float32 [1024, 512], P('dp', 'tensor'), may hold values from -0.25 to 0.25
- key_proj: float32 [1024, 256], P('dp', 'tensor'), may hold values from -0.25 to 0.25
- value_proj: float32 [1024, 256], P('dp', 'tensor'), may hold values from -0.1875 to 0.1875
- mamba_out: float32 [1536, 1024], P('tensor', 'dp'), may hold values from -0.15625 to 0.15625
- attend_out: float32 [512, 1024], P('tensor', 'dp'), may hold values from -3 to 3
- mlp_gate: float32 [1024, 2048], P('dp', 'tensor'), may hold values from -0.1875 to 0.1875
- mlp_up: float32 [1024, 2048], P('dp', 'tensor'), may hold values from -0.1875 to 0.1875
- mlp_down: float32 [2048, 1024], P('tensor', 'dp'), may hold values from -0.125 to 0.125
- state_proj: float32 [1024, 256], P(('dp', 'tensor')), may hold values from -0.1875 to 0.1875
- conv_state: float32 [5, 256], P(None, ('dp', 'tensor')), may hold values from -3 to 3
- norm_gains: float32 [2, 1024], P(None, ('dp', 'tensor')), may hold values from 0.5 to 1.5
- conv_mamba: float32 [5, 1536], P(None, 'tensor'), may hold values from -3 to 3
- step_bias: float32 [24], P('tensor'), may hold values from -3 to -0.5
- decay_log: float32 [24], P('tensor'), may hold values from -4 to 1
- skip_gain: float32 [24], P('tensor'), may hold values from 0.5 to 1.5
Outputs:
- layer_out: bfloat16 [1024, 8, 1024], P('tensor', 'dp')
- in_grad: bfloat16 [1024, 8, 1024], P('tensor', 'dp')
- mamba_x_grad: float32 [1024, 1536], P('dp', 'tensor')
- mamba_z_grad: float32 [1024, 1536], P('dp', 'tensor')
- mamba_step_grad: float32 [1024, 24], P('dp', 'tensor')
- query_proj_grad: float32 [1024, 512], P('dp', 'tensor')
- key_proj_grad: float32 [1024, 256], P('dp', 'tensor')
- value_proj_grad: float32 [1024, 256], P('dp', 'tensor')
- mamba_out_grad: float32 [1536, 1024], P('tensor', 'dp')
- attend_out_grad: float32 [512, 1024], P('tensor', 'dp')
- mlp_gate_grad: float32 [1024, 2048], P('dp', 'tensor')
- mlp_up_grad: float32 [1024, 2048], P('dp', 'tensor')
- mlp_down_grad: float32 [2048, 1024], P('tensor', 'dp')
- state_proj_grad: float32 [1024, 256], P(('dp', 'tensor'))
- conv_state_grad: float32 [5, 256], P(None, ('dp', 'tensor'))
- norm_gains_grad: float32 [2, 1024], P(None, ('dp', 'tensor'))
- conv_mamba_grad: float32 [5, 1536], P(None, 'tensor')
- step_bias_grad: float32 [24], P('tensor')
- decay_log_grad: float32 [24], P('tensor')
- skip_gain_grad: float32 [24], P('tensor')
The draws below stay inside these ranges and needn't reach their ends.
Inputs may be any that keep to these rules, and one draw needn't show every extreme that they name: `lengths`: the valid tokens of a sequence are its first ones; in every draw one sequence has exactly 1024 and another exactly half of 1024.
All inputs are finite; a program needn't handle non-finite values.
Results may differ from the reference program's by a relative error of at most 0.019.
Values may be sent and summed in bfloat16 or wider, within the bound.
No kernel may reach another device: no remote copies, remote signals or barrier semaphores. Data moves between devices by JAX's collectives and lax.ppermute only.
A program may use at most 128 MiB of HBM per device.

```python
import jax
import jax.numpy as jnp
from jax import lax

D = 1024
FF = 2048
MH = 24
P_SIZE = 64
N = 128
H = 8
KV = 4
HD = 64
KCONV = 4
LEN = 1024
ATT_BLOCK = 512
SPAN = 256
SEQS = 8
N_TENSOR = 4


def draw_lengths(key, part):
    first, second, third = jax.random.split(key, 3)
    values = jax.random.randint(first, (SEQS,), LEN // 2, LEN + 1)
    longest = jax.random.randint(second, (), 0, SEQS)
    offset = jax.random.randint(third, (), 1, SEQS)
    shortest = (longest + offset) % SEQS
    places = jnp.arange(SEQS)
    values = jnp.where(places == longest, LEN, values)
    values = jnp.where(places == shortest, LEN // 2, values)
    return values.astype(jnp.int32)


def levels(key, shape, cuts, least, largest):
    factor_of, own = 1.0, jax.random.fold_in(key, 6)
    for axis_at, shards_of in cuts:
        heights = jnp.exp(jax.random.uniform(jax.random.fold_in(own, axis_at), (shards_of,), jnp.float32, least / len(cuts), largest / len(cuts)))
        factor_of = factor_of * jnp.repeat(heights, shape[axis_at] // shards_of).reshape([-1 if axis == axis_at else 1 for axis in range(len(shape))])
    return factor_of


def scatter_about(own_key, shape, scale, most, cuts=(), held_as=jnp.bfloat16):
    array = scale * jax.random.normal(own_key, shape, jnp.float32)
    if cuts:
        array = array * levels(own_key, shape, cuts, -0.22, 0.18)
    return jnp.clip(array, -most, most).astype(held_as)


def setup_inputs(seed: int = 0) -> dict:
    key_of = jax.random.split(jax.random.key(seed), 22)
    return {
        "layer_in": scatter_about(key_of[0], (LEN, SEQS, D), 1.0, 6.0, ((0, 4), (1, 8))),
        "out_grad": scatter_about(key_of[1], (LEN, SEQS, D), 1.0, 6.0, ((0, 4), (1, 8))),
        "lengths": draw_lengths(jax.random.fold_in(key_of[21], 71), 0),
        "mamba_x": scatter_about(key_of[3], (D, MH * P_SIZE), D ** -0.5, 0.1875, ((0, 8), (1, 4)), jnp.float32),
        "mamba_z": scatter_about(key_of[4], (D, MH * P_SIZE), D ** -0.5, 0.1875, ((0, 8), (1, 4)), jnp.float32),
        "mamba_step": scatter_about(key_of[5], (D, MH), D ** -0.5, 0.1875, ((0, 8), (1, 4)), jnp.float32),
        "query_proj": scatter_about(key_of[6], (D, H * HD), (D // 2) ** -0.5, 0.25, ((0, 8), (1, 4)), jnp.float32),
        "key_proj": scatter_about(key_of[7], (D, KV * HD), (D // 2) ** -0.5, 0.25, ((0, 8), (1, 4)), jnp.float32),
        "value_proj": scatter_about(key_of[8], (D, KV * HD), D ** -0.5, 0.1875, ((0, 8), (1, 4)), jnp.float32),
        "mamba_out": scatter_about(key_of[9], (MH * P_SIZE, D), (MH * P_SIZE) ** -0.5, 0.15625, ((0, 4), (1, 8)), jnp.float32),
        "attend_out": scatter_about(key_of[10], (H * HD, D), (max(1, H * HD * 8 // LEN)) ** -0.5, 3.0, ((0, 4), (1, 8)), jnp.float32),
        "mlp_gate": scatter_about(key_of[11], (D, FF), D ** -0.5, 0.1875, ((0, 8), (1, 4)), jnp.float32),
        "mlp_up": scatter_about(key_of[12], (D, FF), D ** -0.5, 0.1875, ((0, 8), (1, 4)), jnp.float32),
        "mlp_down": scatter_about(key_of[13], (FF, D), FF ** -0.5, 0.125, ((0, 4), (1, 8)), jnp.float32),
        "state_proj": scatter_about(key_of[14], (D, 2 * N), D ** -0.5, 0.1875, ((0, 32),), jnp.float32),
        "conv_state": scatter_about(key_of[15], (KCONV + 1, 2 * N), 0.5, 3.0, ((1, 32),), jnp.float32),
        "norm_gains": jnp.clip(1.0 + 0.1 * jax.random.normal(key_of[16], (2, D), jnp.float32), 0.5, 1.5),
        "conv_mamba": scatter_about(key_of[17], (KCONV + 1, MH * P_SIZE), 0.5, 3.0, ((1, 4),), jnp.float32),
        "step_bias": jnp.clip(-3.0 + 2.5 * jax.random.uniform(key_of[18], (MH,), jnp.float32) ** levels(key_of[18], (MH,), ((0, 4),), -0.2, 0.2), -3.0, -0.5),
        "decay_log": jnp.clip(-4.0 + 5.0 * jax.random.uniform(key_of[19], (MH,), jnp.float32) ** levels(key_of[19], (MH,), ((0, 4),), -0.2, 0.2), -4.0, 1.0),
        "skip_gain": jnp.clip(0.5 + 1.0 * jax.random.uniform(key_of[20], (MH,), jnp.float32) ** levels(key_of[20], (MH,), ((0, 4),), -0.2, 0.2), 0.5, 1.5),
    }


epsilon = 1e-05
rotary_base = 100000000000.0
HIGHEST = lax.Precision.HIGHEST

@jax.custom_vjp
def low(v):
    return lax.optimization_barrier(v.astype(jnp.bfloat16)).astype(jnp.float32)

@jax.custom_vjp
def low_back(v):
    return v

def low_keep(v):
    return (low(v), None)

def low_pass(kept, grad):
    return (grad,)

def back_keep(v):
    return (v, None)

def back_low(kept, grad):
    return (low(grad),)
low.defvjp(low_keep, low_pass)
low_back.defvjp(back_keep, back_low)

def root_norm(values, gain):
    return values * lax.rsqrt(lax.optimization_barrier(jnp.mean(values * values, axis=-1, keepdims=True)) + epsilon) * gain

def rotary_tables(length, size):
    frequency = rotary_base ** (-2.0 * jnp.arange(size // 2, dtype=jnp.float32) / size)
    angles = jnp.arange(length, dtype=jnp.float32)[:, None] * frequency[None, :]
    return (jnp.cos(angles), jnp.sin(angles))

def rotate_pairs(values, cosine, sine):
    half = values.shape[-1] // 2
    first = values[..., :half]
    second = values[..., half:]
    return jnp.concatenate([first * cosine - second * sine, second * cosine + first * sine], axis=-1)

def causal_conv(values, taps):
    width = taps.shape[0] - 1
    length = values.shape[0]
    padded = jnp.pad(values, ((width - 1, 0), (0, 0)))
    total = jnp.broadcast_to(taps[width], values.shape)
    for offset in range(width):
        total = total + padded[offset:offset + length] * taps[offset]
    return total

def scan_block(rate, state, block):
    inputs, steps, entry, readout = block
    size = steps.shape[0]
    logs = jnp.cumsum(steps * rate, axis=0)
    order = jnp.arange(size, dtype=jnp.int32)
    causal = (order[:, None] >= order[None, :])[:, :, None]
    spread = jnp.where(causal, logs[:, None, :] - logs[None, :, :], 0.0)
    decay = jnp.where(causal, jnp.exp(spread), 0.0)
    intersection = jnp.dot(readout, entry.T, precision=HIGHEST)
    mixing = decay * intersection[:, :, None] * steps[None, :, :]
    local = jnp.einsum('tsh,shp->thp', mixing, inputs, precision=HIGHEST)
    carried = jnp.einsum('tn,hpn->thp', readout, state, precision=HIGHEST) * jnp.exp(logs)[:, :, None]
    tail = jnp.exp(logs[-1][None, :] - logs) * steps
    fresh = state * jnp.exp(logs[-1])[:, None, None] + jnp.einsum('sh,shp,sn->hpn', tail, inputs, entry, precision=HIGHEST)
    return (fresh, local + carried)

def state_scan(inputs, steps, rate, entry, readout):
    length, heads, size = inputs.shape
    blocks = length // SPAN
    pieces = (inputs.reshape(blocks, SPAN, heads, size), steps.reshape(blocks, SPAN, heads), entry.reshape(blocks, SPAN, entry.shape[1]), readout.reshape(blocks, SPAN, readout.shape[1]))
    start = jnp.zeros((heads, size, entry.shape[1]), jnp.float32)
    kept_block = jax.checkpoint(scan_block)

    def stepper(state, block):
        return kept_block(rate, state, block)
    final, outs = lax.scan(stepper, start, pieces)
    return outs.reshape(length, heads, size)

def mamba_core(ssm_input, ssm_gating, ssm_states, ssm_steps, conv_taps, conv_shared, step_bias, decay_log, skip_gain):
    length = ssm_input.shape[0]
    heads = step_bias.shape[0]
    inputs = jax.nn.silu(causal_conv(ssm_input, conv_taps)).reshape(length, heads, -1)
    shared = jax.nn.silu(causal_conv(ssm_states, conv_shared))
    states = shared.shape[1] // 2
    steps = jax.nn.softplus(ssm_steps + step_bias)
    rate = -jnp.exp(decay_log)
    result = state_scan(inputs, steps, rate, shared[:, :states], shared[:, states:]) + skip_gain[None, :, None] * inputs
    return result.reshape(length, -1) * jax.nn.silu(ssm_gating)

def attend_block(block, start, keys_all, values_all):
    length, heads, size = keys_all.shape
    scale = size ** (-0.5)
    scores = jnp.einsum('qhd,khd->hqk', block, keys_all, precision=HIGHEST) * scale
    rows = start + jnp.arange(block.shape[0], dtype=jnp.int32)
    allowed = jnp.arange(length, dtype=jnp.int32)[None, :] <= rows[:, None]
    scores = low_back(jnp.where(allowed[None], scores, -1e+30))
    chance = low(jax.nn.softmax(scores, axis=-1))
    return jnp.einsum('hqk,khd->qhd', chance, values_all, precision=HIGHEST)

def attend_reference(query, keys, values):
    length, heads, size = query.shape
    groups = heads // keys.shape[1]
    keys_all = jnp.repeat(keys, groups, axis=1)
    values_all = jnp.repeat(values, groups, axis=1)
    blocks = length // ATT_BLOCK
    starts = jnp.arange(blocks, dtype=jnp.int32) * ATT_BLOCK
    kept = jax.checkpoint(attend_block)

    def apply_block(item):
        return kept(item[0], item[1], keys_all, values_all)
    outs = lax.map(apply_block, (query.reshape(blocks, ATT_BLOCK, heads, size), starts))
    return outs.reshape(length, heads, size)

def one_sequence(params, inputs, limit):
    mamba_x, mamba_z, mamba_step, query_proj, key_proj, value_proj, mamba_out, attend_out, mlp_gate, mlp_up, mlp_down, state_proj, conv_state, norm_gains, conv_mamba, step_bias, decay_log, skip_gain = params
    valid = (jnp.arange(LEN, dtype=jnp.int32) < limit).astype(jnp.float32)[:, None]
    normed = low(root_norm(inputs, norm_gains[0]))

    def project(weight):
        return jnp.dot(normed, low(weight), precision=HIGHEST)
    ssm_input = low_back(project(mamba_x))
    ssm_gating = low_back(project(mamba_z))
    ssm_steps = low_back(project(mamba_step))
    ssm_states = project(state_proj)
    chans = MH * P_SIZE // N_TENSOR
    heads = MH // N_TENSOR
    pieces = []
    for group in range(N_TENSOR):
        col_lo = group * chans
        head_lo = group * heads
        pieces.append(mamba_core(ssm_input[:, col_lo:col_lo + chans], ssm_gating[:, col_lo:col_lo + chans], low_back(ssm_states), ssm_steps[:, head_lo:head_lo + heads], conv_mamba[:, col_lo:col_lo + chans], conv_state, step_bias[head_lo:head_lo + heads], decay_log[head_lo:head_lo + heads], skip_gain[head_lo:head_lo + heads]))
    ssm_low = low(jnp.concatenate(pieces, axis=1))
    cosine, sine = rotary_tables(LEN, HD)
    query = low(rotate_pairs(low_back(project(query_proj)).reshape(LEN, H, HD), cosine[:, None, :], sine[:, None, :]))
    keys = low(rotate_pairs(low_back(project(key_proj)).reshape(LEN, KV, HD), cosine[:, None, :], sine[:, None, :]))
    values = low(low_back(project(value_proj)).reshape(LEN, KV, HD))
    attended = attend_reference(query, keys, values)
    att_low = low(low_back(attended.reshape(LEN, H * HD)))
    mamba_out_low = low(mamba_out)
    attend_out_low = low(attend_out)
    att_cols = H * HD // N_TENSOR
    mix_terms = []
    for group in range(N_TENSOR):
        col_lo = group * chans
        att_lo = group * att_cols
        mix_terms.append(low(jnp.dot(ssm_low[:, col_lo:col_lo + chans], mamba_out_low[col_lo:col_lo + chans], precision=HIGHEST) + jnp.dot(att_low[:, att_lo:att_lo + att_cols], attend_out_low[att_lo:att_lo + att_cols], precision=HIGHEST)))
    mixed = low_back(sum(mix_terms[1:], mix_terms[0]))
    middle = inputs + mixed
    normed_two = low(root_norm(middle, norm_gains[1]))
    gate = low_back(jnp.dot(normed_two, low(mlp_gate), precision=HIGHEST))
    upward = low_back(jnp.dot(normed_two, low(mlp_up), precision=HIGHEST))
    hidden = low(jax.nn.silu(gate) * upward)
    down_low = low(mlp_down)
    ff_cols = FF // N_TENSOR
    ffn_terms = []
    for group in range(N_TENSOR):
        ff_lo = group * ff_cols
        ffn_terms.append(low(jnp.dot(hidden[:, ff_lo:ff_lo + ff_cols], down_low[ff_lo:ff_lo + ff_cols], precision=HIGHEST)))
    ffn = low_back(sum(ffn_terms[1:], ffn_terms[0]))
    return valid * (middle + ffn)

def reference(layer_in, out_grad, lengths, mamba_x, mamba_z, mamba_step, query_proj, key_proj, value_proj, mamba_out, attend_out, mlp_gate, mlp_up, mlp_down, state_proj, conv_state, norm_gains, conv_mamba, step_bias, decay_log, skip_gain):
    params = (mamba_x, mamba_z, mamba_step, query_proj, key_proj, value_proj, mamba_out, attend_out, mlp_gate, mlp_up, mlp_down, state_proj, conv_state, norm_gains, conv_mamba, step_bias, decay_log, skip_gain)
    params = tuple((item.astype(jnp.float32) for item in params))
    inputs = jnp.transpose(layer_in.astype(jnp.float32), (1, 0, 2))
    kept = jax.checkpoint(one_sequence)

    def forward(weights, values):

        def apply_one(item):
            return kept(weights, item[0], item[1])
        return lax.map(apply_one, (values, lengths))
    result, pullback = jax.vjp(forward, params, inputs)
    weight_grads, input_grad = pullback(jnp.transpose(out_grad.astype(jnp.float32), (1, 0, 2)))
    mamba_x_grad, mamba_z_grad, mamba_step_grad, query_proj_grad, key_proj_grad, value_proj_grad, mamba_out_grad, attend_out_grad, mlp_gate_grad, mlp_up_grad, mlp_down_grad, state_proj_grad, conv_state_grad, norm_gains_grad, conv_mamba_grad, step_bias_grad, decay_log_grad, skip_gain_grad = weight_grads
    layer_out = jnp.transpose(result, (1, 0, 2)).astype(jnp.bfloat16)
    in_grad = jnp.transpose(input_grad, (1, 0, 2)).astype(jnp.bfloat16)
    return (layer_out, in_grad, mamba_x_grad, mamba_z_grad, mamba_step_grad, query_proj_grad, key_proj_grad, value_proj_grad, mamba_out_grad, attend_out_grad, mlp_gate_grad, mlp_up_grad, mlp_down_grad, state_proj_grad, conv_state_grad, norm_gains_grad, conv_mamba_grad, step_bias_grad, decay_log_grad, skip_gain_grad)
```

```python
import jax
import jax.numpy as jnp
from jax import lax
from jax.sharding import PartitionSpec as P

HD = 64
ATT_BLOCK = 512
SPAN = 256
epsilon = 1e-05
rotary_base = 100000000000.0
HIGHEST = lax.Precision.HIGHEST
bf16 = jnp.bfloat16
f32 = jnp.float32


def flip(value, axis, mask):
    size = lax.axis_size(axis)
    return lax.ppermute(value, axis, [(i, i ^ mask) for i in range(size)])


def bits_of(size):
    bits = size.bit_length() - 1
    assert size == 1 << bits
    return bits


def relative_order(size):
    order = [0]
    for bit in reversed(range(bits_of(size))):
        order = order + [k | (1 << bit) for k in order]
    return order


def gather_pieces(own, axis):
    size = lax.axis_size(axis)
    if size > 8:
        held = own
        for bit in reversed(range(bits_of(size))):
            held = jnp.concatenate([held, flip(held, axis, 1 << bit)], axis=0)
        return held
    held = [own]
    for bit in reversed(range(bits_of(size))):
        held = held + [flip(piece, axis, 1 << bit) for piece in held]
    return jnp.concatenate(held, axis=0)


def scatter_sum(whole, axis):
    size = lax.axis_size(axis)
    rows = whole.shape[0] // size
    if size > 8:
        held = whole
        for bit in range(bits_of(size)):
            half = held.shape[0] // 2
            held = held[:half] + flip(held[half:].astype(bf16), axis, 1 << bit).astype(f32)
        return held
    order = relative_order(size)
    held = {k: whole[p * rows : (p + 1) * rows] for p, k in enumerate(order)}
    for bit in range(bits_of(size)):
        mask = 1 << bit
        got = {k ^ mask: flip(v.astype(bf16), axis, mask) for k, v in held.items() if k & mask}
        held = {k: v + got[k].astype(f32) for k, v in held.items() if not k & mask}
    return held[0]


def blocks_by_xor(value, member, size, axis):
    width = value.shape[axis] // size
    return jnp.concatenate(
        [
            lax.dynamic_slice_in_dim(value, (member ^ k) * width, width, axis)
            for k in relative_order(size)
        ],
        axis=axis,
    )


def blocks_back(value, member, size, axis):
    width = value.shape[axis] // size
    where = [0] * size
    for p, k in enumerate(relative_order(size)):
        where[k] = p
    table = jnp.array(where, jnp.int32)
    return jnp.concatenate(
        [
            lax.dynamic_slice_in_dim(value, table[member ^ j] * width, width, axis)
            for j in range(size)
        ],
        axis=axis,
    )


def pick(bit, one, zero):
    return jnp.where(bit == 1, one, zero)


def gather_y(own, y):
    other = flip(own, "tensor", 2)
    return jnp.stack([pick(y, other, own), pick(y, own, other)])


def gather_core(pair, core):
    other = flip(pair, "tensor", 1)
    full = jnp.stack([pick(core, other, pair), pick(core, pair, other)], axis=1)
    return full.reshape((4 * full.shape[2],) + full.shape[3:])


def reduce_core(part, core):
    rows = part.shape[0] // 4
    cut = part.reshape((2, 2, rows) + part.shape[1:])
    sent = pick(core, cut[:, 0], cut[:, 1])
    kept = pick(core, cut[:, 1], cut[:, 0])
    return (kept.astype(f32) + flip(sent, "tensor", 1).astype(f32)).astype(bf16)


def reduce_y_both(pair):
    return pair.astype(f32) + flip(pair, "tensor", 2).astype(f32)


def reduce_y_own(pair, y):
    sent = pick(y, pair[0], pair[1])
    kept = pick(y, pair[1], pair[0])
    return kept.astype(f32) + flip(sent, "tensor", 2).astype(f32)


def rotary_tables(length, size):
    frequency = rotary_base ** (-2.0 * jnp.arange(size // 2, dtype=jnp.float32) / size)
    angles = jnp.arange(length, dtype=jnp.float32)[:, None] * frequency[None, :]
    return (jnp.cos(angles), jnp.sin(angles))


def rotate_pairs(values, cosine, sine):
    half = values.shape[-1] // 2
    first = values[..., :half]
    second = values[..., half:]
    return jnp.concatenate(
        [first * cosine - second * sine, second * cosine + first * sine], axis=-1
    )


def causal_conv(values, taps):
    width = taps.shape[0] - 1
    length = values.shape[0]
    padded = jnp.pad(values, ((width - 1, 0), (0, 0)))
    total = jnp.broadcast_to(taps[width], values.shape)
    for offset in range(width):
        total = total + padded[offset : offset + length] * taps[offset]
    return total


def scan_block(rate, state, block):
    inputs, steps, entry, readout = block
    size = steps.shape[0]
    logs = jnp.cumsum(steps * rate, axis=0)
    order = jnp.arange(size, dtype=jnp.int32)
    causal = (order[:, None] >= order[None, :])[:, :, None]
    spread = jnp.where(causal, logs[:, None, :] - logs[None, :, :], 0.0)
    decay = jnp.where(causal, jnp.exp(spread), 0.0)
    intersection = jnp.dot(readout, entry.T, precision=HIGHEST)
    mixing = decay * intersection[:, :, None] * steps[None, :, :]
    local = jnp.einsum("tsh,shp->thp", mixing, inputs, precision=HIGHEST)
    carried = (
        jnp.einsum("tn,hpn->thp", readout, state, precision=HIGHEST) * jnp.exp(logs)[:, :, None]
    )
    tail = jnp.exp(logs[-1][None, :] - logs) * steps
    fresh = state * jnp.exp(logs[-1])[:, None, None] + jnp.einsum(
        "sh,shp,sn->hpn", tail, inputs, entry, precision=HIGHEST
    )
    return (fresh, local + carried)


def state_scan(inputs, steps, rate, entry, readout):
    length, heads, size = inputs.shape
    blocks = length // SPAN
    pieces = (
        inputs.reshape(blocks, SPAN, heads, size),
        steps.reshape(blocks, SPAN, heads),
        entry.reshape(blocks, SPAN, entry.shape[1]),
        readout.reshape(blocks, SPAN, readout.shape[1]),
    )
    start = jnp.zeros((heads, size, entry.shape[1]), jnp.float32)
    kept_block = jax.checkpoint(scan_block)

    def stepper(state, block):
        return kept_block(rate, state, block)

    final, outs = lax.scan(stepper, start, pieces)
    return outs.reshape(length, heads, size)


def mamba_core(
    ssm_input,
    ssm_gating,
    ssm_states,
    ssm_steps,
    conv_taps,
    conv_shared,
    step_bias,
    decay_log,
    skip_gain,
):
    length = ssm_input.shape[0]
    heads = step_bias.shape[0]
    inputs = jax.nn.silu(causal_conv(ssm_input, conv_taps)).reshape(length, heads, -1)
    shared = jax.nn.silu(causal_conv(ssm_states, conv_shared))
    states = shared.shape[1] // 2
    steps = jax.nn.softplus(ssm_steps + step_bias)
    rate = -jnp.exp(decay_log)
    result = (
        state_scan(inputs, steps, rate, shared[:, :states], shared[:, states:])
        + skip_gain[None, :, None] * inputs
    )
    return result.reshape(length, -1) * jax.nn.silu(ssm_gating)


def swiglu(gate_part, up_part):
    return jax.nn.silu(gate_part) * up_part


def block_scores(block, keys, start, scale):
    length = keys.shape[0]
    scores = jnp.einsum("qcgd,scd->cgqs", block, keys, preferred_element_type=jnp.float32) * scale
    rows = start + jnp.arange(block.shape[0], dtype=jnp.int32)
    allowed = jnp.arange(length, dtype=jnp.int32)[None, :] <= rows[:, None]
    return jnp.where(allowed, scores, -1e30)


def attend_forward(query, keys, values):
    length, heads, size = query.shape
    kv_heads = keys.shape[1]
    groups = heads // kv_heads
    blocks = length // ATT_BLOCK
    scale = size ** (-0.5)
    grouped = query.reshape(blocks, ATT_BLOCK, kv_heads, groups, size)
    starts = jnp.arange(blocks, dtype=jnp.int32) * ATT_BLOCK

    def one_block(item):
        block, start = item
        scores = block_scores(block, keys, start, scale)
        top = jnp.max(scores, axis=-1, keepdims=True)
        expo = jnp.exp(scores - top)
        total = jnp.sum(expo, axis=-1, keepdims=True)
        chance = (expo / total).astype(jnp.bfloat16)
        result = jnp.einsum("cgqs,scd->qcgd", chance, values, preferred_element_type=jnp.float32)
        return (result, (top + jnp.log(total))[..., 0])

    outs, logsum = lax.map(one_block, (grouped, starts))
    return (outs.reshape(length, heads, size), logsum)


def attend_backward(query, keys, values, logsum, grad_out):
    length, heads, size = query.shape
    kv_heads = keys.shape[1]
    groups = heads // kv_heads
    blocks = length // ATT_BLOCK
    scale = size ** (-0.5)
    grouped = query.reshape(blocks, ATT_BLOCK, kv_heads, groups, size)
    grad_grouped = grad_out.reshape(blocks, ATT_BLOCK, kv_heads, groups, size)
    starts = jnp.arange(blocks, dtype=jnp.int32) * ATT_BLOCK

    def one_block(carry, item):
        key_grad, value_grad = carry
        block, start, block_sum, block_grad = item
        scores = block_scores(block, keys, start, scale)
        chance = jnp.exp(scores - block_sum[..., None])
        grad_chance = jnp.einsum(
            "qcgd,scd->cgqs", block_grad, values, preferred_element_type=jnp.float32
        )
        center = jnp.sum(chance * grad_chance, axis=-1, keepdims=True)
        grad_scores = (chance * (grad_chance - center)).astype(jnp.bfloat16)
        query_grad = (
            jnp.einsum("cgqs,scd->qcgd", grad_scores, keys, preferred_element_type=jnp.float32)
            * scale
        )
        key_grad = (
            key_grad
            + jnp.einsum("cgqs,qcgd->scd", grad_scores, block, preferred_element_type=jnp.float32)
            * scale
        )
        value_grad = value_grad + jnp.einsum(
            "cgqs,qcgd->scd",
            chance.astype(jnp.bfloat16),
            block_grad,
            preferred_element_type=jnp.float32,
        )
        return ((key_grad, value_grad), query_grad)

    zeros = jnp.zeros((length, kv_heads, size), jnp.float32)
    (key_grad, value_grad), query_grad = lax.scan(
        one_block, (zeros, zeros), (grouped, starts, logsum, grad_grouped)
    )
    return (query_grad.reshape(length, heads, size), key_grad, value_grad)


def mm(a, b):
    return jnp.dot(a, b, preferred_element_type=f32)


def mm_t(a, b):
    return lax.dot_general(a, b, (((1,), (1,)), ((), ())), preferred_element_type=f32)


def t_mm(a, b):
    return lax.dot_general(a, b, (((0,), (0,)), ((), ())), preferred_element_type=f32)


def body(
    layer_in,
    out_grad,
    lengths,
    mamba_x,
    mamba_z,
    mamba_step,
    query_proj,
    key_proj,
    value_proj,
    mamba_out,
    attend_out,
    mlp_gate,
    mlp_up,
    mlp_down,
    state_proj,
    conv_state,
    norm_gains,
    conv_mamba,
    step_bias,
    decay_log,
    skip_gain,
):
    ranks = lax.axis_size("tensor")
    assert ranks == 4 and layer_in.shape[1] == 1
    rank = lax.axis_index("tensor")
    y, core = rank // 2, rank % 2
    peers = lax.axis_size("dp")
    me = lax.axis_index("dp")
    rows, _, width = layer_in.shape
    length = rows * ranks
    chans = mamba_x.shape[1]
    heads = step_bias.shape[0]
    q_cols, k_cols = query_proj.shape[1], key_proj.shape[1]
    ff = mlp_gate.shape[1]
    d_rows = width // peers
    n2 = state_proj.shape[1]

    own_in = blocks_by_xor(layer_in[:, 0], me, peers, 1)
    own_go = blocks_by_xor(out_grad[:, 0], me, peers, 1)
    in_pair = gather_y(own_in, y)
    in_full = gather_core(in_pair, core)

    taps_own = conv_state.shape[1]
    gains_own = norm_gains.shape[1]
    small = jnp.concatenate([conv_state.reshape(-1), norm_gains.reshape(-1)])
    fill = -small.shape[0] % 128
    small = jnp.pad(small, (0, fill)).reshape(1, -1)
    small = gather_core(gather_y(small, y), core)
    small = gather_pieces(small[None], "dp")
    cut = conv_state.size
    taps_pieces = small[:, :, :cut].reshape(peers, ranks, conv_state.shape[0], taps_own)
    taps_rel = jnp.transpose(taps_pieces, (2, 0, 1, 3)).reshape(conv_state.shape[0], -1)
    conv_shared = blocks_back(taps_rel, me, peers, 1)
    gain_pair = jnp.transpose(
        small[:, :, cut : cut + norm_gains.size].reshape(peers, ranks, 2, gains_own), (2, 0, 1, 3)
    ).reshape(2, width)

    step_pad = -heads % 128
    pack_a = jnp.concatenate(
        [mamba_x.astype(bf16), jnp.pad(mamba_step.astype(bf16), ((0, 0), (0, step_pad)))], axis=1
    )
    w_a = gather_pieces(pack_a, "dp")
    state_own = gather_core(gather_y(state_proj.astype(bf16), y), core)
    w_bc = gather_pieces(state_own, "dp")
    pack_b = jnp.concatenate(
        [item.astype(bf16) for item in (mamba_z, query_proj, key_proj, value_proj)], axis=1
    )
    w_b = gather_pieces(pack_b, "dp")
    pack_o = jnp.concatenate([mamba_out.T.astype(bf16), attend_out.T.astype(bf16)], axis=1)
    w_o = gather_pieces(pack_o, "dp")
    pack_m = jnp.concatenate(
        [mlp_gate.astype(bf16), mlp_up.astype(bf16), mlp_down.T.astype(bf16)], axis=1
    )
    w_m = gather_pieces(pack_m, "dp")

    limit = lengths[0]
    go_pair = gather_y(own_go, y)
    go_full = gather_core(go_pair, core)
    all_valid = jnp.arange(length, dtype=jnp.int32) < limit
    block_valid = all_valid.reshape(2, 2, rows)
    pair_valid = pick(core, block_valid[:, 1], block_valid[:, 0])
    gf = jnp.where(all_valid[:, None], go_full, 0).astype(bf16)

    def norm_parts(values):
        rho = lax.rsqrt(jnp.mean(values * values, axis=-1, keepdims=True) + epsilon)
        return rho

    x_full = in_full.astype(f32)
    rho_one = norm_parts(x_full)
    a1 = (x_full * rho_one * gain_pair[0]).astype(bf16)

    w_x, w_dt = w_a[:, :chans], w_a[:, chans : chans + heads]
    w_z = w_b[:, :chans]
    w_qkv = w_b[:, chans:]
    proj_qkv = mm(a1, w_qkv)
    core_args = (
        mm(a1, w_x),
        mm(a1, w_z),
        mm(a1, w_bc),
        mm(a1, w_dt),
        conv_mamba,
        conv_shared,
        step_bias,
        decay_log,
        skip_gain,
    )
    ssm_out, core_back = jax.vjp(mamba_core, *core_args)
    om = ssm_out.astype(bf16)
    cosine, sine = rotary_tables(length, HD)

    def turn(pre, sign):
        shaped = pre.reshape(length, pre.shape[1] // HD, HD)
        return rotate_pairs(shaped, cosine[:, None, :], sign * sine[:, None, :])

    query = turn(proj_qkv[:, :q_cols], 1.0).astype(bf16)
    keys = turn(proj_qkv[:, q_cols : q_cols + k_cols], 1.0).astype(bf16)
    values = proj_qkv[:, q_cols + k_cols :].reshape(length, -1, HD).astype(bf16)
    att_out, logsum = attend_forward(query, keys, values)
    oa = att_out.reshape(length, -1).astype(bf16)
    mixed_in = jnp.concatenate([om, oa], axis=1)
    m_pair = reduce_y_both(reduce_core(mm_t(mixed_in, w_o).astype(bf16), core))
    r1 = in_pair.astype(f32) + m_pair
    rho_two = norm_parts(r1)
    a2_pair = (r1 * rho_two * gain_pair[1]).astype(bf16)
    a2 = gather_core(a2_pair, core)
    w_gu, w_dn = w_m[:, : 2 * ff], w_m[:, 2 * ff :]
    gate_up = mm(a2, w_gu)
    gate, up = gate_up[:, :ff], gate_up[:, ff:]
    hidden_full, glu_back = jax.vjp(swiglu, gate, up)
    hid = hidden_full.astype(bf16)
    ffn = reduce_y_own(reduce_core(mm_t(hid, w_dn).astype(bf16), core), y)
    r1_own = pick(y, r1[1], r1[0])
    own_valid = pick(y, pair_valid[1], pair_valid[0])
    layer_out = jnp.where(own_valid[:, None], r1_own + ffn, 0.0).astype(bf16)
    layer_out = blocks_back(layer_out, me, peers, 1)[:, None]

    g_hid = mm(gf, w_dn)
    gate_grad, up_grad = glu_back(g_hid)
    g_gu = jnp.concatenate([gate_grad.astype(bf16), up_grad.astype(bf16)], axis=1)
    g_a2_pair = reduce_y_both(reduce_core(mm_t(g_gu, w_gu).astype(bf16), core))
    n_two = r1 * rho_two
    e_two = g_a2_pair * gain_pair[1]
    gf_pair = jnp.where(pair_valid[:, :, None], go_pair.astype(f32), 0.0)
    g_r1 = gf_pair + rho_two * (e_two - n_two * jnp.mean(e_two * n_two, axis=-1, keepdims=True))
    gain_two_pair = jnp.sum(g_a2_pair * n_two, axis=1)
    gain_two_grad = pick(y, gain_two_pair[1], gain_two_pair[0])
    g_m = gather_core(g_r1.astype(bf16), core)
    g_mix = mm(g_m, w_o)
    g_ym = g_mix[:, :chans]
    g_oa = g_mix[:, chans:].astype(bf16)

    mlp_w_grad = jnp.concatenate([t_mm(a2, g_gu), t_mm(gf, hid)], axis=1)
    mlp_sum = scatter_sum(mlp_w_grad, "dp")
    out_sum = scatter_sum(t_mm(g_m, mixed_in), "dp")

    query_grad, keys_grad, values_grad = attend_backward(
        query, keys, values, logsum, g_oa.reshape(length, -1, HD)
    )
    g_qkv = jnp.concatenate(
        [
            turn(query_grad.reshape(length, -1), -1.0).reshape(length, -1),
            turn(keys_grad.reshape(length, -1), -1.0).reshape(length, -1),
            values_grad.reshape(length, -1),
        ],
        axis=1,
    ).astype(bf16)
    (
        g_px,
        g_pz,
        g_pbc,
        g_pdt,
        conv_taps_grad,
        conv_shared_grad,
        bias_grad,
        decay_grad,
        skip_grad,
    ) = core_back(g_ym)
    g_b = jnp.concatenate([g_pz.astype(bf16), g_qkv], axis=1)
    g_a = jnp.concatenate(
        [g_px.astype(bf16), jnp.pad(g_pdt.astype(bf16), ((0, 0), (0, step_pad)))], axis=1
    )
    g_bc = g_pbc.astype(bf16)
    b_sum = scatter_sum(t_mm(a1, g_b), "dp")
    a_sum = scatter_sum(t_mm(a1, g_a), "dp")
    state_part = t_mm(a1, g_bc).astype(bf16).reshape(peers, 4, gains_own, n2)
    state_part = jnp.swapaxes(state_part, 0, 1).reshape(4 * peers * gains_own, n2)
    state_part = reduce_y_own(reduce_core(state_part, core), y)
    state_proj_grad = scatter_sum(state_part, "dp")

    g_a1_part = mm_t(g_b, w_b) + mm_t(g_a, w_a) + mm_t(g_bc, w_bc)
    gain_one_grad = jnp.sum(g_a1_part * (x_full * rho_one), axis=0)
    g_a1 = reduce_y_own(reduce_core(g_a1_part.astype(bf16), core), y)
    x_own = own_in.astype(f32)
    rho_own = norm_parts(x_own)
    n_one = x_own * rho_own
    e_one = g_a1 * gain_pair[0]
    g_r1_own = pick(y, g_r1[1], g_r1[0])
    in_grad = g_r1_own + rho_own * (e_one - n_one * jnp.mean(e_one * n_one, axis=-1, keepdims=True))
    in_grad = blocks_back(in_grad.astype(bf16), me, peers, 1)[:, None]

    gain_grads = blocks_back(jnp.stack([gain_one_grad, gain_two_grad]), me, peers, 1)
    both = jnp.concatenate([conv_shared_grad.reshape(-1), gain_grads.reshape(-1)])
    both_rows = -(-both.shape[0] // 128)
    both = jnp.pad(both, (0, both_rows * 128 - both.shape[0]))
    only = jnp.concatenate([conv_taps_grad.reshape(-1), bias_grad, decay_grad, skip_grad])
    only_count = only.shape[0]
    only = jnp.pad(only, (0, -only_count % 128))
    packed = jnp.concatenate([both, only]).reshape(-1, 128)
    for bit in range(bits_of(peers)):
        packed = packed + flip(packed, "dp", 1 << bit)
    both = packed[:both_rows]
    for mask in (1, 2):
        both = both + flip(both, "tensor", mask)
    both = both.reshape(-1)
    only = packed[both_rows:].reshape(-1)
    conv_state_sum = both[: conv_shared.size].reshape(conv_shared.shape)
    gain_sum = both[conv_shared.size : conv_shared.size + 2 * width].reshape(2, width)
    member = me * ranks + rank
    conv_state_grad = lax.dynamic_slice_in_dim(conv_state_sum, member * taps_own, taps_own, 1)
    norm_gains_grad = lax.dynamic_slice_in_dim(gain_sum, member * gains_own, gains_own, 1)
    cut = conv_taps_grad.size
    conv_mamba_grad = only[:cut].reshape(conv_taps_grad.shape)
    step_bias_grad = only[cut : cut + heads]
    decay_log_grad = only[cut + heads : cut + 2 * heads]
    skip_gain_grad = only[cut + 2 * heads : cut + 3 * heads]

    return (
        layer_out,
        in_grad,
        a_sum[:, :chans],
        b_sum[:, :chans],
        a_sum[:, chans : chans + heads],
        b_sum[:, chans : chans + q_cols],
        b_sum[:, chans + q_cols : chans + q_cols + k_cols],
        b_sum[:, chans + q_cols + k_cols :],
        out_sum[:, :chans].T,
        out_sum[:, chans:].T,
        mlp_sum[:, :ff],
        mlp_sum[:, ff : 2 * ff],
        mlp_sum[:, 2 * ff :].T,
        state_proj_grad,
        conv_state_grad,
        norm_gains_grad,
        conv_mamba_grad,
        step_bias_grad,
        decay_log_grad,
        skip_gain_grad,
    )


def solution(mesh):
    in_specs = (
        P("tensor", "dp", None),
        P("tensor", "dp", None),
        P("dp"),
        P("dp", "tensor"),
        P("dp", "tensor"),
        P("dp", "tensor"),
        P("dp", "tensor"),
        P("dp", "tensor"),
        P("dp", "tensor"),
        P("tensor", "dp"),
        P("tensor", "dp"),
        P("dp", "tensor"),
        P("dp", "tensor"),
        P("tensor", "dp"),
        P(("dp", "tensor"), None),
        P(None, ("dp", "tensor")),
        P(None, ("dp", "tensor")),
        P(None, "tensor"),
        P("tensor"),
        P("tensor"),
        P("tensor"),
    )
    out_specs = (
        P("tensor", "dp", None),
        P("tensor", "dp", None),
        P("dp", "tensor"),
        P("dp", "tensor"),
        P("dp", "tensor"),
        P("dp", "tensor"),
        P("dp", "tensor"),
        P("dp", "tensor"),
        P("tensor", "dp"),
        P("tensor", "dp"),
        P("dp", "tensor"),
        P("dp", "tensor"),
        P("tensor", "dp"),
        P(("dp", "tensor"), None),
        P(None, ("dp", "tensor")),
        P(None, ("dp", "tensor")),
        P(None, "tensor"),
        P("tensor"),
        P("tensor"),
        P("tensor"),
    )
    return jax.shard_map(body, mesh=mesh, in_specs=in_specs, out_specs=out_specs, check_vma=False)
```

```python
import functools

import jax
import jax.numpy as jnp
from jax import lax
from jax.experimental import pallas as pl
from jax.experimental.pallas import tpu as pltpu
from jax.sharding import PartitionSpec as P

epsilon = 1e-05
rotary_base = 100000000000.0
HIGHEST = lax.Precision.HIGHEST
bf16 = jnp.bfloat16
f32 = jnp.float32


def flip(value, axis, mask):
    size = lax.axis_size(axis)
    return lax.ppermute(value, axis, [(i, i ^ mask) for i in range(size)])


def bits_of(size):
    bits = size.bit_length() - 1
    assert size == 1 << bits
    return bits


def relative_order(size):
    order = [0]
    for bit in reversed(range(bits_of(size))):
        order = order + [k | (1 << bit) for k in order]
    return order


def gather_pieces(own, axis):
    size = lax.axis_size(axis)
    if size > 8:
        held = own
        for bit in reversed(range(bits_of(size))):
            held = jnp.concatenate([held, flip(held, axis, 1 << bit)], axis=0)
        return held
    held = [own]
    for bit in reversed(range(bits_of(size))):
        held = held + [flip(piece, axis, 1 << bit) for piece in held]
    return jnp.concatenate(held, axis=0)


def scatter_sum(whole, axis):
    size = lax.axis_size(axis)
    rows = whole.shape[0] // size
    if size > 8:
        held = whole
        for bit in range(bits_of(size)):
            half = held.shape[0] // 2
            held = held[:half] + flip(held[half:].astype(bf16), axis, 1 << bit).astype(f32)
        return held
    order = relative_order(size)
    held = {k: whole[p * rows : (p + 1) * rows] for p, k in enumerate(order)}
    for bit in range(bits_of(size)):
        mask = 1 << bit
        got = {k ^ mask: flip(v.astype(bf16), axis, mask) for k, v in held.items() if k & mask}
        held = {k: v + got[k].astype(f32) for k, v in held.items() if not k & mask}
    return held[0]


def blocks_by_xor(value, member, size, axis):
    width = value.shape[axis] // size
    return jnp.concatenate(
        [
            lax.dynamic_slice_in_dim(value, (member ^ k) * width, width, axis)
            for k in relative_order(size)
        ],
        axis=axis,
    )


def blocks_back(value, member, size, axis):
    width = value.shape[axis] // size
    where = [0] * size
    for p, k in enumerate(relative_order(size)):
        where[k] = p
    table = jnp.array(where, jnp.int32)
    return jnp.concatenate(
        [
            lax.dynamic_slice_in_dim(value, table[member ^ j] * width, width, axis)
            for j in range(size)
        ],
        axis=axis,
    )


def pick(bit, one, zero):
    return jnp.where(bit == 1, one, zero)


def gather_y(own, y):
    other = flip(own, "tensor", 2)
    return jnp.stack([pick(y, other, own), pick(y, own, other)])


def gather_core(pair, core):
    other = flip(pair, "tensor", 1)
    full = jnp.stack([pick(core, other, pair), pick(core, pair, other)], axis=1)
    return full.reshape((4 * full.shape[2],) + full.shape[3:])


def reduce_core(part, core):
    rows = part.shape[0] // 4
    cut = part.reshape((2, 2, rows) + part.shape[1:])
    sent = pick(core, cut[:, 0], cut[:, 1])
    kept = pick(core, cut[:, 1], cut[:, 0])
    return (kept.astype(f32) + flip(sent, "tensor", 1).astype(f32)).astype(bf16)


def reduce_y_both(pair):
    return pair.astype(f32) + flip(pair, "tensor", 2).astype(f32)


def reduce_y_own(pair, y):
    sent = pick(y, pair[0], pair[1])
    kept = pick(y, pair[1], pair[0])
    return kept.astype(f32) + flip(sent, "tensor", 2).astype(f32)


CHUNK = 128
HEAD = 64
TAPS = 4


def dot_nn(a, b):
    return lax.dot_general(a, b, (((1,), (0,)), ((), ())), preferred_element_type=f32)


def dot_nt(a, b):
    return lax.dot_general(a, b, (((1,), (1,)), ((), ())), preferred_element_type=f32)


def dot_tn(a, b):
    return lax.dot_general(a, b, (((0,), (0,)), ((), ())), preferred_element_type=f32)


def dot_exact(a, b):
    return lax.dot_general(
        a, b, (((1,), (0,)), ((), ())), precision=HIGHEST, preferred_element_type=f32
    )


def iota(shape, axis):
    return lax.broadcasted_iota(jnp.int32, shape, axis)


def earlier(tail, block, back):
    if back == 0:
        return block
    return pltpu.roll(jnp.concatenate([tail, block], axis=0), back, 0)[8:]


def later(block, head, ahead):
    if ahead == 0:
        return block
    both = jnp.concatenate([block, head], axis=0)
    return pltpu.roll(both, both.shape[0] - ahead, 0)[: block.shape[0]]


def conv_rows(tail, block, taps):
    total = block * taps[TAPS - 1 : TAPS] + taps[TAPS : TAPS + 1]
    for j in range(TAPS - 1):
        total = total + earlier(tail, block, TAPS - 1 - j) * taps[j : j + 1]
    return total


def conv_rows_back(grad, head, taps):
    total = grad * taps[TAPS - 1 : TAPS]
    for j in range(TAPS - 1):
        total = total + later(grad, head, TAPS - 1 - j) * taps[j : j + 1]
    return total


def conv_taps_back(tail, block, grad):
    rows = [
        jnp.sum(earlier(tail, block, TAPS - 1 - j) * grad, axis=0, keepdims=True)
        for j in range(TAPS)
    ]
    rows.append(jnp.sum(grad, axis=0, keepdims=True))
    rows.append(jnp.zeros((8 - len(rows), grad.shape[1]), f32))
    return jnp.concatenate(rows, axis=0)


def head_columns(columns, heads):
    rows = columns.shape[0]
    low = iota((rows, 2 * HEAD), 1) < HEAD
    return jnp.concatenate(
        [
            jnp.where(low, columns[:, h : h + 1], columns[:, h + 1 : h + 2])
            for h in range(0, heads, 2)
        ],
        axis=1,
    )


def head_sums(values, heads):
    rows = values.shape[0]
    low = iota((rows, 2 * HEAD), 1) < HEAD
    sums = []
    for pair in range(heads // 2):
        part = values[:, pair * 2 * HEAD : (pair + 1) * 2 * HEAD]
        sums.append(jnp.sum(jnp.where(low, part, 0.0), axis=1, keepdims=True))
        sums.append(jnp.sum(jnp.where(low, 0.0, part), axis=1, keepdims=True))
    return sums


def softplus(value):
    return jnp.maximum(value, 0.0) + jnp.log1p(jnp.exp(-jnp.abs(value)))


def step_rows(pdt, vec):
    size = pdt.shape[1]
    raw = pdt + vec[:, 0:1]
    dt = softplus(raw)
    rate = -jnp.exp(vec[:, 1:2])
    upper = (iota((size, size), 0) <= iota((size, size), 1)).astype(f32)
    logs = dot_exact(dt * rate, upper)
    last = logs[:, size - 1 : size]
    return raw, dt, rate, logs, jnp.exp(logs), jnp.exp(last - logs), jnp.exp(last)


def mamba_fwd_kernel(
    heads, px, px_tail, pz, pbc, pbc_tail, pdt, taps, shared_taps, vec, om, kept, states, state
):
    step = pl.program_id(0)

    @pl.when(step == 0)
    def _():
        state[...] = jnp.zeros_like(state)

    started = jnp.where(step == 0, 0.0, 1.0)
    u = conv_rows(px_tail[...] * started, px[...], taps[...])
    u = u * jax.nn.sigmoid(u)
    bc = conv_rows(pbc_tail[...] * started, pbc[...], shared_taps[...])
    bc = (bc * jax.nn.sigmoid(bc)).astype(bf16)
    half = bc.shape[1] // 2
    b_in, c_out = bc[:, :half], bc[:, half:]
    _, dt, _, logs, grow, fade, last = step_rows(pdt[...], vec[...])
    columns = jnp.transpose(jnp.concatenate([logs, grow, fade * dt, dt], axis=0))
    size = u.shape[0]
    causal = iota((size, size), 0) >= iota((size, size), 1)
    mixing = dot_nt(c_out, b_in)
    u_low = u.astype(bf16)
    low = iota((size, 2 * HEAD), 1) < HEAD
    local = []
    for pair in range(heads // 2):
        piece = u_low[:, pair * 2 * HEAD : (pair + 1) * 2 * HEAD]
        outs = []
        for h in (2 * pair, 2 * pair + 1):
            spread = jnp.where(causal, columns[:, h : h + 1] - logs[h : h + 1], -1e30)
            matrix = (mixing * jnp.exp(spread) * dt[h : h + 1]).astype(bf16)
            outs.append(dot_nn(matrix, piece))
        local.append(jnp.where(low, outs[0], outs[1]))
    before = state[...]
    states[0] = before
    carried = dot_nn(c_out, before.astype(bf16)) * head_columns(columns[:, 8:16], heads)
    skip = head_columns(jnp.transpose(jnp.broadcast_to(vec[:, 2:3], (8, size))), heads)
    total = jnp.concatenate(local, axis=1) + carried + skip * u
    z = pz[...]
    om[...] = (total * (z * jax.nn.sigmoid(z))).astype(bf16)
    kept[...] = total.astype(bf16)
    fed = (u * head_columns(columns[:, 16:24], heads)).astype(bf16)
    end = head_columns(jnp.transpose(jnp.broadcast_to(last, (8, 128))), heads)[:1]
    state[...] = before * end + dot_tn(b_in, fed)


def mamba_bwd_kernel(
    heads,
    px,
    px_tail,
    pz,
    pbc,
    pbc_tail,
    pdt,
    taps,
    shared_taps,
    vec,
    kept,
    states,
    gym,
    g_px,
    g_pz,
    g_pbc,
    g_pdt,
    g_taps,
    g_shared,
    g_vec,
    g_skip,
    d_state,
    next_px,
    next_bc,
):
    step = pl.program_id(0)
    steps = pl.num_programs(0)

    @pl.when(step == 0)
    def _():
        d_state[...] = jnp.zeros_like(d_state)
        next_px[...] = jnp.zeros_like(next_px)
        next_bc[...] = jnp.zeros_like(next_bc)
        g_taps[...] = jnp.zeros_like(g_taps)
        g_shared[...] = jnp.zeros_like(g_shared)
        g_vec[...] = jnp.zeros_like(g_vec)
        g_skip[...] = jnp.zeros_like(g_skip)

    started = jnp.where(step == steps - 1, 0.0, 1.0)
    size = px.shape[0]
    tail_x = px_tail[...] * started
    block_x = px[...]
    pre_u = conv_rows(tail_x, block_x, taps[...])
    sig_u = jax.nn.sigmoid(pre_u)
    u = pre_u * sig_u
    tail_bc = pbc_tail[...] * started
    block_bc = pbc[...]
    pre_bc = conv_rows(tail_bc, block_bc, shared_taps[...])
    sig_bc = jax.nn.sigmoid(pre_bc)
    bc = (pre_bc * sig_bc).astype(bf16)
    half = bc.shape[1] // 2
    b_in, c_out = bc[:, :half], bc[:, half:]
    raw, dt, rate, logs, grow, fade, last = step_rows(pdt[...], vec[...])
    columns = jnp.transpose(jnp.concatenate([logs, grow, fade, dt], axis=0))
    z = pz[...]
    sig_z = jax.nn.sigmoid(z)
    g = gym[...]
    g_pz[...] = (g * kept[...].astype(f32) * (sig_z * (1.0 + z * (1.0 - sig_z)))).astype(bf16)
    dy = g * (z * sig_z)
    dy_low = dy.astype(bf16)
    u_low = u.astype(bf16)
    before = states[0]
    before_low = before.astype(bf16)
    d_after = d_state[...]
    d_after_low = d_after.astype(bf16)
    causal = iota((size, size), 0) <= iota((size, size), 1)
    mixing = dot_nt(b_in, c_out)
    low = iota((size, 2 * HEAD), 1) < HEAD
    d_mixing = jnp.zeros((size, size), f32)
    du_local, col_sums, row_sums = [], [], []
    for pair in range(heads // 2):
        lanes = slice(pair * 2 * HEAD, (pair + 1) * 2 * HEAD)
        u_piece, dy_piece = u_low[:, lanes], dy_low[:, lanes]
        outs = []
        for h in (2 * pair, 2 * pair + 1):
            dt_col = columns[:, 24 + h : 25 + h]
            spread = jnp.where(causal, logs[h : h + 1] - columns[:, h : h + 1], -1e30)
            decay = jnp.exp(spread)
            keep = low if h % 2 == 0 else jnp.logical_not(low)
            masked = jnp.where(keep, u_piece, jnp.zeros_like(u_piece))
            product = dot_nt(masked, dy_piece) * decay
            d_mixing = d_mixing + product * dt_col
            product = product * mixing
            col_sums.append(jnp.sum(product, axis=1, keepdims=True))
            row_sums.append(jnp.sum(product * dt_col, axis=0, keepdims=True))
            outs.append(dot_nn((mixing * decay).astype(bf16), dy_piece))
        du_local.append(jnp.where(low, outs[0], outs[1]))
    grow_all = head_columns(columns[:, 8:16], heads)
    fade_all = head_columns(columns[:, 16:24], heads)
    dt_all = head_columns(columns[:, 24:32], heads)
    dy_grown = dy * grow_all
    dy_grown_low = dy_grown.astype(bf16)
    fed_low = (u * fade_all * dt_all).astype(bf16)
    back = dot_nn(b_in, d_after_low) * fade_all
    inter = head_sums(dy_grown * dot_nn(c_out, before_low), heads)
    tails = head_sums(u * back, heads)
    skip = head_columns(jnp.transpose(jnp.broadcast_to(vec[:, 2:3], (8, size))), heads)
    du = (jnp.concatenate(du_local, axis=1) + back) * dt_all + skip * dy
    d_mixing_low = d_mixing.astype(bf16)
    db = dot_nn(d_mixing_low, c_out) + dot_nt(fed_low, d_after_low)
    dc = dot_tn(d_mixing_low, b_in) + dot_nt(dy_grown_low, before_low)
    end = head_columns(jnp.transpose(jnp.broadcast_to(last, (8, 128))), heads)[:1]
    ended = d_after * end
    ends = head_sums(jnp.sum(ended * before, axis=0, keepdims=True), heads)
    d_state[...] = ended + dot_tn(c_out, dy_grown_low)
    lane = iota((size, 128), 1)
    gathered = jnp.zeros((size, 128), f32)
    for h in range(heads):
        gathered = jnp.where(lane == h, col_sums[h] + tails[h], gathered)
        gathered = jnp.where(lane == 8 + h, tails[h], gathered)
        gathered = jnp.where(lane == 16 + h, inter[h], gathered)
    turned = jnp.transpose(gathered)
    direct, tail_row, inter_row = turned[0:8], turned[8:16], turned[16:24]
    pad = [jnp.zeros((1, size), f32)] * (8 - heads)
    row_sum = jnp.concatenate(row_sums + pad, axis=0)
    zero = jnp.zeros((1, 1), f32)
    end_col = jnp.concatenate(ends + [zero] * (8 - heads), axis=0)
    d_logs = row_sum + inter_row - dt * direct
    at_last = end_col + jnp.sum(dt * tail_row, axis=1, keepdims=True)
    lower = (iota((size, size), 0) >= iota((size, size), 1)).astype(f32)
    d_rate = dot_exact(d_logs, lower) + at_last
    d_dt = direct + rate * d_rate
    d_raw = d_dt * jax.nn.sigmoid(raw)
    g_pdt[...] = d_raw
    g_vec[0:8] += d_raw
    g_vec[8:16] += rate * dt * d_rate
    g_skip[...] += jnp.sum((dy * u).reshape(size // 8, 8, u.shape[1]), axis=0)
    d_pre = du * (sig_u * (1.0 + pre_u * (1.0 - sig_u)))
    g_px[...] = conv_rows_back(d_pre, next_px[...], taps[...]).astype(bf16)
    g_taps[...] += conv_taps_back(tail_x, block_x, d_pre)
    next_px[...] = d_pre[:8]
    d_bc = jnp.concatenate([db, dc], axis=1) * (sig_bc * (1.0 + pre_bc * (1.0 - sig_bc)))
    g_pbc[...] = conv_rows_back(d_bc, next_bc[...], shared_taps[...]).astype(bf16)
    g_shared[...] += conv_taps_back(tail_bc, block_bc, d_bc)
    next_bc[...] = d_bc[:8]


def pad_rows(value):
    return jnp.pad(value, ((0, -value.shape[0] % 8), (0, 0)))


def vec_of(step_bias, decay_log, skip_gain):
    table = jnp.stack([step_bias, decay_log, skip_gain], axis=1)
    return jnp.pad(table, ((0, 8 - table.shape[0]), (0, 128 - table.shape[1])))


def whole(shape):
    return pl.BlockSpec(shape, lambda i: tuple(0 for _ in shape))


def mamba_fwd(px, pz, pbc, pdt, taps, shared_taps, vec, heads):
    length, chans = px.shape
    wide = pbc.shape[1]
    steps = length // CHUNK
    per = CHUNK // 8

    def at(cols):
        return pl.BlockSpec((CHUNK, cols), lambda i: (i, 0))

    def tail(cols):
        return pl.BlockSpec((8, cols), lambda i: (jnp.maximum(i * per - 1, 0), 0))

    return pl.pallas_call(
        functools.partial(mamba_fwd_kernel, heads),
        grid=(steps,),
        in_specs=[
            at(chans),
            tail(chans),
            at(chans),
            at(wide),
            tail(wide),
            pl.BlockSpec((8, CHUNK), lambda i: (0, i)),
            whole((8, chans)),
            whole((8, wide)),
            whole((8, 128)),
        ],
        out_specs=[
            at(chans),
            at(chans),
            pl.BlockSpec((1, wide // 2, chans), lambda i: (i, 0, 0)),
        ],
        out_shape=[
            jax.ShapeDtypeStruct((length, chans), bf16),
            jax.ShapeDtypeStruct((length, chans), bf16),
            jax.ShapeDtypeStruct((steps, wide // 2, chans), f32),
        ],
        scratch_shapes=[pltpu.VMEM((wide // 2, chans), f32)],
        name="mamba_forward",
    )(px, px, pz, pbc, pbc, pdt, taps, shared_taps, vec)


def mamba_bwd(px, pz, pbc, pdt, taps, shared_taps, vec, kept, states, gym, heads):
    length, chans = px.shape
    wide = pbc.shape[1]
    steps = length // CHUNK
    per = CHUNK // 8

    def at(cols):
        return pl.BlockSpec((CHUNK, cols), lambda i: (steps - 1 - i, 0))

    def tail(cols):
        return pl.BlockSpec((8, cols), lambda i: (jnp.maximum((steps - 1 - i) * per - 1, 0), 0))

    row = pl.BlockSpec((8, CHUNK), lambda i: (0, steps - 1 - i))
    return pl.pallas_call(
        functools.partial(mamba_bwd_kernel, heads),
        grid=(steps,),
        in_specs=[
            at(chans),
            tail(chans),
            at(chans),
            at(wide),
            tail(wide),
            row,
            whole((8, chans)),
            whole((8, wide)),
            whole((8, 128)),
            at(chans),
            pl.BlockSpec((1, wide // 2, chans), lambda i: (steps - 1 - i, 0, 0)),
            at(chans),
        ],
        out_specs=[
            at(chans),
            at(chans),
            at(wide),
            row,
            whole((8, chans)),
            whole((8, wide)),
            whole((16, 128)),
            whole((8, chans)),
        ],
        out_shape=[
            jax.ShapeDtypeStruct((length, chans), bf16),
            jax.ShapeDtypeStruct((length, chans), bf16),
            jax.ShapeDtypeStruct((length, wide), bf16),
            jax.ShapeDtypeStruct((8, length), f32),
            jax.ShapeDtypeStruct((8, chans), f32),
            jax.ShapeDtypeStruct((8, wide), f32),
            jax.ShapeDtypeStruct((16, 128), f32),
            jax.ShapeDtypeStruct((8, chans), f32),
        ],
        scratch_shapes=[
            pltpu.VMEM((wide // 2, chans), f32),
            pltpu.VMEM((8, chans), f32),
            pltpu.VMEM((8, wide), f32),
        ],
        name="mamba_backward",
    )(px, px, pz, pbc, pbc, pdt, taps, shared_taps, vec, kept, states, gym)


ROWS = 256


def turn(pre, cosine, sine):
    inner = iota(pre.shape, 1) % HEAD < HEAD // 2
    lanes = pre.shape[1]
    other = jnp.where(
        inner, pltpu.roll(pre, lanes - HEAD // 2, 1), pltpu.roll(pre, HEAD // 2, 1)
    )
    return pre * cosine + other * sine


def attend_fwd_kernel(scale, qkv, cosine, sine, out):
    length, wide = out.shape
    low = iota((ROWS, 2 * HEAD), 1) < HEAD
    q = turn(qkv[:, :wide], cosine[...], sine[...]).astype(bf16)
    k = turn(qkv[:, wide : 2 * wide], cosine[...], sine[...]).astype(bf16)
    v = qkv[:, 2 * wide :].astype(bf16)
    for i in range(length // ROWS):
        seen = (i + 1) * ROWS
        block = q[i * ROWS : (i + 1) * ROWS]
        keys, values = k[:seen], v[:seen]
        allowed = iota((ROWS, seen), 1) <= iota((ROWS, seen), 0) + i * ROWS
        outs = []
        for h in range(2):
            keep = low if h == 0 else jnp.logical_not(low)
            part = jnp.where(keep, block, jnp.zeros_like(block))
            scores = jnp.where(allowed, dot_nt(part, keys) * scale, -1e30)
            expo = jnp.exp(scores - jnp.max(scores, axis=1, keepdims=True))
            chance = expo * (1.0 / jnp.sum(expo, axis=1, keepdims=True))
            outs.append(dot_nn(chance.astype(bf16), values))
        out[i * ROWS : (i + 1) * ROWS] = jnp.where(low, outs[0], outs[1]).astype(bf16)


def attend_bwd_kernel(scale, qkv, cosine, sine, go, g_qkv, dk, dv):
    length, wide = dk.shape
    low = iota((ROWS, 2 * HEAD), 1) < HEAD
    q = turn(qkv[:, :wide], cosine[...], sine[...]).astype(bf16)
    k = turn(qkv[:, wide : 2 * wide], cosine[...], sine[...]).astype(bf16)
    v = qkv[:, 2 * wide :].astype(bf16)
    dk[...] = jnp.zeros_like(dk)
    dv[...] = jnp.zeros_like(dv)
    for i in range(length // ROWS):
        seen = (i + 1) * ROWS
        rows = slice(i * ROWS, (i + 1) * ROWS)
        block, grads = q[rows], go[rows]
        keys, values = k[:seen], v[:seen]
        allowed = iota((seen, ROWS), 0) <= iota((seen, ROWS), 1) + i * ROWS
        dqs, dks, dvs = [], [], []
        for h in range(2):
            keep = low if h == 0 else jnp.logical_not(low)
            part = jnp.where(keep, block, jnp.zeros_like(block))
            part_g = jnp.where(keep, grads, jnp.zeros_like(grads))
            scores = jnp.where(allowed, dot_nt(keys, part) * scale, -1e30)
            expo = jnp.exp(scores - jnp.max(scores, axis=0, keepdims=True))
            chance = expo * (1.0 / jnp.sum(expo, axis=0, keepdims=True))
            g_chance = dot_nt(values, part_g)
            center = jnp.sum(chance * g_chance, axis=0, keepdims=True)
            g_scores = (chance * (g_chance - center)).astype(bf16)
            dqs.append(dot_tn(g_scores, keys))
            dks.append(dot_nn(g_scores, part))
            dvs.append(dot_nn(chance.astype(bf16), part_g))
        dq = jnp.where(low, dqs[0], dqs[1]) * scale
        g_qkv[rows, :wide] = turn(dq, cosine[rows], -sine[rows]).astype(bf16)
        dk[:seen] += (dks[0] + dks[1]) * scale
        dv[:seen] += dvs[0] + dvs[1]
    all_low = iota((length, wide), 1) < HEAD
    g_k, g_v = dk[...], dv[...]
    g_k = turn(g_k + pltpu.roll(g_k, HEAD, 1), cosine[...], -sine[...])
    g_v = g_v + pltpu.roll(g_v, HEAD, 1)
    g_qkv[:, wide:] = jnp.where(all_low, g_k, g_v).astype(bf16)


def attend_fwd(qkv, cosine, sine):
    length, wide = cosine.shape
    return pl.pallas_call(
        functools.partial(attend_fwd_kernel, HEAD**-0.5),
        out_shape=jax.ShapeDtypeStruct((length, wide), bf16),
        name="attend_forward",
    )(qkv, cosine, sine)


def attend_bwd(qkv, cosine, sine, go):
    length, wide = cosine.shape
    return pl.pallas_call(
        functools.partial(attend_bwd_kernel, HEAD**-0.5),
        out_shape=jax.ShapeDtypeStruct((length, 2 * wide), bf16),
        scratch_shapes=[pltpu.VMEM((length, wide), f32)] * 2,
        name="attend_backward",
    )(qkv, cosine, sine, go)


def rotary_tables(length):
    half = HEAD // 2
    frequency = rotary_base ** (-2.0 * jnp.arange(half, dtype=f32) / HEAD)
    angles = jnp.arange(length, dtype=f32)[:, None] * frequency[None, :]
    cosine, sine = jnp.cos(angles), jnp.sin(angles)
    return (
        jnp.concatenate([cosine] * 4, axis=1),
        jnp.concatenate([-sine, sine, -sine, sine], axis=1),
    )


def swiglu(gate_part, up_part):
    return jax.nn.silu(gate_part) * up_part


def mm(a, b):
    return jnp.dot(a, b, preferred_element_type=f32)


def mm_t(a, b):
    return lax.dot_general(a, b, (((1,), (1,)), ((), ())), preferred_element_type=f32)


def t_mm(a, b):
    return lax.dot_general(a, b, (((0,), (0,)), ((), ())), preferred_element_type=f32)


def body(
    layer_in,
    out_grad,
    lengths,
    mamba_x,
    mamba_z,
    mamba_step,
    query_proj,
    key_proj,
    value_proj,
    mamba_out,
    attend_out,
    mlp_gate,
    mlp_up,
    mlp_down,
    state_proj,
    conv_state,
    norm_gains,
    conv_mamba,
    step_bias,
    decay_log,
    skip_gain,
):
    ranks = lax.axis_size("tensor")
    assert ranks == 4 and layer_in.shape[1] == 1
    rank = lax.axis_index("tensor")
    y, core = rank // 2, rank % 2
    peers = lax.axis_size("dp")
    me = lax.axis_index("dp")
    rows, _, width = layer_in.shape
    length = rows * ranks
    chans = mamba_x.shape[1]
    heads = step_bias.shape[0]
    q_cols, k_cols = query_proj.shape[1], key_proj.shape[1]
    ff = mlp_gate.shape[1]
    d_rows = width // peers
    n2 = state_proj.shape[1]

    own_in = blocks_by_xor(layer_in[:, 0], me, peers, 1)
    own_go = blocks_by_xor(out_grad[:, 0], me, peers, 1)
    in_pair = gather_y(own_in, y)
    in_full = gather_core(in_pair, core)

    taps_own = conv_state.shape[1]
    gains_own = norm_gains.shape[1]
    small = jnp.concatenate([conv_state.reshape(-1), norm_gains.reshape(-1)])
    fill = -small.shape[0] % 128
    small = jnp.pad(small, (0, fill)).reshape(1, -1)
    small = gather_core(gather_y(small, y), core)
    small = gather_pieces(small[None], "dp")
    cut = conv_state.size
    taps_pieces = small[:, :, :cut].reshape(peers, ranks, conv_state.shape[0], taps_own)
    taps_rel = jnp.transpose(taps_pieces, (2, 0, 1, 3)).reshape(conv_state.shape[0], -1)
    conv_shared = blocks_back(taps_rel, me, peers, 1)
    gain_pair = jnp.transpose(
        small[:, :, cut : cut + norm_gains.size].reshape(peers, ranks, 2, gains_own), (2, 0, 1, 3)
    ).reshape(2, width)

    step_pad = -heads % 128
    pack_a = jnp.concatenate(
        [mamba_x.astype(bf16), jnp.pad(mamba_step.astype(bf16), ((0, 0), (0, step_pad)))], axis=1
    )
    w_a = gather_pieces(pack_a, "dp")
    state_own = gather_core(gather_y(state_proj.astype(bf16), y), core)
    w_bc = gather_pieces(state_own, "dp")
    pack_b = jnp.concatenate(
        [item.astype(bf16) for item in (mamba_z, query_proj, key_proj, value_proj)], axis=1
    )
    w_b = gather_pieces(pack_b, "dp")
    pack_o = jnp.concatenate([mamba_out.T.astype(bf16), attend_out.T.astype(bf16)], axis=1)
    w_o = gather_pieces(pack_o, "dp")
    pack_m = jnp.concatenate(
        [mlp_gate.astype(bf16), mlp_up.astype(bf16), mlp_down.T.astype(bf16)], axis=1
    )
    w_m = gather_pieces(pack_m, "dp")

    limit = lengths[0]
    go_pair = gather_y(own_go, y)
    go_full = gather_core(go_pair, core)
    all_valid = jnp.arange(length, dtype=jnp.int32) < limit
    block_valid = all_valid.reshape(2, 2, rows)
    pair_valid = pick(core, block_valid[:, 1], block_valid[:, 0])
    gf = jnp.where(all_valid[:, None], go_full, 0).astype(bf16)

    def norm_parts(values):
        rho = lax.rsqrt(jnp.mean(values * values, axis=-1, keepdims=True) + epsilon)
        return rho

    x_full = in_full.astype(f32)
    rho_one = norm_parts(x_full)
    a1 = (x_full * rho_one * gain_pair[0]).astype(bf16)

    w_x, w_dt = w_a[:, :chans], w_a[:, chans : chans + 8]
    w_z = w_b[:, :chans]
    w_qkv = w_b[:, chans:]
    w_k, w_v = w_qkv[:, q_cols : q_cols + k_cols], w_qkv[:, q_cols + k_cols :]
    w_att = jnp.concatenate([w_qkv[:, :q_cols], w_k, w_k, w_v, w_v], axis=1)
    px, pz, pbc, qkv = mm(a1, w_x), mm(a1, w_z), mm(a1, w_bc), mm(a1, w_att)
    pdt = lax.dot_general(w_dt, a1, (((0,), (1,)), ((), ())), preferred_element_type=f32)
    vec = vec_of(step_bias, decay_log, skip_gain)
    taps, shared_taps = pad_rows(conv_mamba), pad_rows(conv_shared)
    om, kept, states = mamba_fwd(px, pz, pbc, pdt, taps, shared_taps, vec, heads)
    cosine, sine = rotary_tables(length)
    oa = attend_fwd(qkv, cosine, sine)
    mixed_in = jnp.concatenate([om, oa], axis=1)
    m_pair = reduce_y_both(reduce_core(mm_t(mixed_in, w_o).astype(bf16), core))
    r1 = in_pair.astype(f32) + m_pair
    rho_two = norm_parts(r1)
    a2_pair = (r1 * rho_two * gain_pair[1]).astype(bf16)
    a2 = gather_core(a2_pair, core)
    w_gu, w_dn = w_m[:, : 2 * ff], w_m[:, 2 * ff :]
    gate_up = mm(a2, w_gu)
    gate, up = gate_up[:, :ff], gate_up[:, ff:]
    hidden_full, glu_back = jax.vjp(swiglu, gate, up)
    hid = hidden_full.astype(bf16)
    ffn = reduce_y_own(reduce_core(mm_t(hid, w_dn).astype(bf16), core), y)
    r1_own = pick(y, r1[1], r1[0])
    own_valid = pick(y, pair_valid[1], pair_valid[0])
    layer_out = jnp.where(own_valid[:, None], r1_own + ffn, 0.0).astype(bf16)
    layer_out = blocks_back(layer_out, me, peers, 1)[:, None]

    g_hid = mm(gf, w_dn)
    gate_grad, up_grad = glu_back(g_hid)
    g_gu = jnp.concatenate([gate_grad.astype(bf16), up_grad.astype(bf16)], axis=1)
    g_a2_pair = reduce_y_both(reduce_core(mm_t(g_gu, w_gu).astype(bf16), core))
    n_two = r1 * rho_two
    e_two = g_a2_pair * gain_pair[1]
    gf_pair = jnp.where(pair_valid[:, :, None], go_pair.astype(f32), 0.0)
    g_r1 = gf_pair + rho_two * (e_two - n_two * jnp.mean(e_two * n_two, axis=-1, keepdims=True))
    gain_two_pair = jnp.sum(g_a2_pair * n_two, axis=1)
    gain_two_grad = pick(y, gain_two_pair[1], gain_two_pair[0])
    g_m = gather_core(g_r1.astype(bf16), core)
    g_mix = mm(g_m, w_o)
    g_ym = g_mix[:, :chans]
    g_oa = g_mix[:, chans:].astype(bf16)

    mlp_w_grad = jnp.concatenate([t_mm(a2, g_gu), t_mm(gf, hid)], axis=1)
    mlp_sum = scatter_sum(mlp_w_grad, "dp")
    out_sum = scatter_sum(t_mm(g_m, mixed_in), "dp")

    g_qkv = attend_bwd(qkv, cosine, sine, g_oa)
    g_px, g_pz, g_bc, g_pdt, g_taps, g_shared, g_vec, g_skip = mamba_bwd(
        px, pz, pbc, pdt, taps, shared_taps, vec, kept, states, g_ym, heads
    )
    conv_taps_grad = g_taps[: conv_mamba.shape[0]]
    conv_shared_grad = g_shared[: conv_state.shape[0]]
    bias_grad = jnp.sum(g_vec[:heads], axis=1)
    decay_grad = jnp.sum(g_vec[8 : 8 + heads], axis=1)
    skip_grad = jnp.sum(g_skip.reshape(8, heads, HEAD), axis=(0, 2))
    g_pdt = g_pdt.astype(bf16)
    step_w_grad = lax.dot_general(
        a1, g_pdt, (((0,), (1,)), ((), ())), preferred_element_type=f32
    )
    step_w_grad = jnp.pad(step_w_grad, ((0, 0), (0, 120)))
    b_sum = scatter_sum(jnp.concatenate([t_mm(a1, g_pz), t_mm(a1, g_qkv)], axis=1), "dp")
    a_sum = scatter_sum(jnp.concatenate([t_mm(a1, g_px), step_w_grad], axis=1), "dp")
    state_part = t_mm(a1, g_bc).astype(bf16).reshape(peers, 4, gains_own, n2)
    state_part = jnp.swapaxes(state_part, 0, 1).reshape(4 * peers * gains_own, n2)
    state_part = reduce_y_own(reduce_core(state_part, core), y)
    state_proj_grad = scatter_sum(state_part, "dp")

    g_a1_part = (
        mm_t(g_pz, w_z)
        + mm_t(g_qkv, w_qkv)
        + mm_t(g_px, w_x)
        + mm_t(g_bc, w_bc)
        + lax.dot_general(g_pdt, w_dt, (((0,), (1,)), ((), ())), preferred_element_type=f32)
    )
    gain_one_grad = jnp.sum(g_a1_part * (x_full * rho_one), axis=0)
    g_a1 = reduce_y_own(reduce_core(g_a1_part.astype(bf16), core), y)
    x_own = own_in.astype(f32)
    rho_own = norm_parts(x_own)
    n_one = x_own * rho_own
    e_one = g_a1 * gain_pair[0]
    g_r1_own = pick(y, g_r1[1], g_r1[0])
    in_grad = g_r1_own + rho_own * (e_one - n_one * jnp.mean(e_one * n_one, axis=-1, keepdims=True))
    in_grad = blocks_back(in_grad.astype(bf16), me, peers, 1)[:, None]

    gain_grads = blocks_back(jnp.stack([gain_one_grad, gain_two_grad]), me, peers, 1)
    both = jnp.concatenate([conv_shared_grad.reshape(-1), gain_grads.reshape(-1)])
    both_rows = -(-both.shape[0] // 128)
    both = jnp.pad(both, (0, both_rows * 128 - both.shape[0]))
    only = jnp.concatenate([conv_taps_grad.reshape(-1), bias_grad, decay_grad, skip_grad])
    only_count = only.shape[0]
    only = jnp.pad(only, (0, -only_count % 128))
    packed = jnp.concatenate([both, only]).reshape(-1, 128)
    for bit in range(bits_of(peers)):
        packed = packed + flip(packed, "dp", 1 << bit)
    both = packed[:both_rows]
    for mask in (1, 2):
        both = both + flip(both, "tensor", mask)
    both = both.reshape(-1)
    only = packed[both_rows:].reshape(-1)
    conv_state_sum = both[: conv_shared.size].reshape(conv_shared.shape)
    gain_sum = both[conv_shared.size : conv_shared.size + 2 * width].reshape(2, width)
    member = me * ranks + rank
    conv_state_grad = lax.dynamic_slice_in_dim(conv_state_sum, member * taps_own, taps_own, 1)
    norm_gains_grad = lax.dynamic_slice_in_dim(gain_sum, member * gains_own, gains_own, 1)
    cut = conv_taps_grad.size
    conv_mamba_grad = only[:cut].reshape(conv_taps_grad.shape)
    step_bias_grad = only[cut : cut + heads]
    decay_log_grad = only[cut + heads : cut + 2 * heads]
    skip_gain_grad = only[cut + 2 * heads : cut + 3 * heads]

    return (
        layer_out,
        in_grad,
        a_sum[:, :chans],
        b_sum[:, :chans],
        a_sum[:, chans : chans + heads],
        b_sum[:, chans : chans + q_cols],
        b_sum[:, chans + q_cols : chans + q_cols + k_cols],
        b_sum[:, chans + q_cols + k_cols :],
        out_sum[:, :chans].T,
        out_sum[:, chans:].T,
        mlp_sum[:, :ff],
        mlp_sum[:, ff : 2 * ff],
        mlp_sum[:, 2 * ff :].T,
        state_proj_grad,
        conv_state_grad,
        norm_gains_grad,
        conv_mamba_grad,
        step_bias_grad,
        decay_log_grad,
        skip_gain_grad,
    )


def solution(mesh):
    in_specs = (
        P("tensor", "dp", None),
        P("tensor", "dp", None),
        P("dp"),
        P("dp", "tensor"),
        P("dp", "tensor"),
        P("dp", "tensor"),
        P("dp", "tensor"),
        P("dp", "tensor"),
        P("dp", "tensor"),
        P("tensor", "dp"),
        P("tensor", "dp"),
        P("dp", "tensor"),
        P("dp", "tensor"),
        P("tensor", "dp"),
        P(("dp", "tensor"), None),
        P(None, ("dp", "tensor")),
        P(None, ("dp", "tensor")),
        P(None, "tensor"),
        P("tensor"),
        P("tensor"),
        P("tensor"),
    )
    out_specs = (
        P("tensor", "dp", None),
        P("tensor", "dp", None),
        P("dp", "tensor"),
        P("dp", "tensor"),
        P("dp", "tensor"),
        P("dp", "tensor"),
        P("dp", "tensor"),
        P("dp", "tensor"),
        P("tensor", "dp"),
        P("tensor", "dp"),
        P("dp", "tensor"),
        P("dp", "tensor"),
        P("tensor", "dp"),
        P(("dp", "tensor"), None),
        P(None, ("dp", "tensor")),
        P(None, ("dp", "tensor")),
        P(None, "tensor"),
        P("tensor"),
        P("tensor"),
        P("tensor"),
    )
    return jax.shard_map(body, mesh=mesh, in_specs=in_specs, out_specs=out_specs, check_vma=False)
```

```python
import functools

import jax
import jax.numpy as jnp
from jax import lax
from jax.experimental import pallas as pl
from jax.experimental.pallas import tpu as pltpu
from jax.sharding import PartitionSpec as P

epsilon = 1e-05
rotary_base = 100000000000.0
HIGHEST = lax.Precision.HIGHEST
bf16 = jnp.bfloat16
f32 = jnp.float32


def flip(value, axis, mask):
    size = lax.axis_size(axis)
    return lax.ppermute(value, axis, [(i, i ^ mask) for i in range(size)])


def bits_of(size):
    bits = size.bit_length() - 1
    assert size == 1 << bits
    return bits


def relative_order(size):
    order = [0]
    for bit in reversed(range(bits_of(size))):
        order = order + [k | (1 << bit) for k in order]
    return order


def gather_pieces(own, axis, early=False):
    size = lax.axis_size(axis)
    if early and size == 8:
        four, two = flip(own, axis, 4), flip(own, axis, 2)
        first = jnp.concatenate([own, two], axis=0)
        first_other = flip(first, axis, 1)
        six = flip(four, axis, 2)
        second = jnp.concatenate([four, six], axis=0)
        second_other = flip(second, axis, 1)
        return jnp.concatenate([own, four, two, six] + [
            part[i * own.shape[0] : (i + 1) * own.shape[0]]
            for i in range(2)
            for part in (first_other, second_other)
        ], axis=0)
    held = own
    for bit in reversed(range(bits_of(size))):
        held = jnp.concatenate([held, flip(held, axis, 1 << bit)], axis=0)
    return held


def scatter_sum(kept, sent, axis):
    for bit in range(bits_of(lax.axis_size(axis))):
        kept = kept + flip(sent, axis, 1 << bit).astype(f32)
        half = kept.shape[0] // 2
        if bit + 1 < bits_of(lax.axis_size(axis)):
            kept, sent = kept[:half], kept[half:].astype(bf16)
    return kept


def sum_of_products(pairs, axis):
    half = pairs[0][0].shape[1] // 2
    sent = sum(t_mm(left[:, half:], right) for left, right in pairs).astype(bf16)
    kept = sum(t_mm(left[:, :half], right) for left, right in pairs)
    return kept, sent


def move_kernel(back, order, me, source, target):
    width = source.shape[1] // len(order)
    for p, k in enumerate(order):
        there = pl.ds(pl.multiple_of((me[0] ^ k) * width, width), width)
        here = slice(p * width, (p + 1) * width)
        if back:
            target[:, there] = source[:, here]
        else:
            target[:, here] = source[:, there]


def move_blocks(value, member, size, back):
    width = value.shape[1] // size
    if width % 128 == 0:
        return pl.pallas_call(
            functools.partial(move_kernel, back, relative_order(size)),
            grid_spec=pltpu.PrefetchScalarGridSpec(
                num_scalar_prefetch=1,
                grid=(1,),
                in_specs=[whole(value.shape)],
                out_specs=whole(value.shape),
            ),
            out_shape=jax.ShapeDtypeStruct(value.shape, value.dtype),
            cost_estimate=cost(0, 2 * value.size * value.dtype.itemsize, 0),
            name="move_blocks",
        )(member.reshape(1), value)
    return take_blocks(value, member, size, back)


def take_blocks(value, member, size, back):
    order = relative_order(size)
    where = [0] * size
    for p, k in enumerate(order):
        where[k] = p
    if back:
        index = jnp.array(where, jnp.int32)[member ^ jnp.arange(size, dtype=jnp.int32)]
    else:
        index = member ^ jnp.array(order, jnp.int32)
    cut = value.reshape(value.shape[0], size, -1)
    return jnp.take(cut, index, axis=1).reshape(value.shape)


def pick(bit, one, zero):
    return jnp.where(bit == 1, one, zero)


def after(value, *others):
    return lax.optimization_barrier((value,) + others)[0]


def flip_core(value):
    return flip(value, "tensor", 1)


def flip_y(value):
    return flip(value, "tensor", 2)


def in_rank_order(own, y, core):
    other = flip_y(own)
    pair = jnp.stack([pick(y, other, own), pick(y, own, other)])
    other = flip_core(pair)
    both = jnp.stack([pick(core, other, pair), pick(core, pair, other)], axis=1)
    return both.reshape((4,) + own.shape)


def core_sum(kept, sent):
    return (kept + flip_core(sent.astype(bf16)).astype(f32)).astype(bf16)


def y_sum(kept, sent):
    return kept.astype(f32) + flip_y(sent).astype(f32)


CHUNK = 128
HEAD = 64
TAPS = 4


def dot_nn(a, b):
    return lax.dot_general(a, b, (((1,), (0,)), ((), ())), preferred_element_type=f32)


def dot_nt(a, b):
    return lax.dot_general(a, b, (((1,), (1,)), ((), ())), preferred_element_type=f32)


def dot_tn(a, b):
    return lax.dot_general(a, b, (((0,), (0,)), ((), ())), preferred_element_type=f32)


def dot_exact(a, b):
    return lax.dot_general(
        a, b, (((1,), (0,)), ((), ())), precision=HIGHEST, preferred_element_type=f32
    )


def iota(shape, axis):
    return lax.broadcasted_iota(jnp.int32, shape, axis)


def earlier(tail, block, back):
    if back == 0:
        return block
    return pltpu.roll(jnp.concatenate([tail, block], axis=0), back, 0)[8:]


def later(block, head, ahead):
    if ahead == 0:
        return block
    both = jnp.concatenate([block, head], axis=0)
    return pltpu.roll(both, both.shape[0] - ahead, 0)[: block.shape[0]]


def conv_rows(tail, block, taps):
    total = block * taps[TAPS - 1 : TAPS] + taps[TAPS : TAPS + 1]
    for j in range(TAPS - 1):
        total = total + earlier(tail, block, TAPS - 1 - j) * taps[j : j + 1]
    return total


def conv_rows_back(grad, head, taps):
    total = grad * taps[TAPS - 1 : TAPS]
    for j in range(TAPS - 1):
        total = total + later(grad, head, TAPS - 1 - j) * taps[j : j + 1]
    return total


def conv_taps_back(tail, block, grad):
    rows = [
        jnp.sum(earlier(tail, block, TAPS - 1 - j) * grad, axis=0, keepdims=True)
        for j in range(TAPS)
    ]
    rows.append(jnp.sum(grad, axis=0, keepdims=True))
    rows.append(jnp.zeros((8 - len(rows), grad.shape[1]), f32))
    return jnp.concatenate(rows, axis=0)


def head_columns(columns, heads):
    rows = columns.shape[0]
    low = iota((rows, 2 * HEAD), 1) < HEAD
    return jnp.concatenate(
        [
            jnp.where(low, columns[:, h : h + 1], columns[:, h + 1 : h + 2])
            for h in range(0, heads, 2)
        ],
        axis=1,
    )


def head_sums(values, heads):
    rows = values.shape[0]
    low = iota((rows, 2 * HEAD), 1) < HEAD
    sums = []
    for pair in range(heads // 2):
        part = values[:, pair * 2 * HEAD : (pair + 1) * 2 * HEAD]
        sums.append(jnp.sum(jnp.where(low, part, 0.0), axis=1, keepdims=True))
        sums.append(jnp.sum(jnp.where(low, 0.0, part), axis=1, keepdims=True))
    return sums


def softplus(value):
    return jnp.maximum(value, 0.0) + jnp.log1p(jnp.exp(-jnp.abs(value)))


def step_rows(pdt, vec):
    size = pdt.shape[1]
    raw = pdt + vec[:, 0:1]
    dt = softplus(raw)
    rate = -jnp.exp(vec[:, 1:2])
    upper = (iota((size, size), 0) <= iota((size, size), 1)).astype(f32)
    logs = dot_exact(dt * rate, upper)
    last = logs[:, size - 1 : size]
    return raw, dt, rate, logs, jnp.exp(logs), jnp.exp(last - logs), jnp.exp(last)


def mamba_fwd_kernel(
    heads,
    rank,
    px,
    px_tail,
    pz,
    pbc,
    pbc_tail,
    pdt,
    taps,
    shared_taps,
    vec,
    om,
    kept,
    states,
    state,
):
    step = pl.program_id(0)

    @pl.when(step == 0)
    def _():
        state[...] = jnp.zeros_like(state)

    started = jnp.where(step == 0, 0.0, 1.0)
    u = conv_rows(px_tail[...] * started, px[...], taps[...])
    u = u * jax.nn.sigmoid(u)
    bc = conv_rows(pbc_tail[...] * started, pbc[...], shared_taps[...])
    bc = (bc * jax.nn.sigmoid(bc)).astype(bf16)
    half = bc.shape[1] // 2
    b_in, c_out = bc[:, :half], bc[:, half:]
    _, dt, _, logs, grow, fade, last = step_rows(pdt[...], vec[...])
    columns = jnp.transpose(jnp.concatenate([logs, grow, fade * dt, dt], axis=0))
    size = u.shape[0]
    causal = iota((size, size), 0) >= iota((size, size), 1)
    mixing = dot_nt(c_out, b_in)
    u_low = u.astype(bf16)
    low = iota((size, 2 * HEAD), 1) < HEAD
    local = []
    for pair in range(heads // 2):
        piece = u_low[:, pair * 2 * HEAD : (pair + 1) * 2 * HEAD]
        outs = []
        for h in (2 * pair, 2 * pair + 1):
            spread = jnp.where(causal, columns[:, h : h + 1] - logs[h : h + 1], -1e30)
            matrix = (mixing * jnp.exp(spread) * dt[h : h + 1]).astype(bf16)
            outs.append(dot_nn(matrix, piece))
        local.append(jnp.where(low, outs[0], outs[1]))
    before = state[...]
    states[0] = before
    carried = dot_nn(c_out, before.astype(bf16)) * head_columns(columns[:, 8:16], heads)
    skip = head_columns(jnp.transpose(jnp.broadcast_to(vec[:, 2:3], (8, size))), heads)
    total = jnp.concatenate(local, axis=1) + carried + skip * u
    z = pz[...]
    om[...] = (total * (z * jax.nn.sigmoid(z))).astype(bf16)
    kept[...] = total.astype(bf16)
    fed = (u * head_columns(columns[:, 16:24], heads)).astype(bf16)
    end = head_columns(jnp.transpose(jnp.broadcast_to(last, (8, 128))), heads)[:1]
    state[...] = before * end + dot_tn(b_in, fed)


def mamba_bwd_kernel(
    heads,
    rank,
    px,
    px_tail,
    pz,
    pbc,
    pbc_tail,
    pdt,
    taps,
    shared_taps,
    vec,
    states,
    gym,
    g_pxs,
    g_pbc,
    g_taps,
    g_shared,
    g_vec,
    g_skip,
    d_state,
    next_px,
    next_bc,
):
    step = pl.program_id(0)
    steps = pl.num_programs(0)

    @pl.when(step == 0)
    def _():
        d_state[...] = jnp.zeros_like(d_state)
        next_px[...] = jnp.zeros_like(next_px)
        next_bc[...] = jnp.zeros_like(next_bc)
        g_taps[...] = jnp.zeros_like(g_taps)
        g_shared[...] = jnp.zeros_like(g_shared)
        g_vec[...] = jnp.zeros_like(g_vec)
        g_skip[...] = jnp.zeros_like(g_skip)

    started = jnp.where(step == steps - 1, 0.0, 1.0)
    size = px.shape[0]
    tail_x = px_tail[...] * started
    block_x = px[...]
    pre_u = conv_rows(tail_x, block_x, taps[...])
    sig_u = jax.nn.sigmoid(pre_u)
    u = pre_u * sig_u
    tail_bc = pbc_tail[...] * started
    block_bc = pbc[...]
    pre_bc = conv_rows(tail_bc, block_bc, shared_taps[...])
    sig_bc = jax.nn.sigmoid(pre_bc)
    bc = (pre_bc * sig_bc).astype(bf16)
    half = bc.shape[1] // 2
    b_in, c_out = bc[:, :half], bc[:, half:]
    raw, dt, rate, logs, grow, fade, last = step_rows(pdt[...], vec[...])
    columns = jnp.transpose(jnp.concatenate([logs, grow, fade, dt], axis=0))
    z = pz[...]
    sig_z = jax.nn.sigmoid(z)
    g = gym[...]
    dy = g * (z * sig_z)
    dy_low = dy.astype(bf16)
    u_low = u.astype(bf16)
    before = states[0]
    before_low = before.astype(bf16)
    d_after = d_state[...]
    d_after_low = d_after.astype(bf16)
    causal = iota((size, size), 0) <= iota((size, size), 1)
    mixing = dot_nt(b_in, c_out)
    low = iota((size, 2 * HEAD), 1) < HEAD
    d_mixing = jnp.zeros((size, size), f32)
    du_local, col_sums, row_sums = [], [], []
    for pair in range(heads // 2):
        lanes = slice(pair * 2 * HEAD, (pair + 1) * 2 * HEAD)
        u_piece, dy_piece = u_low[:, lanes], dy_low[:, lanes]
        outs = []
        for h in (2 * pair, 2 * pair + 1):
            dt_col = columns[:, 24 + h : 25 + h]
            spread = jnp.where(causal, logs[h : h + 1] - columns[:, h : h + 1], -1e30)
            decay = jnp.exp(spread)
            keep = low if h % 2 == 0 else jnp.logical_not(low)
            masked = jnp.where(keep, u_piece, jnp.zeros_like(u_piece))
            product = dot_nt(masked, dy_piece) * decay
            d_mixing = d_mixing + product * dt_col
            product = product * mixing
            col_sums.append(jnp.sum(product, axis=1, keepdims=True))
            row_sums.append(jnp.sum(product * dt_col, axis=0, keepdims=True))
            outs.append(dot_nn((mixing * decay).astype(bf16), dy_piece))
        du_local.append(jnp.where(low, outs[0], outs[1]))
    grow_all = head_columns(columns[:, 8:16], heads)
    fade_all = head_columns(columns[:, 16:24], heads)
    dt_all = head_columns(columns[:, 24:32], heads)
    dy_grown = dy * grow_all
    dy_grown_low = dy_grown.astype(bf16)
    fed_low = (u * fade_all * dt_all).astype(bf16)
    back = dot_nn(b_in, d_after_low) * fade_all
    inter = head_sums(dy_grown * dot_nn(c_out, before_low), heads)
    tails = head_sums(u * back, heads)
    skip = head_columns(jnp.transpose(jnp.broadcast_to(vec[:, 2:3], (8, size))), heads)
    du = (jnp.concatenate(du_local, axis=1) + back) * dt_all + skip * dy
    d_mixing_low = d_mixing.astype(bf16)
    db = dot_nn(d_mixing_low, c_out) + dot_nt(fed_low, d_after_low)
    dc = dot_tn(d_mixing_low, b_in) + dot_nt(dy_grown_low, before_low)
    end = head_columns(jnp.transpose(jnp.broadcast_to(last, (8, 128))), heads)[:1]
    ended = d_after * end
    ends = head_sums(jnp.sum(ended * before, axis=0, keepdims=True), heads)
    d_state[...] = ended + dot_tn(c_out, dy_grown_low)
    lane = iota((size, 128), 1)
    gathered = jnp.zeros((size, 128), f32)
    for h in range(heads):
        gathered = jnp.where(lane == h, col_sums[h] + tails[h], gathered)
        gathered = jnp.where(lane == 8 + h, tails[h], gathered)
        gathered = jnp.where(lane == 16 + h, inter[h], gathered)
    turned = jnp.transpose(gathered)
    direct, tail_row, inter_row = turned[0:8], turned[8:16], turned[16:24]
    pad = [jnp.zeros((1, size), f32)] * (8 - heads)
    row_sum = jnp.concatenate(row_sums + pad, axis=0)
    zero = jnp.zeros((1, 1), f32)
    end_col = jnp.concatenate(ends + [zero] * (8 - heads), axis=0)
    d_logs = row_sum + inter_row - dt * direct
    at_last = end_col + jnp.sum(dt * tail_row, axis=1, keepdims=True)
    lower = (iota((size, size), 0) >= iota((size, size), 1)).astype(f32)
    d_rate = dot_exact(d_logs, lower) + at_last
    d_dt = direct + rate * d_rate
    d_raw = d_dt * jax.nn.sigmoid(raw)
    spread_rows = jnp.concatenate([d_raw, jnp.zeros((120, size), f32)], axis=0)
    g_pxs[:, u.shape[1] :] = jnp.transpose(spread_rows).astype(bf16)
    g_vec[0:8] += d_raw
    g_vec[8:16] += rate * dt * d_rate
    g_skip[...] += jnp.sum((dy * u).reshape(size // 8, 8, u.shape[1]), axis=0)
    d_pre = du * (sig_u * (1.0 + pre_u * (1.0 - sig_u)))
    g_pxs[:, : u.shape[1]] = conv_rows_back(d_pre, next_px[...], taps[...]).astype(bf16)
    g_taps[...] += conv_taps_back(tail_x, block_x, d_pre)
    next_px[...] = d_pre[:8]
    d_bc = jnp.concatenate([db, dc], axis=1) * (sig_bc * (1.0 + pre_bc * (1.0 - sig_bc)))
    g_pbc[...] = conv_rows_back(d_bc, next_bc[...], shared_taps[...]).astype(bf16)
    g_shared[...] += conv_taps_back(tail_bc, block_bc, d_bc)
    next_bc[...] = d_bc[:8]


def pad_rows(value):
    return jnp.pad(value, ((0, -value.shape[0] % 8), (0, 0)))


def vec_of(step_bias, decay_log, skip_gain):
    table = jnp.stack([step_bias, decay_log, skip_gain], axis=1)
    return jnp.pad(table, ((0, 8 - table.shape[0]), (0, 128 - table.shape[1])))


def whole(shape):
    return pl.BlockSpec(shape, lambda i, r: tuple(0 for _ in shape))


def cost(flops, moved, exps):
    return pl.CostEstimate(flops=flops, bytes_accessed=moved, transcendentals=exps)


def chunk_specs(length, ranks, order):
    per_block = length // ranks // CHUNK
    per = CHUNK // 8

    def place(i, r):
        c = order(i)
        return ((c // per_block) ^ r[0]) * per_block + c % per_block

    def at(cols):
        return pl.BlockSpec((CHUNK, cols), lambda i, r: (place(i, r), 0))

    def tail(cols):
        def index(i, r):
            c = jnp.maximum(order(i) - 1, 0)
            return ((((c // per_block) ^ r[0]) * per_block + c % per_block) * per + per - 1, 0)

        return pl.BlockSpec((8, cols), index)

    row = pl.BlockSpec((8, CHUNK), lambda i, r: (0, place(i, r)))
    return at, tail, row


def mamba_fwd(rank, px, pz, pbc, pdt, taps, shared_taps, vec, heads, ranks):
    length, chans = px.shape
    wide = pbc.shape[1]
    steps = length // CHUNK
    at, tail, row = chunk_specs(length, ranks, lambda i: i)
    return pl.pallas_call(
        functools.partial(mamba_fwd_kernel, heads),
        grid_spec=pltpu.PrefetchScalarGridSpec(
            num_scalar_prefetch=1,
            grid=(steps,),
            in_specs=[
                at(chans),
                tail(chans),
                at(chans),
                at(wide),
                tail(wide),
                row,
                whole((8, chans)),
                whole((8, wide)),
                whole((8, 128)),
            ],
            out_specs=[
                at(chans),
                at(chans),
                pl.BlockSpec((1, wide // 2, chans), lambda i, r: (i, 0, 0)),
            ],
            scratch_shapes=[pltpu.VMEM((wide // 2, chans), f32)],
        ),
        out_shape=[
            jax.ShapeDtypeStruct((length, chans), bf16),
            jax.ShapeDtypeStruct((length, chans), bf16),
            jax.ShapeDtypeStruct((steps, wide // 2, chans), f32),
        ],
        cost_estimate=cost(4 * 10**9, 8 * 10**6, 10**6),
        name="mamba_forward",
    )(rank, px, px, pz, pbc, pbc, pdt, taps, shared_taps, vec)


def mamba_bwd(rank, px, pz, pbc, pdt, taps, shared_taps, vec, states, gym, heads, ranks):
    length, chans = px.shape
    wide = pbc.shape[1]
    steps = length // CHUNK
    at, tail, row = chunk_specs(length, ranks, lambda i: steps - 1 - i)
    return pl.pallas_call(
        functools.partial(mamba_bwd_kernel, heads),
        grid_spec=pltpu.PrefetchScalarGridSpec(
            num_scalar_prefetch=1,
            grid=(steps,),
            in_specs=[
                at(chans),
                tail(chans),
                at(chans),
                at(wide),
                tail(wide),
                row,
                whole((8, chans)),
                whole((8, wide)),
                whole((8, 128)),
                pl.BlockSpec((1, wide // 2, chans), lambda i, r: (steps - 1 - i, 0, 0)),
                at(chans),
            ],
            out_specs=[
                at(chans + 128),
                at(wide),
                whole((8, chans)),
                whole((8, wide)),
                whole((16, 128)),
                whole((8, chans)),
            ],
            scratch_shapes=[
                pltpu.VMEM((wide // 2, chans), f32),
                pltpu.VMEM((8, chans), f32),
                pltpu.VMEM((8, wide), f32),
            ],
        ),
        out_shape=[
            jax.ShapeDtypeStruct((length, chans + 128), bf16),
            jax.ShapeDtypeStruct((length, wide), bf16),
            jax.ShapeDtypeStruct((8, chans), f32),
            jax.ShapeDtypeStruct((8, wide), f32),
            jax.ShapeDtypeStruct((16, 128), f32),
            jax.ShapeDtypeStruct((8, chans), f32),
        ],
        cost_estimate=cost(9 * 10**9, 10**7, 10**6),
        name="mamba_backward",
    )(rank, px, px, pz, pbc, pbc, pdt, taps, shared_taps, vec, states, gym)


ROWS = 256


def turn(pre, cosine, sine):
    inner = iota(pre.shape, 1) % HEAD < HEAD // 2
    lanes = pre.shape[1]
    other = jnp.where(
        inner, pltpu.roll(pre, lanes - HEAD // 2, 1), pltpu.roll(pre, HEAD // 2, 1)
    )
    return pre * cosine + other * sine


def attend_fwd_kernel(scale, rank, qkv, cosine, sine, out, q, k, v):
    length, wide = out.shape
    blocks = length // ROWS
    low = iota((ROWS, 2 * HEAD), 1) < HEAD
    load_qkv(rank, qkv, cosine, sine, q, k, v)
    for i in range(blocks):
        seen = (i + 1) * ROWS
        block = q[i * ROWS : (i + 1) * ROWS]
        keys, values = k[:seen], v[:seen]
        allowed = iota((ROWS, seen), 1) <= iota((ROWS, seen), 0) + i * ROWS
        outs = []
        for h in range(2):
            keep = low if h == 0 else jnp.logical_not(low)
            part = jnp.where(keep, block, jnp.zeros_like(block))
            scores = jnp.where(allowed, dot_nt(part, keys) * scale, -1e30)
            expo = jnp.exp(scores - jnp.max(scores, axis=1, keepdims=True))
            chance = expo * (1.0 / jnp.sum(expo, axis=1, keepdims=True))
            outs.append(dot_nn(chance.astype(bf16), values))
        out[relative_rows(rank, i)] = jnp.where(low, outs[0], outs[1]).astype(bf16)


def relative_rows(rank, i):
    return pl.ds(pl.multiple_of((i ^ rank[0]) * ROWS, ROWS), ROWS)


def load_qkv(rank, qkv, cosine, sine, q, k, v):
    wide = q.shape[1]
    for i in range(q.shape[0] // ROWS):
        rows = slice(i * ROWS, (i + 1) * ROWS)
        piece = qkv[relative_rows(rank, i)]
        q[rows] = turn(piece[:, :wide], cosine[rows], sine[rows]).astype(bf16)
        k[rows] = turn(piece[:, wide : 2 * wide], cosine[rows], sine[rows]).astype(bf16)
        v[rows] = piece[:, 2 * wide :].astype(bf16)


def attend_bwd_kernel(scale, rank, qkv, cosine, sine, go, g_qkv, q, k, v, dk, dv):
    length, wide = dk.shape
    blocks = length // ROWS
    low = iota((ROWS, 2 * HEAD), 1) < HEAD
    load_qkv(rank, qkv, cosine, sine, q, k, v)
    dk[...] = jnp.zeros_like(dk)
    dv[...] = jnp.zeros_like(dv)
    for i in range(blocks):
        seen = (i + 1) * ROWS
        rows = slice(i * ROWS, (i + 1) * ROWS)
        block, grads = q[rows], go[relative_rows(rank, i)]
        keys, values = k[:seen], v[:seen]
        allowed = iota((seen, ROWS), 0) <= iota((seen, ROWS), 1) + i * ROWS
        dqs, dks, dvs = [], [], []
        for h in range(2):
            keep = low if h == 0 else jnp.logical_not(low)
            part = jnp.where(keep, block, jnp.zeros_like(block))
            part_g = jnp.where(keep, grads, jnp.zeros_like(grads))
            scores = jnp.where(allowed, dot_nt(keys, part) * scale, -1e30)
            expo = jnp.exp(scores - jnp.max(scores, axis=0, keepdims=True))
            chance = expo * (1.0 / jnp.sum(expo, axis=0, keepdims=True))
            g_chance = dot_nt(values, part_g)
            center = jnp.sum(chance * g_chance, axis=0, keepdims=True)
            g_scores = (chance * (g_chance - center)).astype(bf16)
            dqs.append(dot_tn(g_scores, keys))
            dks.append(dot_nn(g_scores, part))
            dvs.append(dot_nn(chance.astype(bf16), part_g))
        dq = jnp.where(low, dqs[0], dqs[1]) * scale
        g_qkv[relative_rows(rank, i), :wide] = turn(dq, cosine[rows], -sine[rows]).astype(bf16)
        dk[:seen] += (dks[0] + dks[1]) * scale
        dv[:seen] += dvs[0] + dvs[1]
    for i in range(blocks):
        rows = slice(i * ROWS, (i + 1) * ROWS)
        g_k, g_v = dk[rows], dv[rows]
        g_k = turn(g_k + pltpu.roll(g_k, HEAD, 1), cosine[rows], -sine[rows])
        g_v = g_v + pltpu.roll(g_v, HEAD, 1)
        g_qkv[relative_rows(rank, i), wide:] = jnp.where(low, g_k, g_v).astype(bf16)


def attend_specs(length, wide):
    return [
        whole((length, 3 * wide)),
        whole((length, wide)),
        whole((length, wide)),
    ], [pltpu.VMEM((length, wide), bf16)] * 3


def attend_fwd(rank, qkv, cosine, sine):
    length, wide = cosine.shape
    ins, scratch = attend_specs(length, wide)
    return pl.pallas_call(
        functools.partial(attend_fwd_kernel, HEAD**-0.5),
        grid_spec=pltpu.PrefetchScalarGridSpec(
            num_scalar_prefetch=1,
            grid=(1,),
            in_specs=ins,
            out_specs=whole((length, wide)),
            scratch_shapes=scratch,
        ),
        out_shape=jax.ShapeDtypeStruct((length, wide), bf16),
        cost_estimate=cost(2 * 10**9, 4 * 10**6, 10**6),
        name="attend_forward",
    )(rank, qkv, cosine, sine)


def attend_bwd(rank, qkv, cosine, sine, g_oa):
    length, wide = cosine.shape
    ins, scratch = attend_specs(length, wide)
    return pl.pallas_call(
        functools.partial(attend_bwd_kernel, HEAD**-0.5),
        grid_spec=pltpu.PrefetchScalarGridSpec(
            num_scalar_prefetch=1,
            grid=(1,),
            in_specs=ins + [whole((length, wide))],
            out_specs=whole((length, 2 * wide)),
            scratch_shapes=scratch + [pltpu.VMEM((length, wide), f32)] * 2,
        ),
        out_shape=jax.ShapeDtypeStruct((length, 2 * wide), bf16),
        cost_estimate=cost(4 * 10**9, 6 * 10**6, 10**6),
        name="attend_backward",
    )(rank, qkv, cosine, sine, g_oa)


def first_norm_kernel(order, me, x0, x1, x2, x3, gain, a1, kept):
    rows, width = x0.shape
    block = width // len(order)
    step = 32
    for at, source in enumerate((x0, x1, x2, x3)):

        def lines(i, carry, at=at, source=source):
            own = pl.ds(pl.multiple_of(i * step, step), step)
            out = pl.ds(pl.multiple_of(at * rows + i * step, step), step)
            value = source[own].astype(f32)
            rho = lax.rsqrt(jnp.mean(value * value, axis=1, keepdims=True) + epsilon)
            for p, k in enumerate(order):
                there = pl.ds(pl.multiple_of((me[0] ^ k) * block, block), block)
                here = slice(p * block, (p + 1) * block)
                piece = source[own, there]
                a1[out, here] = (piece.astype(f32) * rho * gain[:, here]).astype(bf16)
                if at % 2 == 0:
                    kept[pl.ds(pl.multiple_of(at // 2 * rows + i * step, step), step), here] = piece
            return carry

        lax.fori_loop(0, rows // step, lines, 0)


def first_norm(pieces, gain, member, size):
    rows, width = pieces[0].shape
    if width // size % 128 == 0:
        return pl.pallas_call(
            functools.partial(first_norm_kernel, relative_order(size)),
            grid_spec=pltpu.PrefetchScalarGridSpec(
                num_scalar_prefetch=1,
                grid=(1,),
                in_specs=[whole((rows, width))] * 4 + [whole((1, width))],
                out_specs=[whole((4 * rows, width)), whole((2 * rows, width))],
            ),
            out_shape=[
                jax.ShapeDtypeStruct((4 * rows, width), bf16),
                jax.ShapeDtypeStruct((2 * rows, width), bf16),
            ],
            cost_estimate=cost(10**7, 10 * rows * width * 2, 4 * rows),
            name="first_norm",
        )(member.reshape(1), *pieces, gain.reshape(1, -1))
    moved = [take_blocks(piece, member, size, False) for piece in pieces]
    normed = []
    for piece in moved:
        value = piece.astype(f32)
        rho = lax.rsqrt(jnp.mean(value * value, axis=-1, keepdims=True) + epsilon)
        normed.append((value * rho * gain).astype(bf16))
    return jnp.concatenate(normed, axis=0), jnp.concatenate([moved[0], moved[2]], axis=0)


def rotary_tables(length):
    half = HEAD // 2
    frequency = rotary_base ** (-2.0 * jnp.arange(half, dtype=f32) / HEAD)
    angles = jnp.arange(length, dtype=f32)[:, None] * frequency[None, :]
    cosine, sine = jnp.cos(angles), jnp.sin(angles)
    return (
        jnp.concatenate([cosine] * 4, axis=1),
        jnp.concatenate([-sine, sine, -sine, sine], axis=1),
    )


def swiglu(gate_part, up_part):
    return jax.nn.silu(gate_part) * up_part


def mm(a, b):
    return jnp.dot(a, b, preferred_element_type=f32)


def mm_t(a, b):
    return lax.dot_general(a, b, (((1,), (1,)), ((), ())), preferred_element_type=f32)


def t_mm(a, b):
    return lax.dot_general(a, b, (((0,), (0,)), ((), ())), preferred_element_type=f32)


def body(
    layer_in,
    out_grad,
    lengths,
    mamba_x,
    mamba_z,
    mamba_step,
    query_proj,
    key_proj,
    value_proj,
    mamba_out,
    attend_out,
    mlp_gate,
    mlp_up,
    mlp_down,
    state_proj,
    conv_state,
    norm_gains,
    conv_mamba,
    step_bias,
    decay_log,
    skip_gain,
):
    ranks = lax.axis_size("tensor")
    assert ranks == 4 and layer_in.shape[1] == 1
    rank = lax.axis_index("tensor")
    y, core = rank // 2, rank % 2
    rank_ref = rank.reshape(1)
    peers = lax.axis_size("dp")
    me = lax.axis_index("dp")
    rows, _, width = layer_in.shape
    length = rows * ranks
    chans = mamba_x.shape[1]
    heads = step_bias.shape[0]
    q_cols, k_cols = query_proj.shape[1], key_proj.shape[1]
    ff = mlp_gate.shape[1]
    own_rows, n2 = state_proj.shape

    raw_0 = layer_in[:, 0]
    raw_2 = flip_y(raw_0)
    raw_1, raw_3 = flip_core(raw_0), flip_core(raw_2)

    small = jnp.concatenate([conv_state.reshape(-1), norm_gains.reshape(-1)])
    parts = []
    rest = small
    for _ in range(3):
        parts.append(lax.reduce_precision(rest, 8, 7))
        rest = rest - parts[-1]
    parts = jnp.concatenate(parts)
    small_rows = -(-parts.shape[0] // n2)
    parts = jnp.pad(parts, (0, small_rows * n2 - parts.shape[0])).reshape(small_rows, n2)
    pack_s = jnp.concatenate([state_proj, parts], axis=0).astype(bf16)
    all_s = gather_pieces(pack_s[None], "dp")
    all_s = jnp.swapaxes(in_rank_order(all_s, y, core), 0, 1)
    w_bc = all_s[:, :, :own_rows].reshape(width, n2)
    parts = all_s[:, :, own_rows:].reshape(peers, ranks, -1).astype(f32)
    count = small.shape[0]
    small = parts[..., :count] + parts[..., count : 2 * count] + parts[..., 2 * count : 3 * count]
    cut = conv_state.size
    taps_own = conv_state.shape[1]
    gains_own = norm_gains.shape[1]
    taps_rel = small[..., :cut].reshape(peers, ranks, conv_state.shape[0], taps_own)
    taps_rel = jnp.transpose(taps_rel, (2, 0, 1, 3)).reshape(conv_state.shape[0], -1)
    conv_shared = take_blocks(taps_rel, me, peers, True)
    gain_pair = jnp.transpose(
        small[..., cut:].reshape(peers, ranks, 2, gains_own), (2, 0, 1, 3)
    ).reshape(2, width)

    pack_q = jnp.concatenate(
        [item.astype(bf16) for item in (query_proj, key_proj, value_proj)], axis=1
    )
    w_qkv = gather_pieces(pack_q, "dp")
    step_low = jnp.pad(mamba_step.astype(bf16), ((0, 0), (0, 128 - heads)))
    pack_a = jnp.concatenate([mamba_x.astype(bf16), step_low, mamba_z.astype(bf16)], axis=1)
    w_a = gather_pieces(pack_a, "dp", True)
    pack_o = jnp.concatenate([mamba_out.T.astype(bf16), attend_out.T.astype(bf16)], axis=1)
    pack_m = jnp.concatenate(
        [mlp_gate.astype(bf16), mlp_up.astype(bf16), mlp_down.T.astype(bf16)], axis=1
    )

    def rho_of(values):
        return lax.rsqrt(jnp.mean(values * values, axis=-1, keepdims=True) + epsilon)

    a1, x02 = first_norm((raw_0, raw_1, raw_2, raw_3), gain_pair[0], me, peers)
    x0, x2 = x02[:rows], x02[rows:]

    w_k, w_v = w_qkv[:, q_cols : q_cols + k_cols], w_qkv[:, q_cols + k_cols :]
    w_att = jnp.concatenate([w_qkv[:, :q_cols], w_k, w_k, w_v, w_v], axis=1)
    qkv = mm(a1, w_att)
    cosine, sine = rotary_tables(length)
    oa = attend_fwd(rank_ref, qkv, cosine, sine)

    pack_o, go_raw = lax.optimization_barrier((pack_o, out_grad, a1))[:2]
    w_o = gather_pieces(pack_o, "dp")
    limit = lengths[0]

    def masked(block, k):
        place = (rank ^ k) * rows + jnp.arange(rows, dtype=jnp.int32)
        return jnp.where((place < limit)[:, None], block, jnp.zeros_like(block))

    gf0 = masked(move_blocks(go_raw[:, 0], me, peers, False), 0)
    gf2 = flip_y(gf0)
    gf1, gf3 = flip_core(gf0), flip_core(gf2)
    gf_a = jnp.concatenate([gf0, gf1], axis=0)
    gf_b = jnp.concatenate([gf2, gf3], axis=0)

    w_x, w_dt = w_a[:, :chans], w_a[:, chans : chans + 8]
    w_z = w_a[:, chans + 128 :]
    px, pz, pbc = mm(a1, w_x), mm(a1, w_z), mm(a1, w_bc)
    pdt = lax.dot_general(w_dt, a1, (((0,), (1,)), ((), ())), preferred_element_type=f32)
    pack_m = after(pack_m, px)
    w_m = gather_pieces(pack_m, "dp", True)
    w_gu, w_dn = w_m[:, : 2 * ff], w_m[:, 2 * ff :]
    vec = vec_of(step_bias, decay_log, skip_gain)
    taps, shared_taps = pad_rows(conv_mamba), pad_rows(conv_shared)
    om, kept, states = mamba_fwd(
        rank_ref, px, pz, pbc, pdt, taps, shared_taps, vec, heads, ranks
    )

    def mixer_term(k):
        lines = slice(k * rows, (k + 1) * rows)
        return mm_t(om[lines], w_o[:, :chans]) + mm_t(oa[lines], w_o[:, chans:])

    s2 = core_sum(mixer_term(2), mixer_term(3))
    s0 = core_sum(mixer_term(0), mixer_term(1))

    def second_norm(low_x, m):
        r1 = low_x.astype(f32) + m
        rho = rho_of(r1)
        return r1, rho, (r1 * rho * gain_pair[1]).astype(bf16)

    r1_0, rho_0, a2_0 = second_norm(x0, y_sum(s0, s2))
    a2_a = jnp.concatenate([a2_0, flip_core(a2_0)], axis=0)
    r1_2, rho_2, a2_2 = second_norm(x2, y_sum(s2, s0))
    a2_b = jnp.concatenate([a2_2, flip_core(a2_2)], axis=0)

    def feed(a2, gf):
        gate_up = mm(a2, w_gu)
        gate, up = gate_up[:, :ff], gate_up[:, ff:]
        hidden, glu_back = jax.vjp(swiglu, gate, up)
        hid = hidden.astype(bf16)
        gate_grad, up_grad = glu_back(mm(gf, w_dn))
        g_gu = jnp.concatenate([gate_grad.astype(bf16), up_grad.astype(bf16)], axis=1)
        return hid, g_gu, mm_t(g_gu, w_gu)

    hid_a, g_gu_a, g_a2_a = feed(a2_a, gf_a)
    t0 = core_sum(g_a2_a[:rows], g_a2_a[rows:])
    hid_b, g_gu_b, g_a2_b = feed(a2_b, gf_b)
    t2 = core_sum(g_a2_b[:rows], g_a2_b[rows:])

    def second_back(g_a2, r1, rho, gf):
        n_two = r1 * rho
        e_two = g_a2 * gain_pair[1]
        inner = jnp.mean(e_two * n_two, axis=-1, keepdims=True)
        return gf.astype(f32) + rho * (e_two - n_two * inner)

    g_r1_2 = second_back(y_sum(t2, t0), r1_2, rho_2, gf2)
    g_m_2 = g_r1_2.astype(bf16)
    g_a2_0 = y_sum(t0, t2)
    g_r1_0 = second_back(g_a2_0, r1_0, rho_0, gf0)
    g_m_0 = g_r1_0.astype(bf16)
    gain_two_grad = jnp.sum(g_a2_0 * (r1_0 * rho_0), axis=0)
    g_m_3, g_m_1 = flip_core(g_m_2), flip_core(g_m_0)
    g_m = jnp.concatenate([g_m_0, g_m_1, g_m_2, g_m_3], axis=0)
    g_ym = mm(g_m, w_o[:, :chans])
    g_oa = mm(g_m, w_o[:, chans:]).astype(bf16)

    dn_kept, dn_sent = sum_of_products([(gf_a, hid_a), (gf_b, hid_b)], "dp")
    dn_sum = scatter_sum(dn_kept, dn_sent, "dp")
    gu_kept, gu_sent = sum_of_products([(a2_a, g_gu_a), (a2_b, g_gu_b)], "dp")
    gu_sum = scatter_sum(gu_kept, gu_sent, "dp")

    hid_a, hid_b = lax.optimization_barrier((hid_a, hid_b, g_m))[:2]
    f_a, f_b = mm_t(hid_a, w_dn), mm_t(hid_b, w_dn)
    f_sent = jnp.concatenate([f_a[rows:], f_b[rows:]], axis=0)
    f02 = core_sum(jnp.concatenate([f_a[:rows], f_b[:rows]], axis=0), f_sent)
    layer_out = masked(r1_0 + y_sum(f02[:rows], f02[rows:]), 0).astype(bf16)
    layer_out = move_blocks(layer_out, me, peers, True)[:, None]

    mixed_in = jnp.concatenate([om, oa], axis=1)
    out_kept, out_sent = sum_of_products([(g_m, mixed_in)], "dp")
    out_sum = scatter_sum(out_kept, out_sent, "dp")

    g_qkv = attend_bwd(rank_ref, qkv, cosine, sine, g_oa)
    sig_z = jax.nn.sigmoid(pz)
    g_pz = g_ym * kept.astype(f32) * (sig_z * (1.0 + pz * (1.0 - sig_z)))
    g_pz = g_pz.astype(bf16)
    z_kept, z_sent = sum_of_products([(a1, jnp.concatenate([g_pz, g_qkv], axis=1))], "dp")
    z_sum = scatter_sum(z_kept, z_sent, "dp")

    g_ym = after(g_ym, z_sent)
    g_pxs, g_bc, g_taps, g_shared, g_vec, g_skip = mamba_bwd(
        rank_ref, px, pz, pbc, pdt, taps, shared_taps, vec, states, g_ym, heads, ranks
    )
    x_kept, x_sent = sum_of_products([(a1, g_pxs)], "dp")
    x_sum = scatter_sum(x_kept, x_sent, "dp")
    state_part = t_mm(a1, g_bc).reshape(peers, 2, 2, own_rows, n2)
    by_core = pick(core, state_part[:, :, ::-1], state_part)
    half_sum = by_core[:, :, 0] + flip_core(by_core[:, :, 1].astype(bf16)).astype(f32)
    by_y = pick(y, half_sum[:, ::-1], half_sum)
    state_sum = by_y[:, 0] + flip_y(by_y[:, 1].astype(bf16)).astype(f32)
    state_sum = state_sum.reshape(peers * own_rows, n2)
    half = state_sum.shape[0] // 2
    state_proj_grad = scatter_sum(state_sum[:half], state_sum[half:].astype(bf16), "dp")

    g_a1 = mm_t(g_pz, w_z) + mm_t(g_qkv, w_qkv) + mm_t(g_pxs, w_a[:, : chans + 128])
    g_a1 = g_a1 + mm_t(g_bc, w_bc)
    gain_one_grad = jnp.sum(g_a1 * a1.astype(f32), axis=0) / gain_pair[0]
    g_sent = jnp.concatenate([g_a1[rows : 2 * rows], g_a1[3 * rows :]], axis=0)
    u02 = core_sum(jnp.concatenate([g_a1[:rows], g_a1[2 * rows : 3 * rows]], axis=0), g_sent)
    e_one = y_sum(u02[:rows], u02[rows:]) * gain_pair[0]
    x_own = x0.astype(f32)
    rho_own = rho_of(x_own)
    n_own = x_own * rho_own
    inner = jnp.mean(e_one * n_own, axis=-1, keepdims=True)
    in_grad = g_r1_0 + rho_own * (e_one - n_own * inner)
    in_grad = move_blocks(in_grad.astype(bf16), me, peers, True)[:, None]

    conv_taps_grad = g_taps[: conv_mamba.shape[0]]
    conv_shared_grad = g_shared[: conv_state.shape[0]]
    bias_grad = jnp.sum(g_vec[:heads], axis=1)
    decay_grad = jnp.sum(g_vec[8 : 8 + heads], axis=1)
    skip_grad = jnp.sum(g_skip.reshape(8, heads, HEAD), axis=(0, 2))
    gain_grads = take_blocks(jnp.stack([gain_one_grad, gain_two_grad]), me, peers, True)
    both = jnp.concatenate([conv_shared_grad.reshape(-1), gain_grads.reshape(-1)])
    both_rows = -(-both.shape[0] // 128)
    both = jnp.pad(both, (0, both_rows * 128 - both.shape[0]))
    only = jnp.concatenate([conv_taps_grad.reshape(-1), bias_grad, decay_grad, skip_grad])
    only = jnp.pad(only, (0, -only.shape[0] % 128))
    packed = jnp.concatenate([both, only]).reshape(-1, 128)
    for bit in range(bits_of(peers)):
        packed = packed + flip(packed, "dp", 1 << bit)
    both = packed[:both_rows]
    for mask in (1, 2):
        both = both + flip(both, "tensor", mask)
    both = both.reshape(-1)
    only = packed[both_rows:].reshape(-1)
    conv_state_sum = both[: conv_state.size * peers * ranks].reshape(conv_shared.shape)
    gain_sum = both[conv_shared.size : conv_shared.size + 2 * width].reshape(2, width)
    member = me * ranks + rank
    conv_state_grad = lax.dynamic_slice_in_dim(conv_state_sum, member * taps_own, taps_own, 1)
    norm_gains_grad = lax.dynamic_slice_in_dim(gain_sum, member * gains_own, gains_own, 1)
    cut = conv_taps_grad.size
    conv_mamba_grad = only[:cut].reshape(conv_taps_grad.shape)
    step_bias_grad = only[cut : cut + heads]
    decay_log_grad = only[cut + heads : cut + 2 * heads]
    skip_gain_grad = only[cut + 2 * heads : cut + 3 * heads]

    return (
        layer_out,
        in_grad,
        x_sum[:, :chans],
        z_sum[:, :chans],
        x_sum[:, chans : chans + heads],
        z_sum[:, chans : chans + q_cols],
        z_sum[:, chans + q_cols : chans + q_cols + k_cols],
        z_sum[:, chans + q_cols + k_cols :],
        out_sum[:, :chans].T,
        out_sum[:, chans:].T,
        gu_sum[:, :ff],
        gu_sum[:, ff:],
        dn_sum.T,
        state_proj_grad,
        conv_state_grad,
        norm_gains_grad,
        conv_mamba_grad,
        step_bias_grad,
        decay_log_grad,
        skip_gain_grad,
    )


def solution(mesh):
    in_specs = (
        P("tensor", "dp", None),
        P("tensor", "dp", None),
        P("dp"),
        P("dp", "tensor"),
        P("dp", "tensor"),
        P("dp", "tensor"),
        P("dp", "tensor"),
        P("dp", "tensor"),
        P("dp", "tensor"),
        P("tensor", "dp"),
        P("tensor", "dp"),
        P("dp", "tensor"),
        P("dp", "tensor"),
        P("tensor", "dp"),
        P(("dp", "tensor"), None),
        P(None, ("dp", "tensor")),
        P(None, ("dp", "tensor")),
        P(None, "tensor"),
        P("tensor"),
        P("tensor"),
        P("tensor"),
    )
    out_specs = (
        P("tensor", "dp", None),
        P("tensor", "dp", None),
        P("dp", "tensor"),
        P("dp", "tensor"),
        P("dp", "tensor"),
        P("dp", "tensor"),
        P("dp", "tensor"),
        P("dp", "tensor"),
        P("tensor", "dp"),
        P("tensor", "dp"),
        P("dp", "tensor"),
        P("dp", "tensor"),
        P("tensor", "dp"),
        P(("dp", "tensor"), None),
        P(None, ("dp", "tensor")),
        P(None, ("dp", "tensor")),
        P(None, "tensor"),
        P("tensor"),
        P("tensor"),
        P("tensor"),
    )
    return jax.shard_map(body, mesh=mesh, in_specs=in_specs, out_specs=out_specs, check_vma=False)
```

```python
import functools

import jax
import jax.numpy as jnp
from jax import lax
from jax.experimental import pallas as pl
from jax.experimental.pallas import tpu as pltpu
from jax.sharding import PartitionSpec as P

epsilon = 1e-05
rotary_base = 100000000000.0
HIGHEST = lax.Precision.HIGHEST
bf16 = jnp.bfloat16
f32 = jnp.float32


def flip(value, axis, mask):
    size = lax.axis_size(axis)
    return lax.ppermute(value, axis, [(i, i ^ mask) for i in range(size)])


def bits_of(size):
    bits = size.bit_length() - 1
    assert size == 1 << bits
    return bits


def relative_order(size):
    order = [0]
    for bit in reversed(range(bits_of(size))):
        order = order + [k | (1 << bit) for k in order]
    return order


def gather_pieces(own, axis, swap=False):
    bits = bits_of(lax.axis_size(axis))
    assert bits >= 2
    held = own
    for bit in reversed(range(2, bits)):
        held = jnp.concatenate([held, flip(held, axis, 1 << bit)], axis=0)
    return gather_last(held, axis, swap)


def gather_last(held, axis, swap):
    count = held.shape[0]
    other = flip(held, axis, 1 if swap else 2)
    far = flip(jnp.concatenate([held, other], axis=0), axis, 2 if swap else 1)
    return join_quarters(held, other, far, count, swap)


def join_quarters(held, other, far, count, swap):
    if swap:
        return jnp.concatenate([held, far[:count], other, far[count:]], axis=0)
    return jnp.concatenate([held, other, far], axis=0)


class Gather:
    def __init__(self, own, axis, swap):
        self.axis, self.swap = axis, swap
        order = list(reversed(range(bits_of(lax.axis_size(axis)))))
        if swap:
            order[-2:] = [0, 1]
        self.order, self.held, self.other = order, own, None
        self.got = flip(own, axis, 1 << order[0])

    def advance(self, *others):
        got = after(self.got, *others) if others else self.got
        left = len(self.order)
        self.order = self.order[1:]
        if left == 1:
            return join_quarters(self.held, self.other, got, self.held.shape[0], self.swap)
        both = jnp.concatenate([self.held, got], axis=0)
        if left == 2:
            self.other = got
        else:
            self.held = both
        self.got = flip(both, self.axis, 1 << self.order[0])
        return both

    def until(self, left, *others):
        while len(self.order) > left:
            both = self.advance(*others)
        return both


class Sum:
    def __init__(self, kept, sent, axis, swap):
        order = list(range(bits_of(lax.axis_size(axis))))
        if swap:
            order[:2] = [1, 0]
        self.order, self.kept, self.axis = order, kept, axis
        self.got = flip(sent, axis, 1 << order[0])

    def advance(self, *others):
        got = after(self.got, *others) if others else self.got
        total = self.kept + got.astype(f32)
        self.order = self.order[1:]
        if not self.order:
            return total
        half = total.shape[0] // 2
        self.kept, sent = total[:half], total[half:].astype(bf16)
        self.got = flip(sent, self.axis, 1 << self.order[0])
        return sent

    def finish(self, *others):
        while self.order:
            total = self.advance(*others)
        return total


def product_kernel(pairs, widths, rank, *refs):
    kept, sent = refs[-2:]
    step = pl.program_id(0)
    per = 1 + len(widths)
    at = 0
    for j, width in enumerate(widths):
        total = 0.0
        for p in range(pairs):
            total = total + dot_tn(refs[p * per][...], refs[p * per + 1 + j][...])
        cols = slice(at, at + width)
        at += width

        @pl.when(step < 2)
        def _():
            sent[:, cols] = total.astype(bf16)

        @pl.when(step >= 2)
        def _():
            kept[:, cols] = total


def product(token, pairs, swap):
    width = pairs[0][0].shape[1]
    length = sum(left.shape[0] for left, _ in pairs)
    quarter = width // 4
    widths = [array.shape[1] for array, _ in pairs[0][1]]
    total = sum(widths)

    def place(i):
        return (2 * i + 1) % 5 if swap else (i + 2) % 4

    specs, operands = [], []
    for left, rights in pairs:
        lines = left.shape[0]
        specs.append(pl.BlockSpec((lines, quarter), lambda i, r: (0, place(i))))
        operands.append(left)
        for array, block in rights:
            specs.append(
                pl.BlockSpec((lines, array.shape[1]), lambda i, r, block=block: (block, 0))
            )
            operands.append(array)
    return pl.pallas_call(
        functools.partial(product_kernel, len(pairs), widths),
        grid_spec=pltpu.PrefetchScalarGridSpec(
            num_scalar_prefetch=1,
            grid=(4,),
            in_specs=specs,
            out_specs=[
                pl.BlockSpec((quarter, total), lambda i, r: (jnp.maximum(i - 2, 0), 0)),
                pl.BlockSpec((quarter, total), lambda i, r: (jnp.minimum(i, 1), 0)),
            ],
        ),
        out_shape=[
            jax.ShapeDtypeStruct((2 * quarter, total), f32),
            jax.ShapeDtypeStruct((2 * quarter, total), bf16),
        ],
        cost_estimate=cost(2 * length * width * total, 8 * width * total, 0),
        name="weight_product",
    )(token, *operands)


def move_kernel(back, order, me, source, target):
    width = source.shape[1] // len(order)
    for p, k in enumerate(order):
        there = pl.ds(pl.multiple_of((me[0] ^ k) * width, width), width)
        here = slice(p * width, (p + 1) * width)
        if back:
            target[:, there] = source[:, here]
        else:
            target[:, here] = source[:, there]


def move_blocks(value, member, size, back):
    width = value.shape[1] // size
    if width % 128 == 0:
        return pl.pallas_call(
            functools.partial(move_kernel, back, relative_order(size)),
            grid_spec=pltpu.PrefetchScalarGridSpec(
                num_scalar_prefetch=1,
                grid=(1,),
                in_specs=[whole(value.shape)],
                out_specs=whole(value.shape),
            ),
            out_shape=jax.ShapeDtypeStruct(value.shape, value.dtype),
            cost_estimate=cost(0, 2 * value.size * value.dtype.itemsize, 0),
            name="move_blocks",
        )(member.reshape(1), value)
    return take_blocks(value, member, size, back)


def take_blocks(value, member, size, back):
    order = relative_order(size)
    where = [0] * size
    for p, k in enumerate(order):
        where[k] = p
    if back:
        index = jnp.array(where, jnp.int32)[member ^ jnp.arange(size, dtype=jnp.int32)]
    else:
        index = member ^ jnp.array(order, jnp.int32)
    cut = value.reshape(value.shape[0], size, -1)
    return jnp.take(cut, index, axis=1).reshape(value.shape)


def pick(bit, one, zero):
    return jnp.where(bit == 1, one, zero)


def after(value, *others):
    return lax.optimization_barrier((value,) + others)[0]


def flip_core(value):
    return flip(value, "tensor", 1)


def flip_y(value):
    return flip(value, "tensor", 2)


def in_rank_order(own, y, core):
    other = flip_y(own)
    pair = jnp.stack([pick(y, other, own), pick(y, own, other)])
    other = flip_core(pair)
    both = jnp.stack([pick(core, other, pair), pick(core, pair, other)], axis=1)
    return both.reshape((4,) + own.shape)


def core_sum(kept, sent):
    return (kept + flip_core(sent.astype(bf16)).astype(f32)).astype(bf16)


def y_sum(kept, sent):
    return kept.astype(f32) + flip_y(sent).astype(f32)


CHUNK = 128
HEAD = 64
TAPS = 4


def dot_nn(a, b):
    return lax.dot_general(a, b, (((1,), (0,)), ((), ())), preferred_element_type=f32)


def dot_nt(a, b):
    return lax.dot_general(a, b, (((1,), (1,)), ((), ())), preferred_element_type=f32)


def dot_tn(a, b):
    return lax.dot_general(a, b, (((0,), (0,)), ((), ())), preferred_element_type=f32)


def dot_exact(a, b):
    return lax.dot_general(
        a, b, (((1,), (0,)), ((), ())), precision=HIGHEST, preferred_element_type=f32
    )


def iota(shape, axis):
    return lax.broadcasted_iota(jnp.int32, shape, axis)


def earlier(tail, block, back):
    if back == 0:
        return block
    return pltpu.roll(jnp.concatenate([tail, block], axis=0), back, 0)[8:]


def later(block, head, ahead):
    if ahead == 0:
        return block
    both = jnp.concatenate([block, head], axis=0)
    return pltpu.roll(both, both.shape[0] - ahead, 0)[: block.shape[0]]


def conv_rows(tail, block, taps):
    total = block * taps[TAPS - 1 : TAPS] + taps[TAPS : TAPS + 1]
    for j in range(TAPS - 1):
        total = total + earlier(tail, block, TAPS - 1 - j) * taps[j : j + 1]
    return total


def conv_rows_back(grad, head, taps):
    total = grad * taps[TAPS - 1 : TAPS]
    for j in range(TAPS - 1):
        total = total + later(grad, head, TAPS - 1 - j) * taps[j : j + 1]
    return total


def conv_taps_back(tail, block, grad):
    rows = [
        jnp.sum(earlier(tail, block, TAPS - 1 - j) * grad, axis=0, keepdims=True)
        for j in range(TAPS)
    ]
    rows.append(jnp.sum(grad, axis=0, keepdims=True))
    rows.append(jnp.zeros((8 - len(rows), grad.shape[1]), f32))
    return jnp.concatenate(rows, axis=0)


def head_columns(columns, heads):
    rows = columns.shape[0]
    low = iota((rows, 2 * HEAD), 1) < HEAD
    return jnp.concatenate(
        [
            jnp.where(low, columns[:, h : h + 1], columns[:, h + 1 : h + 2])
            for h in range(0, heads, 2)
        ],
        axis=1,
    )


def head_sums(values, heads):
    rows = values.shape[0]
    low = iota((rows, 2 * HEAD), 1) < HEAD
    sums = []
    for pair in range(heads // 2):
        part = values[:, pair * 2 * HEAD : (pair + 1) * 2 * HEAD]
        sums.append(jnp.sum(jnp.where(low, part, 0.0), axis=1, keepdims=True))
        sums.append(jnp.sum(jnp.where(low, 0.0, part), axis=1, keepdims=True))
    return sums


def softplus(value):
    return jnp.maximum(value, 0.0) + jnp.log1p(jnp.exp(-jnp.abs(value)))


def step_rows(pdt, vec):
    size = pdt.shape[1]
    raw = pdt + vec[:, 0:1]
    dt = softplus(raw)
    rate = -jnp.exp(vec[:, 1:2])
    upper = (iota((size, size), 0) <= iota((size, size), 1)).astype(f32)
    logs = dot_exact(dt * rate, upper)
    last = logs[:, size - 1 : size]
    return raw, dt, rate, logs, jnp.exp(logs), jnp.exp(last - logs), jnp.exp(last)


def mamba_fwd_kernel(
    heads,
    rank,
    px,
    px_tail,
    pz,
    pbc,
    pbc_tail,
    pdt,
    taps,
    shared_taps,
    vec,
    om,
    kept,
    states,
    state,
):
    step = pl.program_id(0)

    @pl.when(step == 0)
    def _():
        state[...] = jnp.zeros_like(state)

    started = jnp.where(step == 0, 0.0, 1.0)
    u = conv_rows(px_tail[...] * started, px[...], taps[...])
    u = u * jax.nn.sigmoid(u)
    bc = conv_rows(pbc_tail[...] * started, pbc[...], shared_taps[...])
    bc = (bc * jax.nn.sigmoid(bc)).astype(bf16)
    half = bc.shape[1] // 2
    b_in, c_out = bc[:, :half], bc[:, half:]
    _, dt, _, logs, grow, fade, last = step_rows(pdt[...], vec[...])
    columns = jnp.transpose(jnp.concatenate([logs, grow, fade * dt, dt], axis=0))
    size = u.shape[0]
    causal = iota((size, size), 0) >= iota((size, size), 1)
    mixing = dot_nt(c_out, b_in)
    u_low = u.astype(bf16)
    low = iota((size, 2 * HEAD), 1) < HEAD
    local = []
    for pair in range(heads // 2):
        piece = u_low[:, pair * 2 * HEAD : (pair + 1) * 2 * HEAD]
        outs = []
        for h in (2 * pair, 2 * pair + 1):
            spread = jnp.where(causal, columns[:, h : h + 1] - logs[h : h + 1], -1e30)
            matrix = (mixing * jnp.exp(spread) * dt[h : h + 1]).astype(bf16)
            outs.append(dot_nn(matrix, piece))
        local.append(jnp.where(low, outs[0], outs[1]))
    before = state[...]
    states[0] = before
    carried = dot_nn(c_out, before.astype(bf16)) * head_columns(columns[:, 8:16], heads)
    skip = head_columns(jnp.transpose(jnp.broadcast_to(vec[:, 2:3], (8, size))), heads)
    total = jnp.concatenate(local, axis=1) + carried + skip * u
    z = pz[...]
    om[...] = (total * (z * jax.nn.sigmoid(z))).astype(bf16)
    kept[...] = total.astype(bf16)
    fed = (u * head_columns(columns[:, 16:24], heads)).astype(bf16)
    end = head_columns(jnp.transpose(jnp.broadcast_to(last, (8, 128))), heads)[:1]
    state[...] = before * end + dot_tn(b_in, fed)


def mamba_bwd_kernel(
    heads,
    rank,
    px,
    px_tail,
    pz,
    pbc,
    pbc_tail,
    pdt,
    taps,
    shared_taps,
    vec,
    states,
    gym,
    g_pxs,
    g_pbc,
    g_taps,
    g_shared,
    g_vec,
    g_skip,
    d_state,
    next_px,
    next_bc,
):
    step = pl.program_id(0)
    steps = pl.num_programs(0)

    @pl.when(step == 0)
    def _():
        d_state[...] = jnp.zeros_like(d_state)
        next_px[...] = jnp.zeros_like(next_px)
        next_bc[...] = jnp.zeros_like(next_bc)
        g_taps[...] = jnp.zeros_like(g_taps)
        g_shared[...] = jnp.zeros_like(g_shared)
        g_vec[...] = jnp.zeros_like(g_vec)
        g_skip[...] = jnp.zeros_like(g_skip)

    started = jnp.where(step == steps - 1, 0.0, 1.0)
    size = px.shape[0]
    tail_x = px_tail[...] * started
    block_x = px[...]
    pre_u = conv_rows(tail_x, block_x, taps[...])
    sig_u = jax.nn.sigmoid(pre_u)
    u = pre_u * sig_u
    tail_bc = pbc_tail[...] * started
    block_bc = pbc[...]
    pre_bc = conv_rows(tail_bc, block_bc, shared_taps[...])
    sig_bc = jax.nn.sigmoid(pre_bc)
    bc = (pre_bc * sig_bc).astype(bf16)
    half = bc.shape[1] // 2
    b_in, c_out = bc[:, :half], bc[:, half:]
    raw, dt, rate, logs, grow, fade, last = step_rows(pdt[...], vec[...])
    columns = jnp.transpose(jnp.concatenate([logs, grow, fade, dt], axis=0))
    z = pz[...]
    sig_z = jax.nn.sigmoid(z)
    g = gym[...]
    dy = g * (z * sig_z)
    dy_low = dy.astype(bf16)
    u_low = u.astype(bf16)
    before = states[0]
    before_low = before.astype(bf16)
    d_after = d_state[...]
    d_after_low = d_after.astype(bf16)
    causal = iota((size, size), 0) <= iota((size, size), 1)
    mixing = dot_nt(b_in, c_out)
    low = iota((size, 2 * HEAD), 1) < HEAD
    d_mixing = jnp.zeros((size, size), f32)
    du_local, col_sums, row_sums = [], [], []
    for pair in range(heads // 2):
        lanes = slice(pair * 2 * HEAD, (pair + 1) * 2 * HEAD)
        u_piece, dy_piece = u_low[:, lanes], dy_low[:, lanes]
        outs = []
        for h in (2 * pair, 2 * pair + 1):
            dt_col = columns[:, 24 + h : 25 + h]
            spread = jnp.where(causal, logs[h : h + 1] - columns[:, h : h + 1], -1e30)
            decay = jnp.exp(spread)
            keep = low if h % 2 == 0 else jnp.logical_not(low)
            masked = jnp.where(keep, u_piece, jnp.zeros_like(u_piece))
            product = dot_nt(masked, dy_piece) * decay
            d_mixing = d_mixing + product * dt_col
            product = product * mixing
            col_sums.append(jnp.sum(product, axis=1, keepdims=True))
            row_sums.append(jnp.sum(product * dt_col, axis=0, keepdims=True))
            outs.append(dot_nn((mixing * decay).astype(bf16), dy_piece))
        du_local.append(jnp.where(low, outs[0], outs[1]))
    grow_all = head_columns(columns[:, 8:16], heads)
    fade_all = head_columns(columns[:, 16:24], heads)
    dt_all = head_columns(columns[:, 24:32], heads)
    dy_grown = dy * grow_all
    dy_grown_low = dy_grown.astype(bf16)
    fed_low = (u * fade_all * dt_all).astype(bf16)
    back = dot_nn(b_in, d_after_low) * fade_all
    inter = head_sums(dy_grown * dot_nn(c_out, before_low), heads)
    tails = head_sums(u * back, heads)
    skip = head_columns(jnp.transpose(jnp.broadcast_to(vec[:, 2:3], (8, size))), heads)
    du = (jnp.concatenate(du_local, axis=1) + back) * dt_all + skip * dy
    d_mixing_low = d_mixing.astype(bf16)
    db = dot_nn(d_mixing_low, c_out) + dot_nt(fed_low, d_after_low)
    dc = dot_tn(d_mixing_low, b_in) + dot_nt(dy_grown_low, before_low)
    end = head_columns(jnp.transpose(jnp.broadcast_to(last, (8, 128))), heads)[:1]
    ended = d_after * end
    ends = head_sums(jnp.sum(ended * before, axis=0, keepdims=True), heads)
    d_state[...] = ended + dot_tn(c_out, dy_grown_low)
    lane = iota((size, 128), 1)
    gathered = jnp.zeros((size, 128), f32)
    for h in range(heads):
        gathered = jnp.where(lane == h, col_sums[h] + tails[h], gathered)
        gathered = jnp.where(lane == 8 + h, tails[h], gathered)
        gathered = jnp.where(lane == 16 + h, inter[h], gathered)
    turned = jnp.transpose(gathered)
    direct, tail_row, inter_row = turned[0:8], turned[8:16], turned[16:24]
    pad = [jnp.zeros((1, size), f32)] * (8 - heads)
    row_sum = jnp.concatenate(row_sums + pad, axis=0)
    zero = jnp.zeros((1, 1), f32)
    end_col = jnp.concatenate(ends + [zero] * (8 - heads), axis=0)
    d_logs = row_sum + inter_row - dt * direct
    at_last = end_col + jnp.sum(dt * tail_row, axis=1, keepdims=True)
    lower = (iota((size, size), 0) >= iota((size, size), 1)).astype(f32)
    d_rate = dot_exact(d_logs, lower) + at_last
    d_dt = direct + rate * d_rate
    d_raw = d_dt * jax.nn.sigmoid(raw)
    spread_rows = jnp.concatenate([d_raw, jnp.zeros((120, size), f32)], axis=0)
    g_pxs[:, u.shape[1] :] = jnp.transpose(spread_rows).astype(bf16)
    g_vec[0:8] += d_raw
    g_vec[8:16] += rate * dt * d_rate
    g_skip[...] += jnp.sum((dy * u).reshape(size // 8, 8, u.shape[1]), axis=0)
    d_pre = du * (sig_u * (1.0 + pre_u * (1.0 - sig_u)))
    g_pxs[:, : u.shape[1]] = conv_rows_back(d_pre, next_px[...], taps[...]).astype(bf16)
    g_taps[...] += conv_taps_back(tail_x, block_x, d_pre)
    next_px[...] = d_pre[:8]
    d_bc = jnp.concatenate([db, dc], axis=1) * (sig_bc * (1.0 + pre_bc * (1.0 - sig_bc)))
    g_pbc[...] = conv_rows_back(d_bc, next_bc[...], shared_taps[...]).astype(bf16)
    g_shared[...] += conv_taps_back(tail_bc, block_bc, d_bc)
    next_bc[...] = d_bc[:8]


def pad_rows(value):
    return jnp.pad(value, ((0, -value.shape[0] % 8), (0, 0)))


def vec_of(step_bias, decay_log, skip_gain):
    table = jnp.stack([step_bias, decay_log, skip_gain], axis=1)
    return jnp.pad(table, ((0, 8 - table.shape[0]), (0, 128 - table.shape[1])))


def whole(shape):
    return pl.BlockSpec(shape, lambda i, r: tuple(0 for _ in shape))


def cost(flops, moved, exps):
    return pl.CostEstimate(flops=flops, bytes_accessed=moved, transcendentals=exps)


def chunk_specs(length, ranks, order):
    per_block = length // ranks // CHUNK
    per = CHUNK // 8

    def place(i, r):
        c = order(i)
        return ((c // per_block) ^ r[0]) * per_block + c % per_block

    def at(cols):
        return pl.BlockSpec((CHUNK, cols), lambda i, r: (place(i, r), 0))

    def tail(cols):
        def index(i, r):
            c = jnp.maximum(order(i) - 1, 0)
            return ((((c // per_block) ^ r[0]) * per_block + c % per_block) * per + per - 1, 0)

        return pl.BlockSpec((8, cols), index)

    row = pl.BlockSpec((8, CHUNK), lambda i, r: (0, place(i, r)))
    return at, tail, row


def mamba_fwd(rank, px, pz, pbc, pdt, taps, shared_taps, vec, heads, ranks):
    length, chans = px.shape
    wide = pbc.shape[1]
    steps = length // CHUNK
    at, tail, row = chunk_specs(length, ranks, lambda i: i)
    return pl.pallas_call(
        functools.partial(mamba_fwd_kernel, heads),
        grid_spec=pltpu.PrefetchScalarGridSpec(
            num_scalar_prefetch=1,
            grid=(steps,),
            in_specs=[
                at(chans),
                tail(chans),
                at(chans),
                at(wide),
                tail(wide),
                row,
                whole((8, chans)),
                whole((8, wide)),
                whole((8, 128)),
            ],
            out_specs=[
                at(chans),
                at(chans),
                pl.BlockSpec((1, wide // 2, chans), lambda i, r: (i, 0, 0)),
            ],
            scratch_shapes=[pltpu.VMEM((wide // 2, chans), f32)],
        ),
        out_shape=[
            jax.ShapeDtypeStruct((length, chans), bf16),
            jax.ShapeDtypeStruct((length, chans), bf16),
            jax.ShapeDtypeStruct((steps, wide // 2, chans), f32),
        ],
        cost_estimate=cost(4 * 10**9, 8 * 10**6, 10**6),
        name="mamba_forward",
    )(rank, px, px, pz, pbc, pbc, pdt, taps, shared_taps, vec)


def mamba_bwd(rank, px, pz, pbc, pdt, taps, shared_taps, vec, states, gym, heads, ranks):
    length, chans = px.shape
    wide = pbc.shape[1]
    steps = length // CHUNK
    at, tail, row = chunk_specs(length, ranks, lambda i: steps - 1 - i)
    return pl.pallas_call(
        functools.partial(mamba_bwd_kernel, heads),
        grid_spec=pltpu.PrefetchScalarGridSpec(
            num_scalar_prefetch=1,
            grid=(steps,),
            in_specs=[
                at(chans),
                tail(chans),
                at(chans),
                at(wide),
                tail(wide),
                row,
                whole((8, chans)),
                whole((8, wide)),
                whole((8, 128)),
                pl.BlockSpec((1, wide // 2, chans), lambda i, r: (steps - 1 - i, 0, 0)),
                at(chans),
            ],
            out_specs=[
                at(chans + 128),
                at(wide),
                whole((8, chans)),
                whole((8, wide)),
                whole((16, 128)),
                whole((8, chans)),
            ],
            scratch_shapes=[
                pltpu.VMEM((wide // 2, chans), f32),
                pltpu.VMEM((8, chans), f32),
                pltpu.VMEM((8, wide), f32),
            ],
        ),
        out_shape=[
            jax.ShapeDtypeStruct((length, chans + 128), bf16),
            jax.ShapeDtypeStruct((length, wide), bf16),
            jax.ShapeDtypeStruct((8, chans), f32),
            jax.ShapeDtypeStruct((8, wide), f32),
            jax.ShapeDtypeStruct((16, 128), f32),
            jax.ShapeDtypeStruct((8, chans), f32),
        ],
        cost_estimate=cost(9 * 10**9, 10**7, 10**6),
        name="mamba_backward",
    )(rank, px, px, pz, pbc, pbc, pdt, taps, shared_taps, vec, states, gym)


ROWS = 256


def turn(pre, cosine, sine):
    inner = iota(pre.shape, 1) % HEAD < HEAD // 2
    lanes = pre.shape[1]
    other = jnp.where(
        inner, pltpu.roll(pre, lanes - HEAD // 2, 1), pltpu.roll(pre, HEAD // 2, 1)
    )
    return pre * cosine + other * sine


def attend_fwd_kernel(scale, rank, qkv, cosine, sine, out, q, k, v):
    length, wide = out.shape
    blocks = length // ROWS
    low = iota((ROWS, 2 * HEAD), 1) < HEAD
    load_qkv(rank, qkv, cosine, sine, q, k, v)
    for i in range(blocks):
        seen = (i + 1) * ROWS
        block = q[i * ROWS : (i + 1) * ROWS]
        keys, values = k[:seen], v[:seen]
        allowed = iota((ROWS, seen), 1) <= iota((ROWS, seen), 0) + i * ROWS
        outs = []
        for h in range(2):
            keep = low if h == 0 else jnp.logical_not(low)
            part = jnp.where(keep, block, jnp.zeros_like(block))
            scores = jnp.where(allowed, dot_nt(part, keys) * scale, -1e30)
            expo = jnp.exp(scores - jnp.max(scores, axis=1, keepdims=True))
            chance = expo * (1.0 / jnp.sum(expo, axis=1, keepdims=True))
            outs.append(dot_nn(chance.astype(bf16), values))
        out[relative_rows(rank, i)] = jnp.where(low, outs[0], outs[1]).astype(bf16)


def relative_rows(rank, i):
    return pl.ds(pl.multiple_of((i ^ rank[0]) * ROWS, ROWS), ROWS)


def load_qkv(rank, qkv, cosine, sine, q, k, v):
    wide = q.shape[1]
    for i in range(q.shape[0] // ROWS):
        rows = slice(i * ROWS, (i + 1) * ROWS)
        piece = qkv[relative_rows(rank, i)]
        q[rows] = turn(piece[:, :wide], cosine[rows], sine[rows]).astype(bf16)
        both = piece[:, wide:]
        turned = pltpu.roll(both, HEAD, 1)
        low = iota(both.shape, 1) < HEAD
        k[rows] = turn(jnp.where(low, both, turned), cosine[rows], sine[rows]).astype(bf16)
        v[rows] = jnp.where(low, turned, both).astype(bf16)


def attend_bwd_kernel(scale, rank, qkv, cosine, sine, go, g_qkv, q, k, v, dk, dv):
    length, wide = dk.shape
    blocks = length // ROWS
    low = iota((ROWS, 2 * HEAD), 1) < HEAD
    load_qkv(rank, qkv, cosine, sine, q, k, v)
    dk[...] = jnp.zeros_like(dk)
    dv[...] = jnp.zeros_like(dv)
    for i in range(blocks):
        seen = (i + 1) * ROWS
        rows = slice(i * ROWS, (i + 1) * ROWS)
        block, grads = q[rows], go[relative_rows(rank, i)]
        keys, values = k[:seen], v[:seen]
        allowed = iota((seen, ROWS), 0) <= iota((seen, ROWS), 1) + i * ROWS
        dqs, dks, dvs = [], [], []
        for h in range(2):
            keep = low if h == 0 else jnp.logical_not(low)
            part = jnp.where(keep, block, jnp.zeros_like(block))
            part_g = jnp.where(keep, grads, jnp.zeros_like(grads))
            scores = jnp.where(allowed, dot_nt(keys, part) * scale, -1e30)
            expo = jnp.exp(scores - jnp.max(scores, axis=0, keepdims=True))
            chance = expo * (1.0 / jnp.sum(expo, axis=0, keepdims=True))
            g_chance = dot_nt(values, part_g)
            center = jnp.sum(chance * g_chance, axis=0, keepdims=True)
            g_scores = (chance * (g_chance - center)).astype(bf16)
            dqs.append(dot_tn(g_scores, keys))
            dks.append(dot_nn(g_scores, part))
            dvs.append(dot_nn(chance.astype(bf16), part_g))
        dq = jnp.where(low, dqs[0], dqs[1]) * scale
        g_qkv[relative_rows(rank, i), :wide] = turn(dq, cosine[rows], -sine[rows]).astype(bf16)
        dk[:seen] += (dks[0] + dks[1]) * scale
        dv[:seen] += dvs[0] + dvs[1]
    for i in range(blocks):
        rows = slice(i * ROWS, (i + 1) * ROWS)
        g_k, g_v = dk[rows], dv[rows]
        g_k = turn(g_k + pltpu.roll(g_k, HEAD, 1), cosine[rows], -sine[rows])
        g_v = g_v + pltpu.roll(g_v, HEAD, 1)
        g_qkv[relative_rows(rank, i), wide:] = jnp.where(low, g_k, g_v).astype(bf16)


def attend_specs(length, wide):
    return [
        whole((length, 2 * wide)),
        whole((length, wide)),
        whole((length, wide)),
    ], [pltpu.VMEM((length, wide), bf16)] * 3


def attend_fwd(rank, qkv, cosine, sine):
    length, wide = cosine.shape
    ins, scratch = attend_specs(length, wide)
    return pl.pallas_call(
        functools.partial(attend_fwd_kernel, HEAD**-0.5),
        grid_spec=pltpu.PrefetchScalarGridSpec(
            num_scalar_prefetch=1,
            grid=(1,),
            in_specs=ins,
            out_specs=whole((length, wide)),
            scratch_shapes=scratch,
        ),
        out_shape=jax.ShapeDtypeStruct((length, wide), bf16),
        cost_estimate=cost(2 * 10**9, 4 * 10**6, 10**6),
        name="attend_forward",
    )(rank, qkv, cosine, sine)


def attend_bwd(rank, qkv, cosine, sine, g_oa):
    length, wide = cosine.shape
    ins, scratch = attend_specs(length, wide)
    return pl.pallas_call(
        functools.partial(attend_bwd_kernel, HEAD**-0.5),
        grid_spec=pltpu.PrefetchScalarGridSpec(
            num_scalar_prefetch=1,
            grid=(1,),
            in_specs=ins + [whole((length, wide))],
            out_specs=whole((length, 2 * wide)),
            scratch_shapes=scratch + [pltpu.VMEM((length, wide), f32)] * 2,
        ),
        out_shape=jax.ShapeDtypeStruct((length, 2 * wide), bf16),
        cost_estimate=cost(4 * 10**9, 6 * 10**6, 10**6),
        name="attend_backward",
    )(rank, qkv, cosine, sine, g_oa)


def project_kernel(order, chans, scalars, even, odd, gain, w_x, w_z, w_bc, *outs):
    a1, kept, px, pz, pbc, pdt, qkv = outs
    rows, width = even.shape
    block = width // len(order)
    is_even = pl.program_id(0) % 2 == 0
    step = 32

    def norm(source, keep):
        for i in range(rows // step):
            own = slice(i * step, (i + 1) * step)
            value = source[own].astype(f32)
            rho = lax.rsqrt(jnp.mean(value * value, axis=1, keepdims=True) + epsilon)
            for p, k in enumerate(order):
                there = pl.ds(pl.multiple_of((scalars[0] ^ k) * block, block), block)
                here = slice(p * block, (p + 1) * block)
                piece = source[own, there]
                a1[own, here] = (piece.astype(f32) * rho * gain[:, here]).astype(bf16)
                if keep:
                    kept[own, here] = piece

    @pl.when(is_even)
    def _():
        norm(even, True)

    @pl.when(jnp.logical_not(is_even))
    def _():
        norm(odd, False)

    value = a1[...]
    px[...] = dot_nn(value, w_x[:, :chans])
    steps = lax.dot_general(
        w_x[:, chans:], value, (((0,), (1,)), ((), ())), preferred_element_type=f32
    )
    pdt[...] = steps[:8]
    pz[...] = dot_nn(value, w_z[:, :chans])
    pbc[...] = dot_nn(value, w_bc[...])
    qkv[...] = dot_nn(value, w_z[:, chans:])


def project(scalars, even, odd, gain, w_x, w_z, w_bc, chans, size):
    rows, width = even.shape[0] // 2, even.shape[1]
    length = 4 * rows
    if width // size % 128:
        member = scalars[0]
        even = take_blocks(even, member, size, False)
        odd = take_blocks(odd, member, size, False)
        order = [0]
    else:
        order = relative_order(size)
    if len(order) == 1:
        scalars = jnp.zeros_like(scalars)

    def at(cols):
        return pl.BlockSpec((rows, cols), lambda i, r: (i, 0))

    def half(cols):
        return pl.BlockSpec((rows, cols), lambda i, r: (i // 2, 0))

    def shape(cols, kind, count=length):
        return jax.ShapeDtypeStruct((count, cols), kind)

    n2, low = w_bc.shape[1], w_z.shape[1] - chans
    return pl.pallas_call(
        functools.partial(project_kernel, order, chans),
        grid_spec=pltpu.PrefetchScalarGridSpec(
            num_scalar_prefetch=1,
            grid=(4,),
            in_specs=[half(width), half(width), whole((1, width))]
            + [whole(item.shape) for item in (w_x, w_z, w_bc)],
            out_specs=[
                at(width),
                half(width),
                at(chans),
                at(chans),
                at(n2),
                pl.BlockSpec((8, rows), lambda i, r: (0, i)),
                at(low),
            ],
        ),
        out_shape=[
            shape(width, bf16),
            shape(width, bf16, 2 * rows),
            shape(chans, f32),
            shape(chans, f32),
            shape(n2, f32),
            shape(length, f32, 8),
            shape(low, f32),
        ],
        cost_estimate=cost(3 * 10**9, 14 * 10**6, length),
        name="norm_project",
    )(scalars, even, odd, gain.reshape(1, -1), w_x, w_z, w_bc)


def mixer_back_kernel(chans, rank, g0, g1, g2, g3, w_o, pz, kept, g_ym, g_oa, g_pz, total):
    for k, piece in enumerate((g0, g1, g2, g3)):

        @pl.when(pl.program_id(0) == k)
        def _(piece=piece):
            total[...] = dot_nn(piece[...], w_o[...])

    back = total[:, :chans]
    g_ym[...] = back
    g_oa[...] = total[:, chans:].astype(bf16)
    z = pz[...]
    sig = jax.nn.sigmoid(z)
    g_pz[...] = (back * kept[...].astype(f32) * (sig * (1.0 + z * (1.0 - sig)))).astype(bf16)


def mixer_back(token, g_m, w_o, pz, kept):
    rows, width = g_m[0].shape
    length, chans = pz.shape
    other = w_o.shape[1] - chans

    def at(cols):
        return pl.BlockSpec((rows, cols), lambda i, r: (i, 0))

    return pl.pallas_call(
        functools.partial(mixer_back_kernel, chans),
        grid_spec=pltpu.PrefetchScalarGridSpec(
            num_scalar_prefetch=1,
            grid=(4,),
            in_specs=[whole((rows, width))] * 4 + [whole(w_o.shape), at(chans), at(chans)],
            out_specs=[at(chans), at(other), at(chans)],
            scratch_shapes=[pltpu.VMEM((rows, w_o.shape[1]), f32)],
        ),
        out_shape=[
            jax.ShapeDtypeStruct((length, chans), f32),
            jax.ShapeDtypeStruct((length, other), bf16),
            jax.ShapeDtypeStruct((length, chans), bf16),
        ],
        cost_estimate=cost(10**9, 9 * 10**6, 10**6),
        name="mixer_back",
    )(token, *g_m, w_o, pz, kept)


def project_back_kernel(chans, rank, a1, g_pz, g_qkv, g_pxs, g_bc, w_x, w_z, w_bc, *outs):
    kept, sent, sums = outs
    step = pl.program_id(0)
    total = dot_nt(g_pz[...], w_z[:, :chans]) + dot_nt(g_pxs[...], w_x[...])
    total = total + dot_nt(g_qkv[...], w_z[:, chans:]) + dot_nt(g_bc[...], w_bc[...])

    @pl.when(step == 0)
    def _():
        sums[...] = jnp.zeros_like(sums)

    rows, width = total.shape
    weighed = total * a1[...].astype(f32)
    sums[...] += jnp.sum(weighed.reshape(rows // 8, 8, width), axis=0)

    @pl.when(step % 2 == 0)
    def _():
        kept[...] = total

    @pl.when(step % 2 == 1)
    def _():
        sent[...] = total.astype(bf16)


def project_back(token, a1, g_pz, g_qkv, g_pxs, g_bc, w_x, w_z, w_bc):
    length, width = a1.shape
    chans = g_pz.shape[1]
    rows = length // 4

    def at(cols):
        return pl.BlockSpec((rows, cols), lambda i, r: (i, 0))

    half = pl.BlockSpec((rows, width), lambda i, r: (i // 2, 0))
    parts = (a1, g_pz, g_qkv, g_pxs, g_bc)
    return pl.pallas_call(
        functools.partial(project_back_kernel, chans),
        grid_spec=pltpu.PrefetchScalarGridSpec(
            num_scalar_prefetch=1,
            grid=(4,),
            in_specs=[at(item.shape[1]) for item in parts]
            + [whole(item.shape) for item in (w_x, w_z, w_bc)],
            out_specs=[half, half, whole((8, width))],
        ),
        out_shape=[
            jax.ShapeDtypeStruct((2 * rows, width), f32),
            jax.ShapeDtypeStruct((2 * rows, width), bf16),
            jax.ShapeDtypeStruct((8, width), f32),
        ],
        cost_estimate=cost(3 * 10**9, 11 * 10**6, 0),
        name="project_back",
    )(token, *parts, w_x, w_z, w_bc)


def rotary_tables(length):
    half = HEAD // 2
    frequency = rotary_base ** (-2.0 * jnp.arange(half, dtype=f32) / HEAD)
    angles = jnp.arange(length, dtype=f32)[:, None] * frequency[None, :]
    cosine, sine = jnp.cos(angles), jnp.sin(angles)
    return (
        jnp.concatenate([cosine] * 4, axis=1),
        jnp.concatenate([-sine, sine, -sine, sine], axis=1),
    )


def swiglu(gate_part, up_part):
    return jax.nn.silu(gate_part) * up_part


def mm(a, b):
    return jnp.dot(a, b, preferred_element_type=f32)


def mm_t(a, b):
    return lax.dot_general(a, b, (((1,), (1,)), ((), ())), preferred_element_type=f32)


def t_mm(a, b):
    return lax.dot_general(a, b, (((0,), (0,)), ((), ())), preferred_element_type=f32)


def body(
    layer_in,
    out_grad,
    lengths,
    mamba_x,
    mamba_z,
    mamba_step,
    query_proj,
    key_proj,
    value_proj,
    mamba_out,
    attend_out,
    mlp_gate,
    mlp_up,
    mlp_down,
    state_proj,
    conv_state,
    norm_gains,
    conv_mamba,
    step_bias,
    decay_log,
    skip_gain,
):
    ranks = lax.axis_size("tensor")
    assert ranks == 4 and layer_in.shape[1] == 1
    rank = lax.axis_index("tensor")
    y, core = rank // 2, rank % 2
    rank_ref = rank.reshape(1)
    peers = lax.axis_size("dp")
    me = lax.axis_index("dp")
    rows, _, width = layer_in.shape
    length = rows * ranks
    chans = mamba_x.shape[1]
    heads = step_bias.shape[0]
    q_cols, k_cols = query_proj.shape[1], key_proj.shape[1]
    ff = mlp_gate.shape[1]
    own_rows, n2 = state_proj.shape

    raw_0 = layer_in[:, 0]
    raw_even = jnp.concatenate([raw_0, flip_y(raw_0)], axis=0)
    raw_odd = flip_core(raw_even)

    step_low = jnp.pad(mamba_step.astype(bf16), ((0, 0), (0, 128 - heads)))
    pack_x = jnp.concatenate([mamba_x.astype(bf16), step_low], axis=1)
    pack_z = jnp.concatenate(
        [item.astype(bf16) for item in (mamba_z, query_proj, key_proj, value_proj)], axis=1
    )
    first = Gather(pack_x, "dp", False)
    second = Gather(pack_z, "dp", True)
    small = jnp.concatenate([conv_state.reshape(-1), norm_gains.reshape(-1)])
    parts = []
    rest = small
    for _ in range(3):
        parts.append(lax.reduce_precision(rest, 8, 7))
        rest = rest - parts[-1]
    parts = jnp.concatenate(parts)
    small_rows = -(-parts.shape[0] // n2)
    parts = jnp.pad(parts, (0, small_rows * n2 - parts.shape[0])).reshape(small_rows, n2)
    pack_s = jnp.concatenate([state_proj, parts], axis=0).astype(bf16)
    pack_o = jnp.concatenate([mamba_out.T.astype(bf16), attend_out.T.astype(bf16)], axis=1)
    pack_d = mlp_down.T.astype(bf16)
    pack_g = jnp.concatenate([mlp_gate.astype(bf16), mlp_up.astype(bf16)], axis=1)
    ranked = in_rank_order(pack_s, y, core)
    third = Gather(ranked.reshape(-1, n2), "dp", False)
    first.until(2)
    second.until(2)
    third.until(2)
    pack_o = after(pack_o, first.held, second.held)
    gather_o = Gather(pack_o, "dp", True)
    far_x = first.advance()
    far_z = second.advance()
    third.advance()
    pack_d, pack_g = lax.optimization_barrier((pack_d, pack_g, far_x, far_z))[:2]
    gather_d = Gather(pack_d, "dp", True)
    gather_g = Gather(pack_g, "dp", False)
    w_x = first.advance()
    w_z = second.advance()
    all_s = third.advance().reshape(peers, ranks, own_rows + small_rows, n2)
    w_bc = all_s[:, :, :own_rows].reshape(width, n2)
    parts = all_s[:, :, own_rows:].reshape(peers, ranks, -1).astype(f32)
    count = small.shape[0]
    small = parts[..., :count] + parts[..., count : 2 * count] + parts[..., 2 * count : 3 * count]
    cut = conv_state.size
    taps_own = conv_state.shape[1]
    gains_own = norm_gains.shape[1]
    taps_rel = small[..., :cut].reshape(peers, ranks, conv_state.shape[0], taps_own)
    taps_rel = jnp.transpose(taps_rel, (2, 0, 1, 3)).reshape(conv_state.shape[0], -1)
    conv_shared = take_blocks(taps_rel, me, peers, True)
    gain_pair = jnp.transpose(
        small[..., cut:].reshape(peers, ranks, 2, gains_own), (2, 0, 1, 3)
    ).reshape(2, width)

    def rho_of(values):
        return lax.rsqrt(jnp.mean(values * values, axis=-1, keepdims=True) + epsilon)

    a1, x02, px, pz, pbc, pdt, qkv = project(
        me.reshape(1), raw_even, raw_odd, gain_pair[0], w_x, w_z, w_bc, chans, peers
    )
    x0, x2 = x02[:rows], x02[rows:]

    limit = lengths[0]

    def masked(block, k):
        place = (rank ^ k) * rows + jnp.arange(rows, dtype=jnp.int32)
        return jnp.where((place < limit)[:, None], block, jnp.zeros_like(block))

    gf0 = masked(move_blocks(after(out_grad, far_x)[:, 0], me, peers, False), 0)

    sent_o = gather_o.until(2, pdt)
    sent_d = gather_d.until(2, pdt)
    sent_g = gather_g.until(2, pdt)
    cosine, sine = rotary_tables(length)
    oa = attend_fwd(after(rank_ref, sent_o, sent_d, sent_g), qkv, cosine, sine)
    gf2 = flip_y(after(gf0, pdt))
    sent_o = gather_o.advance(oa)
    sent_g = gather_g.advance(oa)
    vec = vec_of(step_bias, decay_log, skip_gain)
    taps, shared_taps = pad_rows(conv_mamba), pad_rows(conv_shared)
    om, kept, states = mamba_fwd(
        after(rank_ref, sent_o, sent_g), px, pz, pbc, pdt, taps, shared_taps, vec, heads, ranks
    )
    w_o = gather_o.advance(om)
    gf1, gf3 = flip_core(after(gf0, oa)), flip_core(after(gf2, oa))
    gf_a = jnp.concatenate([gf0, gf1], axis=0)
    gf_b = jnp.concatenate([gf2, gf3], axis=0)
    gather_d.advance(om)
    w_dn = gather_d.advance()
    w_gu = gather_g.advance(om)

    def mixer_term(k):
        lines = slice(k * rows, (k + 1) * rows)
        return mm_t(om[lines], w_o[:, :chans]) + mm_t(oa[lines], w_o[:, chans:])

    s2 = core_sum(mixer_term(2), mixer_term(3))
    s0 = core_sum(mixer_term(0), mixer_term(1))

    def second_norm(low_x, m):
        r1 = low_x.astype(f32) + m
        rho = rho_of(r1)
        return r1, rho, (r1 * rho * gain_pair[1]).astype(bf16)

    r1_0, rho_0, a2_0 = second_norm(x0, y_sum(s0, s2))
    a2_1 = flip_core(a2_0)
    a2_a = jnp.concatenate([a2_0, a2_1], axis=0)
    r1_2, rho_2, a2_2 = second_norm(x2, y_sum(s2, s0))
    a2_3 = flip_core(a2_2)
    a2_b = jnp.concatenate([a2_2, a2_3], axis=0)

    def feed(a2, gf):
        gate_up = mm(a2, w_gu)
        gate, up = gate_up[:, :ff], gate_up[:, ff:]
        hidden, glu_back = jax.vjp(swiglu, gate, up)
        hid = hidden.astype(bf16)
        gate_grad, up_grad = glu_back(mm(gf, w_dn))
        g_gu = jnp.concatenate([gate_grad.astype(bf16), up_grad.astype(bf16)], axis=1)
        return hid, g_gu, mm_t(g_gu, w_gu)

    hid_a, g_gu_a, g_a2_a = feed(a2_a, gf_a)
    t0 = core_sum(g_a2_a[:rows], g_a2_a[rows:])
    hid_b, g_gu_b, g_a2_b = feed(a2_b, gf_b)
    t2 = core_sum(g_a2_b[:rows], g_a2_b[rows:])

    halves = ((0, 0), (0, 1), (1, 0), (1, 1))
    dn_kept, dn_sent = product(
        after(rank_ref, g_a2_b),
        [(left, [((hid_a, hid_b)[p], b)]) for left, (p, b) in zip((gf0, gf1, gf2, gf3), halves)],
        True,
    )
    dn = Sum(dn_kept, dn_sent, "dp", True)
    gu_kept, gu_sent = product(
        after(rank_ref, dn_sent),
        [
            (left, [((g_gu_a, g_gu_b)[p], b)])
            for left, (p, b) in zip((a2_0, a2_1, a2_2, a2_3), halves)
        ],
        False,
    )
    gu = Sum(gu_kept, gu_sent, "dp", False)

    def second_back(g_a2, r1, rho, gf):
        n_two = r1 * rho
        e_two = g_a2 * gain_pair[1]
        inner = jnp.mean(e_two * n_two, axis=-1, keepdims=True)
        return gf.astype(f32) + rho * (e_two - n_two * inner)

    t0_got, t2_got = flip_y(t0), flip_y(t2)
    g_a2_2 = t2.astype(f32) + after(t0_got, t2, dn_sent).astype(f32)
    g_r1_2 = second_back(g_a2_2, r1_2, rho_2, gf2)
    g_m_2 = g_r1_2.astype(bf16)
    g_a2_0 = t0.astype(f32) + after(t2_got, gu_sent).astype(f32)
    g_r1_0 = second_back(g_a2_0, r1_0, rho_0, gf0)
    g_m_0 = g_r1_0.astype(bf16)
    gain_two_grad = jnp.sum(g_a2_0 * (r1_0 * rho_0), axis=0)
    g_m_3, g_m_1 = flip_core(g_m_2), flip_core(g_m_0)
    g_m = (g_m_0, g_m_1, g_m_2, g_m_3)
    g_ym, g_oa, g_pz = mixer_back(after(rank_ref, dn_sent, gu_sent), g_m, w_o, pz, kept)

    out_kept, out_sent = product(
        after(rank_ref, g_oa), [(g_m[k], [(om, k), (oa, k)]) for k in range(4)], True
    )
    out = Sum(out_kept, out_sent, "dp", True)

    hid_a, hid_b = lax.optimization_barrier((hid_a, hid_b, g_m_0))[:2]
    f_a, f_b = mm_t(hid_a, w_dn), mm_t(hid_b, w_dn)
    f_sent = jnp.concatenate([f_a[rows:], f_b[rows:]], axis=0).astype(bf16)
    f_got = flip_core(f_sent)
    g_qkv = attend_bwd(after(rank_ref, out_sent, f_sent), qkv, cosine, sine, g_oa)
    sent_dn = dn.advance(g_qkv)
    sent_gu = gu.advance(g_qkv)
    f_kept = jnp.concatenate([f_a[:rows], f_b[:rows]], axis=0)
    f02 = (f_kept + after(f_got, g_qkv).astype(f32)).astype(bf16)
    f_other = flip_y(f02[rows:])
    z_kept, z_sent = product(
        after(rank_ref, sent_dn, sent_gu, f02), [(a1, [(g_pz, 0), (g_qkv, 0)])], False
    )
    z = Sum(z_kept, z_sent, "dp", False)

    g_pxs, g_bc, g_taps, g_shared, g_vec, g_skip = mamba_bwd(
        after(rank_ref, z_sent),
        px, pz, pbc, pdt, taps, shared_taps, vec, states, g_ym, heads, ranks,
    )
    x_kept, x_sent = product(rank_ref, [(a1, [(g_pxs, 0)])], False)
    x = Sum(x_kept, x_sent, "dp", False)
    f_other = after(f_other, x_sent)
    sent_dn = dn.advance(x_sent)
    sent_gu = gu.advance(x_sent)
    sent_out = out.advance(x_sent)
    sent_z = z.advance(x_sent)
    state_part = t_mm(after(a1, x_sent), g_bc).reshape(peers, 2, 2, own_rows, n2)
    g_kept, g_sent, g_sums = project_back(
        after(rank_ref, sent_dn, sent_gu, sent_out, sent_z),
        a1, g_pz, g_qkv, g_pxs, g_bc, w_x, w_z, w_bc,
    )
    g_got = flip_core(g_sent)
    gain_one_grad = jnp.sum(g_sums, axis=0) / gain_pair[0]

    sent_out = out.advance(g_sums)
    sent_z = z.advance(g_sums)
    dn_sum, gu_sum = dn.finish(g_sums), gu.finish(g_sums)
    u02 = (g_kept + after(g_got, sent_out, sent_z).astype(f32)).astype(bf16)
    u_other = flip_y(u02[rows:])

    conv_taps_grad = g_taps[: conv_mamba.shape[0]]
    conv_shared_grad = g_shared[: conv_state.shape[0]]
    bias_grad = jnp.sum(g_vec[:heads], axis=1)
    decay_grad = jnp.sum(g_vec[8 : 8 + heads], axis=1)
    skip_grad = jnp.sum(g_skip.reshape(8, heads, HEAD), axis=(0, 2))
    gain_grads = take_blocks(jnp.stack([gain_one_grad, gain_two_grad]), me, peers, True)

    def rows_of(items):
        flat = jnp.concatenate([item.reshape(-1) for item in items])
        return jnp.pad(flat, (0, -flat.shape[0] % (8 * n2))).reshape(-1, n2)

    both = rows_of([conv_shared_grad, gain_grads])
    only = rows_of([conv_taps_grad, bias_grad, decay_grad, skip_grad])

    def exchange(kept, sent, shared, axis, mask, *others):
        got = flip(jnp.concatenate([sent.reshape(-1, n2), shared], axis=0), axis, mask)
        got = after(got, *others)
        count = got.shape[0] - shared.shape[0]
        return kept + got[:count].reshape(kept.shape), shared + got[count:]

    by_core = pick(core, state_part[:, :, ::-1], state_part)
    state, both = exchange(by_core[:, :, 0], by_core[:, :, 1], both, "tensor", 1, u02)
    by_y = pick(y, state[:, ::-1], state)
    sent_x = x.advance(by_y)
    state, both = exchange(by_y[:, 0], by_y[:, 1], both, "tensor", 2, sent_x)
    state = state.reshape(peers * own_rows, n2)
    shared = jnp.concatenate([both, only], axis=0)
    out_sum, z_sum = out.finish(state), z.finish(state)
    tie = ()
    for bit in range(bits_of(peers)):
        half = state.shape[0] // 2
        state, shared = exchange(state[:half], state[half:], shared, "dp", 1 << bit, *tie)
        if bit == 0:
            tie = (x.advance(state),)
        elif bit == 1:
            tie = ()
    state_proj_grad = state
    both_rows = both.shape[0]
    both = shared[:both_rows].reshape(-1)
    only = shared[both_rows:].reshape(-1)

    f_sum = f02[:rows].astype(f32) + f_other.astype(f32)
    layer_out = masked(r1_0 + f_sum, 0).astype(bf16)
    layer_out = move_blocks(layer_out, me, peers, True)[:, None]
    x_sum = x.finish()
    e_one = (u02[:rows].astype(f32) + u_other.astype(f32)) * gain_pair[0]
    x_own = x0.astype(f32)
    rho_own = rho_of(x_own)
    n_own = x_own * rho_own
    inner = jnp.mean(e_one * n_own, axis=-1, keepdims=True)
    in_grad = g_r1_0 + rho_own * (e_one - n_own * inner)
    in_grad = move_blocks(in_grad.astype(bf16), me, peers, True)[:, None]

    conv_state_sum = both[: conv_state.size * peers * ranks].reshape(conv_shared.shape)
    gain_sum = both[conv_shared.size : conv_shared.size + 2 * width].reshape(2, width)
    member = me * ranks + rank
    conv_state_grad = lax.dynamic_slice_in_dim(conv_state_sum, member * taps_own, taps_own, 1)
    norm_gains_grad = lax.dynamic_slice_in_dim(gain_sum, member * gains_own, gains_own, 1)
    cut = conv_taps_grad.size
    conv_mamba_grad = only[:cut].reshape(conv_taps_grad.shape)
    step_bias_grad = only[cut : cut + heads]
    decay_log_grad = only[cut + heads : cut + 2 * heads]
    skip_gain_grad = only[cut + 2 * heads : cut + 3 * heads]

    return (
        layer_out,
        in_grad,
        x_sum[:, :chans],
        z_sum[:, :chans],
        x_sum[:, chans : chans + heads],
        z_sum[:, chans : chans + q_cols],
        z_sum[:, chans + q_cols : chans + q_cols + k_cols],
        z_sum[:, chans + q_cols + k_cols :],
        out_sum[:, :chans].T,
        out_sum[:, chans:].T,
        gu_sum[:, :ff],
        gu_sum[:, ff:],
        dn_sum.T,
        state_proj_grad,
        conv_state_grad,
        norm_gains_grad,
        conv_mamba_grad,
        step_bias_grad,
        decay_log_grad,
        skip_gain_grad,
    )


def solution(mesh):
    in_specs = (
        P("tensor", "dp", None),
        P("tensor", "dp", None),
        P("dp"),
        P("dp", "tensor"),
        P("dp", "tensor"),
        P("dp", "tensor"),
        P("dp", "tensor"),
        P("dp", "tensor"),
        P("dp", "tensor"),
        P("tensor", "dp"),
        P("tensor", "dp"),
        P("dp", "tensor"),
        P("dp", "tensor"),
        P("tensor", "dp"),
        P(("dp", "tensor"), None),
        P(None, ("dp", "tensor")),
        P(None, ("dp", "tensor")),
        P(None, "tensor"),
        P("tensor"),
        P("tensor"),
        P("tensor"),
    )
    out_specs = (
        P("tensor", "dp", None),
        P("tensor", "dp", None),
        P("dp", "tensor"),
        P("dp", "tensor"),
        P("dp", "tensor"),
        P("dp", "tensor"),
        P("dp", "tensor"),
        P("dp", "tensor"),
        P("tensor", "dp"),
        P("tensor", "dp"),
        P("dp", "tensor"),
        P("dp", "tensor"),
        P("tensor", "dp"),
        P(("dp", "tensor"), None),
        P(None, ("dp", "tensor")),
        P(None, ("dp", "tensor")),
        P(None, "tensor"),
        P("tensor"),
        P("tensor"),
        P("tensor"),
    )
    return jax.shard_map(body, mesh=mesh, in_specs=in_specs, out_specs=out_specs, check_vma=False)
```

```python
import functools

import jax
import jax.numpy as jnp
from jax import lax
from jax.experimental import pallas as pl
from jax.experimental.pallas import tpu as pltpu
from jax.sharding import PartitionSpec as P

epsilon = 1e-05
rotary_base = 100000000000.0
HIGHEST = lax.Precision.HIGHEST
bf16 = jnp.bfloat16
f32 = jnp.float32


def flip(value, axis, mask):
    size = lax.axis_size(axis)
    return lax.ppermute(value, axis, [(i, i ^ mask) for i in range(size)])


def bits_of(size):
    bits = size.bit_length() - 1
    assert size == 1 << bits
    return bits


def relative_order(size):
    order = [0]
    for bit in reversed(range(bits_of(size))):
        order = order + [k | (1 << bit) for k in order]
    return order


def join_quarters(quarters):
    count = quarters[0][0].shape[0]
    return jnp.concatenate(
        [item[k * count : (k + 1) * count] for item, k in quarters], axis=0
    )


def quarter_specs(quarters):
    count, cols = quarters[0][0].shape
    return [
        pl.BlockSpec((count, cols), lambda i, r, block=block: (block, 0)) for _, block in quarters
    ]


def arrays_of(quarters):
    return [array for array, _ in quarters]


class Gather:
    def __init__(self, own, axis, swap, split=False):
        self.axis, self.swap, self.split = axis, swap, split
        order = list(reversed(range(bits_of(lax.axis_size(axis)))))
        if swap:
            order[-2:] = [0, 1]
        self.order, self.held = order, own
        self.send()

    def send(self):
        self.got = flip(self.held, self.axis, 1 << self.order[0])
        if self.split and len(self.order) == 2:
            self.cross = flip(self.held, self.axis, 1 << self.order[1])

    def advance(self, *others):
        got = after(self.got, *others) if others else self.got
        left = len(self.order)
        self.order = self.order[1:]
        if left > 2:
            self.held = jnp.concatenate([self.held, got], axis=0)
            self.send()
            return self.held
        if left == 2:
            self.near = got
            sent = got if self.split else jnp.concatenate([self.held, got], axis=0)
            self.got = flip(sent, self.axis, 1 << self.order[0])
            return sent
        cross, last = ((self.cross, 0), (got, 0)) if self.split else ((got, 0), (got, 1))
        one, two = (cross, (self.near, 0)) if self.swap else ((self.near, 0), cross)
        return [(self.held, 0), one, two, last]

    def until(self, left, *others):
        while len(self.order) > left:
            both = self.advance(*others)
        return both


class Sum:
    def __init__(self, kept, sent, axis, swap):
        order = list(range(bits_of(lax.axis_size(axis))))
        if swap:
            order[:2] = [1, 0]
        self.order, self.kept, self.axis = order, kept, axis
        self.got = flip(sent, axis, 1 << order[0])

    def advance(self, *others):
        got = after(self.got, *others) if others else self.got
        self.order = self.order[1:]
        if not self.order:
            return self.kept + got.astype(f32)
        half = got.shape[0] // 2
        sent = (self.kept[half:] + got[half:].astype(f32)).astype(bf16)
        self.kept = self.kept[:half] + got[:half].astype(f32)
        self.got = flip(sent, self.axis, 1 << self.order[0])
        return sent

    def finish(self, *others):
        while self.order:
            total = self.advance(*others)
        return total


def product_kernel(groups, rank, *refs):
    kept, sent = refs[-2:]
    step = pl.program_id(0)
    first, at = 0, 0
    for pairs, widths in groups:
        per = 1 + len(widths)
        for j, width in enumerate(widths):
            total = 0.0
            for p in range(pairs):
                left, right = refs[first + p * per], refs[first + p * per + 1 + j]
                total = total + dot_tn(left[...], right[...])
            cols = slice(at, at + width)
            at += width

            @pl.when(step < 2)
            def _(total=total, cols=cols):
                sent[:, cols] = total.astype(bf16)

            @pl.when(step >= 2)
            def _(total=total, cols=cols):
                kept[:, cols] = total

        first += pairs * per


def product(token, groups, swap):
    width = groups[0][0][0].shape[1]
    quarter = width // 4

    def place(i):
        return (2 * i + 1) % 5 if swap else (i + 2) % 4

    specs, operands, shapes, total, flops = [], [], [], 0, 0
    for pairs in groups:
        widths = [array.shape[1] for array, _ in pairs[0][1]]
        shapes.append((len(pairs), widths))
        total += sum(widths)
        for left, rights in pairs:
            lines = left.shape[0]
            flops += 2 * lines * width * sum(widths)
            specs.append(pl.BlockSpec((lines, quarter), lambda i, r: (0, place(i))))
            operands.append(left)
            for array, block in rights:
                specs.append(
                    pl.BlockSpec((lines, array.shape[1]), lambda i, r, block=block: (block, 0))
                )
                operands.append(array)
    return pl.pallas_call(
        functools.partial(product_kernel, shapes),
        grid_spec=pltpu.PrefetchScalarGridSpec(
            num_scalar_prefetch=1,
            grid=(4,),
            in_specs=specs,
            out_specs=[
                pl.BlockSpec((quarter, total), lambda i, r: (jnp.maximum(i - 2, 0), 0)),
                pl.BlockSpec((quarter, total), lambda i, r: (jnp.minimum(i, 1), 0)),
            ],
        ),
        out_shape=[
            jax.ShapeDtypeStruct((2 * quarter, total), f32),
            jax.ShapeDtypeStruct((2 * quarter, total), bf16),
        ],
        cost_estimate=cost(flops, 8 * width * total, 0),
        name="weight_product",
    )(token, *operands)


def pack_kernel(chans, x, step, z, q, k, v, pack_x, pack_z):
    pack_x[:, :chans] = x[...].astype(bf16)
    pack_x[:, chans:] = jnp.zeros((x.shape[0], 128), bf16)
    pack_x[:, chans : chans + step.shape[1]] = step[...].astype(bf16)
    pack_z[:, :chans] = z[...].astype(bf16)
    pack_z[:, chans : chans + q.shape[1]] = q[...].astype(bf16)
    both = jnp.concatenate([k[...], v[...]], axis=1)
    pack_z[:, chans + q.shape[1] :] = both.astype(bf16)


def pack_early(x, step, z, q, k, v):
    lines, chans = x.shape
    cols = chans + q.shape[1] + k.shape[1] + v.shape[1]
    return pl.pallas_call(
        functools.partial(pack_kernel, chans),
        out_shape=[
            jax.ShapeDtypeStruct((lines, chans + 128), bf16),
            jax.ShapeDtypeStruct((lines, cols), bf16),
        ],
        cost_estimate=cost(0, lines * 7000, 0),
        name="pack_weights",
    )(x, step, z, q, k, v)


def move_kernel(back, order, me, source, target):
    width = source.shape[1] // len(order)
    for p, k in enumerate(order):
        there = pl.ds(pl.multiple_of((me[0] ^ k) * width, width), width)
        here = slice(p * width, (p + 1) * width)
        if back:
            target[:, there] = source[:, here]
        else:
            target[:, here] = source[:, there]


def final_kernel(order, me, u_own, u_other, gain, source, g_r1, target):
    width = source.shape[1] // len(order)
    step = 32
    for i in range(source.shape[0] // step):
        rows = slice(i * step, (i + 1) * step)
        x = source[rows].astype(f32)
        e = (u_own[rows].astype(f32) + u_other[rows].astype(f32)) * gain[...]
        rho = lax.rsqrt(jnp.mean(x * x, axis=1, keepdims=True) + epsilon)
        n = x * rho
        inner = jnp.mean(e * n, axis=1, keepdims=True)
        out = (g_r1[rows] + rho * (e - n * inner)).astype(bf16)
        for p, k in enumerate(order):
            there = pl.ds(pl.multiple_of((me[0] ^ k) * width, width), width)
            target[rows, there] = out[:, p * width : (p + 1) * width]


def final_gradient(member, size, u02, u_other, gain, x02, g_r1):
    shape = u_other.shape
    moved = shape[1] // size % 128 == 0
    result = pl.pallas_call(
        functools.partial(final_kernel, relative_order(size) if moved else [0]),
        grid_spec=pltpu.PrefetchScalarGridSpec(
            num_scalar_prefetch=1,
            grid=(1,),
            in_specs=[whole(shape), whole(shape), whole((1, shape[1])), whole(shape), whole(shape)],
            out_specs=whole(shape),
        ),
        out_shape=jax.ShapeDtypeStruct(shape, bf16),
        cost_estimate=cost(10**7, 10**7, 0),
        name="input_gradient",
    )(
        member.reshape(1) if moved else jnp.zeros((1,), jnp.int32),
        u02, u_other, gain.reshape(1, -1), x02, g_r1,
    )
    return result if moved else take_blocks(result, member, size, True)


def move_blocks(value, member, size, back):
    width = value.shape[1] // size
    if width % 128 == 0:
        return pl.pallas_call(
            functools.partial(move_kernel, back, relative_order(size)),
            grid_spec=pltpu.PrefetchScalarGridSpec(
                num_scalar_prefetch=1,
                grid=(1,),
                in_specs=[whole(value.shape)],
                out_specs=whole(value.shape),
            ),
            out_shape=jax.ShapeDtypeStruct(value.shape, value.dtype),
            cost_estimate=cost(0, 2 * value.size * value.dtype.itemsize, 0),
            name="move_blocks",
        )(member.reshape(1), value)
    return take_blocks(value, member, size, back)


def take_blocks(value, member, size, back):
    order = relative_order(size)
    where = [0] * size
    for p, k in enumerate(order):
        where[k] = p
    if back:
        index = jnp.array(where, jnp.int32)[member ^ jnp.arange(size, dtype=jnp.int32)]
    else:
        index = member ^ jnp.array(order, jnp.int32)
    cut = value.reshape(value.shape[0], size, -1)
    return jnp.take(cut, index, axis=1).reshape(value.shape)


def pick(bit, one, zero):
    return jnp.where(bit == 1, one, zero)


def after(value, *others):
    return lax.optimization_barrier((value,) + others)[0]


def flip_core(value):
    return flip(value, "tensor", 1)


def flip_y(value):
    return flip(value, "tensor", 2)


def in_rank_order(own, y, core):
    other = flip_y(own)
    pair = jnp.stack([pick(y, other, own), pick(y, own, other)])
    other = flip_core(pair)
    both = jnp.stack([pick(core, other, pair), pick(core, pair, other)], axis=1)
    return both.reshape((4,) + own.shape)


def add_low(kept, got):
    return lax.optimization_barrier((kept.astype(f32) + got.astype(f32)).astype(bf16))


def core_sum(kept, sent):
    return add_low(kept, flip_core(sent.astype(bf16)))


def y_sum(kept, sent):
    return kept.astype(f32) + flip_y(sent).astype(f32)


CHUNK = 128
HEAD = 64
TAPS = 4


def dot_nn(a, b):
    return lax.dot_general(a, b, (((1,), (0,)), ((), ())), preferred_element_type=f32)


def dot_nt(a, b):
    return lax.dot_general(a, b, (((1,), (1,)), ((), ())), preferred_element_type=f32)


def dot_tn(a, b):
    return lax.dot_general(a, b, (((0,), (0,)), ((), ())), preferred_element_type=f32)


def dot_exact(a, b):
    return lax.dot_general(
        a, b, (((1,), (0,)), ((), ())), precision=HIGHEST, preferred_element_type=f32
    )


def iota(shape, axis):
    return lax.broadcasted_iota(jnp.int32, shape, axis)


def earlier(tail, block, back):
    if back == 0:
        return block
    return pltpu.roll(jnp.concatenate([tail, block], axis=0), back, 0)[8:]


def later(block, head, ahead):
    if ahead == 0:
        return block
    both = jnp.concatenate([block, head], axis=0)
    return pltpu.roll(both, both.shape[0] - ahead, 0)[: block.shape[0]]


def conv_rows(tail, block, taps):
    total = block * taps[TAPS - 1 : TAPS] + taps[TAPS : TAPS + 1]
    for j in range(TAPS - 1):
        total = total + earlier(tail, block, TAPS - 1 - j) * taps[j : j + 1]
    return total


def conv_rows_back(grad, head, taps):
    total = grad * taps[TAPS - 1 : TAPS]
    for j in range(TAPS - 1):
        total = total + later(grad, head, TAPS - 1 - j) * taps[j : j + 1]
    return total


def conv_taps_back(tail, block, grad):
    rows = [
        jnp.sum(earlier(tail, block, TAPS - 1 - j) * grad, axis=0, keepdims=True)
        for j in range(TAPS)
    ]
    rows.append(jnp.sum(grad, axis=0, keepdims=True))
    rows.append(jnp.zeros((8 - len(rows), grad.shape[1]), f32))
    return jnp.concatenate(rows, axis=0)


def head_columns(columns, heads):
    rows = columns.shape[0]
    low = iota((rows, 2 * HEAD), 1) < HEAD
    return jnp.concatenate(
        [
            jnp.where(low, columns[:, h : h + 1], columns[:, h + 1 : h + 2])
            for h in range(0, heads, 2)
        ],
        axis=1,
    )


def head_sums(values, heads):
    rows = values.shape[0]
    low = iota((rows, 2 * HEAD), 1) < HEAD
    sums = []
    for pair in range(heads // 2):
        part = values[:, pair * 2 * HEAD : (pair + 1) * 2 * HEAD]
        sums.append(jnp.sum(jnp.where(low, part, 0.0), axis=1, keepdims=True))
        sums.append(jnp.sum(jnp.where(low, 0.0, part), axis=1, keepdims=True))
    return sums


def softplus(value):
    return jnp.maximum(value, 0.0) + jnp.log1p(jnp.exp(-jnp.abs(value)))


def step_rows(pdt, vec):
    size = pdt.shape[1]
    raw = pdt + vec[:, 0:1]
    dt = softplus(raw)
    rate = -jnp.exp(vec[:, 1:2])
    upper = (iota((size, size), 0) <= iota((size, size), 1)).astype(f32)
    logs = dot_exact(dt * rate, upper)
    last = logs[:, size - 1 : size]
    return raw, dt, rate, logs, jnp.exp(logs), jnp.exp(last - logs), jnp.exp(last)


def mamba_fwd_kernel(
    heads,
    rank,
    px,
    px_tail,
    pz,
    pbc,
    pbc_tail,
    pdt,
    taps,
    shared_taps,
    vec,
    om,
    kept,
    states,
    state,
):
    step = pl.program_id(0)

    @pl.when(step == 0)
    def _():
        state[...] = jnp.zeros_like(state)

    started = jnp.where(step == 0, 0.0, 1.0)
    u = conv_rows(px_tail[...] * started, px[...], taps[...])
    u = u * jax.nn.sigmoid(u)
    bc = conv_rows(pbc_tail[...] * started, pbc[...], shared_taps[...])
    bc = (bc * jax.nn.sigmoid(bc)).astype(bf16)
    half = bc.shape[1] // 2
    b_in, c_out = bc[:, :half], bc[:, half:]
    _, dt, _, logs, grow, fade, last = step_rows(pdt[...], vec[...])
    columns = jnp.transpose(jnp.concatenate([logs, grow, fade * dt, dt], axis=0))
    size = u.shape[0]
    causal = iota((size, size), 0) >= iota((size, size), 1)
    mixing = dot_nt(c_out, b_in)
    u_low = u.astype(bf16)
    low = iota((size, 2 * HEAD), 1) < HEAD
    local = []
    for pair in range(heads // 2):
        piece = u_low[:, pair * 2 * HEAD : (pair + 1) * 2 * HEAD]
        outs = []
        for h in (2 * pair, 2 * pair + 1):
            spread = jnp.where(causal, columns[:, h : h + 1] - logs[h : h + 1], -1e30)
            matrix = (mixing * jnp.exp(spread) * dt[h : h + 1]).astype(bf16)
            outs.append(dot_nn(matrix, piece))
        local.append(jnp.where(low, outs[0], outs[1]))
    before = state[...]
    states[0] = before
    carried = dot_nn(c_out, before.astype(bf16)) * head_columns(columns[:, 8:16], heads)
    skip = head_columns(jnp.transpose(jnp.broadcast_to(vec[:, 2:3], (8, size))), heads)
    total = jnp.concatenate(local, axis=1) + carried + skip * u
    z = pz[...]
    om[...] = (total * (z * jax.nn.sigmoid(z))).astype(bf16)
    kept[...] = total.astype(bf16)
    fed = (u * head_columns(columns[:, 16:24], heads)).astype(bf16)
    end = head_columns(jnp.transpose(jnp.broadcast_to(last, (8, 128))), heads)[:1]
    state[...] = before * end + dot_tn(b_in, fed)


def mamba_bwd_kernel(
    heads,
    rank,
    px,
    px_tail,
    pz,
    pbc,
    pbc_tail,
    pdt,
    taps,
    shared_taps,
    vec,
    states,
    gym,
    g_pxs,
    g_pbc,
    g_taps,
    g_shared,
    g_vec,
    g_skip,
    d_state,
    next_px,
    next_bc,
):
    step = pl.program_id(0)
    steps = pl.num_programs(0)

    @pl.when(step == 0)
    def _():
        d_state[...] = jnp.zeros_like(d_state)
        next_px[...] = jnp.zeros_like(next_px)
        next_bc[...] = jnp.zeros_like(next_bc)
        g_taps[...] = jnp.zeros_like(g_taps)
        g_shared[...] = jnp.zeros_like(g_shared)
        g_vec[...] = jnp.zeros_like(g_vec)
        g_skip[...] = jnp.zeros_like(g_skip)

    started = jnp.where(step == steps - 1, 0.0, 1.0)
    size = px.shape[0]
    tail_x = px_tail[...] * started
    block_x = px[...]
    pre_u = conv_rows(tail_x, block_x, taps[...])
    sig_u = jax.nn.sigmoid(pre_u)
    u = pre_u * sig_u
    tail_bc = pbc_tail[...] * started
    block_bc = pbc[...]
    pre_bc = conv_rows(tail_bc, block_bc, shared_taps[...])
    sig_bc = jax.nn.sigmoid(pre_bc)
    bc = (pre_bc * sig_bc).astype(bf16)
    half = bc.shape[1] // 2
    b_in, c_out = bc[:, :half], bc[:, half:]
    raw, dt, rate, logs, grow, fade, last = step_rows(pdt[...], vec[...])
    columns = jnp.transpose(jnp.concatenate([logs, grow, fade, dt], axis=0))
    z = pz[...]
    sig_z = jax.nn.sigmoid(z)
    g = gym[...]
    dy = g * (z * sig_z)
    dy_low = dy.astype(bf16)
    u_low = u.astype(bf16)
    before = states[0]
    before_low = before.astype(bf16)
    d_after = d_state[...]
    d_after_low = d_after.astype(bf16)
    causal = iota((size, size), 0) <= iota((size, size), 1)
    mixing = dot_nt(b_in, c_out)
    low = iota((size, 2 * HEAD), 1) < HEAD
    d_mixing = jnp.zeros((size, size), f32)
    du_local, col_sums, row_sums = [], [], []
    for pair in range(heads // 2):
        lanes = slice(pair * 2 * HEAD, (pair + 1) * 2 * HEAD)
        u_piece, dy_piece = u_low[:, lanes], dy_low[:, lanes]
        outs = []
        for h in (2 * pair, 2 * pair + 1):
            dt_col = columns[:, 24 + h : 25 + h]
            spread = jnp.where(causal, logs[h : h + 1] - columns[:, h : h + 1], -1e30)
            decay = jnp.exp(spread)
            keep = low if h % 2 == 0 else jnp.logical_not(low)
            masked = jnp.where(keep, u_piece, jnp.zeros_like(u_piece))
            product = dot_nt(masked, dy_piece) * decay
            d_mixing = d_mixing + product * dt_col
            product = product * mixing
            col_sums.append(jnp.sum(product, axis=1, keepdims=True))
            row_sums.append(jnp.sum(product * dt_col, axis=0, keepdims=True))
            outs.append(dot_nn((mixing * decay).astype(bf16), dy_piece))
        du_local.append(jnp.where(low, outs[0], outs[1]))
    grow_all = head_columns(columns[:, 8:16], heads)
    fade_all = head_columns(columns[:, 16:24], heads)
    dt_all = head_columns(columns[:, 24:32], heads)
    dy_grown = dy * grow_all
    dy_grown_low = dy_grown.astype(bf16)
    fed_low = (u * fade_all * dt_all).astype(bf16)
    back = dot_nn(b_in, d_after_low) * fade_all
    inter = head_sums(dy_grown * dot_nn(c_out, before_low), heads)
    tails = head_sums(u * back, heads)
    skip = head_columns(jnp.transpose(jnp.broadcast_to(vec[:, 2:3], (8, size))), heads)
    du = (jnp.concatenate(du_local, axis=1) + back) * dt_all + skip * dy
    d_mixing_low = d_mixing.astype(bf16)
    db = dot_nn(d_mixing_low, c_out) + dot_nt(fed_low, d_after_low)
    dc = dot_tn(d_mixing_low, b_in) + dot_nt(dy_grown_low, before_low)
    end = head_columns(jnp.transpose(jnp.broadcast_to(last, (8, 128))), heads)[:1]
    ended = d_after * end
    ends = head_sums(jnp.sum(ended * before, axis=0, keepdims=True), heads)
    d_state[...] = ended + dot_tn(c_out, dy_grown_low)
    lane = iota((size, 128), 1)
    gathered = jnp.zeros((size, 128), f32)
    for h in range(heads):
        gathered = jnp.where(lane == h, col_sums[h] + tails[h], gathered)
        gathered = jnp.where(lane == 8 + h, tails[h], gathered)
        gathered = jnp.where(lane == 16 + h, inter[h], gathered)
    turned = jnp.transpose(gathered)
    direct, tail_row, inter_row = turned[0:8], turned[8:16], turned[16:24]
    pad = [jnp.zeros((1, size), f32)] * (8 - heads)
    row_sum = jnp.concatenate(row_sums + pad, axis=0)
    zero = jnp.zeros((1, 1), f32)
    end_col = jnp.concatenate(ends + [zero] * (8 - heads), axis=0)
    d_logs = row_sum + inter_row - dt * direct
    at_last = end_col + jnp.sum(dt * tail_row, axis=1, keepdims=True)
    lower = (iota((size, size), 0) >= iota((size, size), 1)).astype(f32)
    d_rate = dot_exact(d_logs, lower) + at_last
    d_dt = direct + rate * d_rate
    d_raw = d_dt * jax.nn.sigmoid(raw)
    spread_rows = jnp.concatenate([d_raw, jnp.zeros((120, size), f32)], axis=0)
    g_pxs[:, u.shape[1] :] = jnp.transpose(spread_rows).astype(bf16)
    g_vec[0:8] += d_raw
    g_vec[8:16] += rate * dt * d_rate
    g_skip[...] += jnp.sum((dy * u).reshape(size // 8, 8, u.shape[1]), axis=0)
    d_pre = du * (sig_u * (1.0 + pre_u * (1.0 - sig_u)))
    g_pxs[:, : u.shape[1]] = conv_rows_back(d_pre, next_px[...], taps[...]).astype(bf16)
    g_taps[...] += conv_taps_back(tail_x, block_x, d_pre)
    next_px[...] = d_pre[:8]
    d_bc = jnp.concatenate([db, dc], axis=1) * (sig_bc * (1.0 + pre_bc * (1.0 - sig_bc)))
    g_pbc[...] = conv_rows_back(d_bc, next_bc[...], shared_taps[...]).astype(bf16)
    g_shared[...] += conv_taps_back(tail_bc, block_bc, d_bc)
    next_bc[...] = d_bc[:8]


def pad_rows(value):
    return jnp.pad(value, ((0, -value.shape[0] % 8), (0, 0)))


def vec_of(step_bias, decay_log, skip_gain):
    table = jnp.stack([step_bias, decay_log, skip_gain], axis=1)
    return jnp.pad(table, ((0, 8 - table.shape[0]), (0, 128 - table.shape[1])))


def whole(shape):
    return pl.BlockSpec(shape, lambda i, r: tuple(0 for _ in shape))


def cost(flops, moved, exps):
    return pl.CostEstimate(flops=flops, bytes_accessed=moved, transcendentals=exps)


def chunk_specs(length, ranks, order):
    per_block = length // ranks // CHUNK
    per = CHUNK // 8

    def place(i, r):
        c = order(i)
        return ((c // per_block) ^ r[0]) * per_block + c % per_block

    def at(cols):
        return pl.BlockSpec((CHUNK, cols), lambda i, r: (place(i, r), 0))

    def tail(cols):
        def index(i, r):
            c = jnp.maximum(order(i) - 1, 0)
            return ((((c // per_block) ^ r[0]) * per_block + c % per_block) * per + per - 1, 0)

        return pl.BlockSpec((8, cols), index)

    row = pl.BlockSpec((8, CHUNK), lambda i, r: (0, place(i, r)))
    return at, tail, row


def mamba_fwd(rank, px, pz, pbc, pdt, taps, shared_taps, vec, heads, ranks):
    length, chans = px.shape
    wide = pbc.shape[1]
    steps = length // CHUNK
    at, tail, row = chunk_specs(length, ranks, lambda i: i)
    return pl.pallas_call(
        functools.partial(mamba_fwd_kernel, heads),
        grid_spec=pltpu.PrefetchScalarGridSpec(
            num_scalar_prefetch=1,
            grid=(steps,),
            in_specs=[
                at(chans),
                tail(chans),
                at(chans),
                at(wide),
                tail(wide),
                row,
                whole((8, chans)),
                whole((8, wide)),
                whole((8, 128)),
            ],
            out_specs=[
                at(chans),
                at(chans),
                pl.BlockSpec((1, wide // 2, chans), lambda i, r: (i, 0, 0)),
            ],
            scratch_shapes=[pltpu.VMEM((wide // 2, chans), f32)],
        ),
        out_shape=[
            jax.ShapeDtypeStruct((length, chans), bf16),
            jax.ShapeDtypeStruct((length, chans), bf16),
            jax.ShapeDtypeStruct((steps, wide // 2, chans), f32),
        ],
        cost_estimate=cost(4 * 10**9, 8 * 10**6, 10**6),
        name="mamba_forward",
    )(rank, px, px, pz, pbc, pbc, pdt, taps, shared_taps, vec)


def mamba_bwd(rank, px, pz, pbc, pdt, taps, shared_taps, vec, states, gym, heads, ranks):
    length, chans = px.shape
    wide = pbc.shape[1]
    steps = length // CHUNK
    at, tail, row = chunk_specs(length, ranks, lambda i: steps - 1 - i)
    return pl.pallas_call(
        functools.partial(mamba_bwd_kernel, heads),
        grid_spec=pltpu.PrefetchScalarGridSpec(
            num_scalar_prefetch=1,
            grid=(steps,),
            in_specs=[
                at(chans),
                tail(chans),
                at(chans),
                at(wide),
                tail(wide),
                row,
                whole((8, chans)),
                whole((8, wide)),
                whole((8, 128)),
                pl.BlockSpec((1, wide // 2, chans), lambda i, r: (steps - 1 - i, 0, 0)),
                at(chans),
            ],
            out_specs=[
                at(chans + 128),
                at(wide),
                whole((8, chans)),
                whole((8, wide)),
                whole((16, 128)),
                whole((8, chans)),
            ],
            scratch_shapes=[
                pltpu.VMEM((wide // 2, chans), f32),
                pltpu.VMEM((8, chans), f32),
                pltpu.VMEM((8, wide), f32),
            ],
        ),
        out_shape=[
            jax.ShapeDtypeStruct((length, chans + 128), bf16),
            jax.ShapeDtypeStruct((length, wide), bf16),
            jax.ShapeDtypeStruct((8, chans), f32),
            jax.ShapeDtypeStruct((8, wide), f32),
            jax.ShapeDtypeStruct((16, 128), f32),
            jax.ShapeDtypeStruct((8, chans), f32),
        ],
        cost_estimate=cost(9 * 10**9, 10**7, 10**6),
        name="mamba_backward",
    )(rank, px, px, pz, pbc, pbc, pdt, taps, shared_taps, vec, states, gym)


ROWS = 256


def turn(pre, cosine, sine):
    inner = iota(pre.shape, 1) % HEAD < HEAD // 2
    lanes = pre.shape[1]
    other = jnp.where(
        inner, pltpu.roll(pre, lanes - HEAD // 2, 1), pltpu.roll(pre, HEAD // 2, 1)
    )
    return pre * cosine + other * sine


def attend_fwd_kernel(scale, rank, qkv, cosine, sine, out, q, k, v):
    length, wide = out.shape
    blocks = length // ROWS
    low = iota((ROWS, 2 * HEAD), 1) < HEAD
    load_qkv(rank, qkv, cosine, sine, q, k, v)
    for i in range(blocks):
        seen = (i + 1) * ROWS
        block = q[i * ROWS : (i + 1) * ROWS]
        keys, values = k[:seen], v[:seen]
        allowed = iota((ROWS, seen), 1) <= iota((ROWS, seen), 0) + i * ROWS
        outs = []
        for h in range(2):
            keep = low if h == 0 else jnp.logical_not(low)
            part = jnp.where(keep, block, jnp.zeros_like(block))
            scores = jnp.where(allowed, dot_nt(part, keys) * scale, -1e30)
            expo = jnp.exp(scores - jnp.max(scores, axis=1, keepdims=True))
            chance = expo * (1.0 / jnp.sum(expo, axis=1, keepdims=True))
            outs.append(dot_nn(chance.astype(bf16), values))
        out[relative_rows(rank, i)] = jnp.where(low, outs[0], outs[1]).astype(bf16)


def relative_rows(rank, i):
    return pl.ds(pl.multiple_of((i ^ rank[0]) * ROWS, ROWS), ROWS)


def load_qkv(rank, qkv, cosine, sine, q, k, v):
    wide = q.shape[1]
    for i in range(q.shape[0] // ROWS):
        rows = slice(i * ROWS, (i + 1) * ROWS)
        piece = qkv[relative_rows(rank, i)]
        q[rows] = turn(piece[:, :wide], cosine[rows], sine[rows]).astype(bf16)
        both = piece[:, wide:]
        turned = pltpu.roll(both, HEAD, 1)
        low = iota(both.shape, 1) < HEAD
        k[rows] = turn(jnp.where(low, both, turned), cosine[rows], sine[rows]).astype(bf16)
        v[rows] = jnp.where(low, turned, both).astype(bf16)


def attend_bwd_kernel(scale, rank, qkv, cosine, sine, go, g_qkv, q, k, v, dk, dv):
    length, wide = dk.shape
    blocks = length // ROWS
    low = iota((ROWS, 2 * HEAD), 1) < HEAD
    load_qkv(rank, qkv, cosine, sine, q, k, v)
    dk[...] = jnp.zeros_like(dk)
    dv[...] = jnp.zeros_like(dv)
    for i in range(blocks):
        seen = (i + 1) * ROWS
        rows = slice(i * ROWS, (i + 1) * ROWS)
        block, grads = q[rows], go[relative_rows(rank, i)]
        keys, values = k[:seen], v[:seen]
        allowed = iota((seen, ROWS), 0) <= iota((seen, ROWS), 1) + i * ROWS
        dqs, dks, dvs = [], [], []
        for h in range(2):
            keep = low if h == 0 else jnp.logical_not(low)
            part = jnp.where(keep, block, jnp.zeros_like(block))
            part_g = jnp.where(keep, grads, jnp.zeros_like(grads))
            scores = jnp.where(allowed, dot_nt(keys, part) * scale, -1e30)
            expo = jnp.exp(scores - jnp.max(scores, axis=0, keepdims=True))
            chance = expo * (1.0 / jnp.sum(expo, axis=0, keepdims=True))
            g_chance = dot_nt(values, part_g)
            center = jnp.sum(chance * g_chance, axis=0, keepdims=True)
            g_scores = (chance * (g_chance - center)).astype(bf16)
            dqs.append(dot_tn(g_scores, keys))
            dks.append(dot_nn(g_scores, part))
            dvs.append(dot_nn(chance.astype(bf16), part_g))
        dq = jnp.where(low, dqs[0], dqs[1]) * scale
        g_qkv[relative_rows(rank, i), :wide] = turn(dq, cosine[rows], -sine[rows]).astype(bf16)
        dk[:seen] += (dks[0] + dks[1]) * scale
        dv[:seen] += dvs[0] + dvs[1]
    for i in range(blocks):
        rows = slice(i * ROWS, (i + 1) * ROWS)
        g_k, g_v = dk[rows], dv[rows]
        g_k = turn(g_k + pltpu.roll(g_k, HEAD, 1), cosine[rows], -sine[rows])
        g_v = g_v + pltpu.roll(g_v, HEAD, 1)
        g_qkv[relative_rows(rank, i), wide:] = jnp.where(low, g_k, g_v).astype(bf16)


def attend_specs(length, wide):
    return [
        whole((length, 2 * wide)),
        whole((length, wide)),
        whole((length, wide)),
    ], [pltpu.VMEM((length, wide), bf16)] * 3


def attend_fwd(rank, qkv, cosine, sine):
    length, wide = cosine.shape
    ins, scratch = attend_specs(length, wide)
    return pl.pallas_call(
        functools.partial(attend_fwd_kernel, HEAD**-0.5),
        grid_spec=pltpu.PrefetchScalarGridSpec(
            num_scalar_prefetch=1,
            grid=(1,),
            in_specs=ins,
            out_specs=whole((length, wide)),
            scratch_shapes=scratch,
        ),
        out_shape=jax.ShapeDtypeStruct((length, wide), bf16),
        cost_estimate=cost(2 * 10**9, 4 * 10**6, 10**6),
        name="attend_forward",
    )(rank, qkv, cosine, sine)


def attend_bwd(rank, qkv, cosine, sine, g_oa):
    length, wide = cosine.shape
    ins, scratch = attend_specs(length, wide)
    return pl.pallas_call(
        functools.partial(attend_bwd_kernel, HEAD**-0.5),
        grid_spec=pltpu.PrefetchScalarGridSpec(
            num_scalar_prefetch=1,
            grid=(1,),
            in_specs=ins + [whole((length, wide))],
            out_specs=whole((length, 2 * wide)),
            scratch_shapes=scratch + [pltpu.VMEM((length, wide), f32)] * 2,
        ),
        out_shape=jax.ShapeDtypeStruct((length, 2 * wide), bf16),
        cost_estimate=cost(4 * 10**9, 6 * 10**6, 10**6),
        name="attend_backward",
    )(rank, qkv, cosine, sine, g_oa)


def project_kernel(order, chans, scalars, even, odd, gain, *refs):
    w_x, w_z, w_bc, outs = refs[:4], refs[4:8], refs[8], refs[9:]
    a1, kept, px, pz, pbc, pdt, qkv = outs
    rows, width = even.shape
    block = width // len(order)
    is_even = pl.program_id(0) % 2 == 0
    step = 32

    def norm(source, keep):
        for i in range(rows // step):
            own = slice(i * step, (i + 1) * step)
            value = source[own].astype(f32)
            rho = lax.rsqrt(jnp.mean(value * value, axis=1, keepdims=True) + epsilon)
            for p, k in enumerate(order):
                there = pl.ds(pl.multiple_of((scalars[0] ^ k) * block, block), block)
                here = slice(p * block, (p + 1) * block)
                piece = source[own, there]
                a1[own, here] = (piece.astype(f32) * rho * gain[:, here]).astype(bf16)
                if keep:
                    kept[own, here] = piece

    @pl.when(is_even)
    def _():
        norm(even, True)

    @pl.when(jnp.logical_not(is_even))
    def _():
        norm(odd, False)

    quarter = width // 4
    parts = [a1[:, q * quarter : (q + 1) * quarter] for q in range(4)]
    px[...] = sum(dot_nn(part, w[:, :chans]) for part, w in zip(parts, w_x))
    steps = sum(
        lax.dot_general(
            w[:, chans:], part, (((0,), (1,)), ((), ())), preferred_element_type=f32
        )
        for part, w in zip(parts, w_x)
    )
    pdt[...] = steps[:8]
    pz[...] = sum(dot_nn(part, w[:, :chans]) for part, w in zip(parts, w_z))
    pbc[...] = dot_nn(a1[...], w_bc[...])
    qkv[...] = sum(dot_nn(part, w[:, chans:]) for part, w in zip(parts, w_z))


def project(scalars, even, odd, gain, w_x, w_z, w_bc, chans, size):
    rows, width = even.shape[0] // 2, even.shape[1]
    length = 4 * rows
    if width // size % 128:
        member = scalars[0]
        even = take_blocks(even, member, size, False)
        odd = take_blocks(odd, member, size, False)
        order = [0]
    else:
        order = relative_order(size)
    if len(order) == 1:
        scalars = jnp.zeros_like(scalars)

    def at(cols):
        return pl.BlockSpec((rows, cols), lambda i, r: (i, 0))

    def half(cols):
        return pl.BlockSpec((rows, cols), lambda i, r: (i // 2, 0))

    def shape(cols, kind, count=length):
        return jax.ShapeDtypeStruct((count, cols), kind)

    n2, low = w_bc.shape[1], w_z[0][0].shape[1] - chans
    return pl.pallas_call(
        functools.partial(project_kernel, order, chans),
        grid_spec=pltpu.PrefetchScalarGridSpec(
            num_scalar_prefetch=1,
            grid=(4,),
            in_specs=[half(width), half(width), whole((1, width))]
            + quarter_specs(w_x)
            + quarter_specs(w_z)
            + [whole(w_bc.shape)],
            out_specs=[
                at(width),
                half(width),
                at(chans),
                at(chans),
                at(n2),
                pl.BlockSpec((8, rows), lambda i, r: (0, i)),
                at(low),
            ],
        ),
        out_shape=[
            shape(width, bf16),
            shape(width, bf16, 2 * rows),
            shape(chans, f32),
            shape(chans, f32),
            shape(n2, f32),
            shape(length, f32, 8),
            shape(low, f32),
        ],
        cost_estimate=cost(3 * 10**9, 14 * 10**6, length),
        name="norm_project",
    )(scalars, even, odd, gain.reshape(1, -1), *arrays_of(w_x), *arrays_of(w_z), w_bc)


def mixer_kernel(chans, rank, om, oa, *refs):
    w_o, (kept, sent) = refs[:4], refs[4:]
    total = jnp.concatenate(
        [dot_nt(om[...], w[:, :chans]) + dot_nt(oa[...], w[:, chans:]) for w in w_o], axis=1
    )

    @pl.when(pl.program_id(0) % 2 == 0)
    def _():
        kept[...] = total

    @pl.when(pl.program_id(0) % 2 == 1)
    def _():
        sent[...] = total.astype(bf16)


def mixer_out(token, om, oa, w_o):
    rows, width = om.shape[0] // 4, 4 * w_o[0][0].shape[0]

    def at(cols):
        return pl.BlockSpec((rows, cols), lambda i, r: (i, 0))

    half = pl.BlockSpec((rows, width), lambda i, r: (i // 2, 0))
    return pl.pallas_call(
        functools.partial(mixer_kernel, om.shape[1]),
        grid_spec=pltpu.PrefetchScalarGridSpec(
            num_scalar_prefetch=1,
            grid=(4,),
            in_specs=[at(om.shape[1]), at(oa.shape[1])] + quarter_specs(w_o),
            out_specs=[half, half],
        ),
        out_shape=[
            jax.ShapeDtypeStruct((2 * rows, width), f32),
            jax.ShapeDtypeStruct((2 * rows, width), bf16),
        ],
        cost_estimate=cost(10**9, 7 * 10**6, 0),
        name="mixer_out",
    )(token, om, oa, *arrays_of(w_o))


def mixer_back_kernel(chans, rank, g0, g1, g2, g3, *refs):
    w_o = refs[:4]
    pz, kept, g_ym, g_oa, g_pz, total = refs[4:]
    quarter = g0.shape[1] // 4
    for k, piece in enumerate((g0, g1, g2, g3)):

        @pl.when(pl.program_id(0) == k)
        def _(piece=piece):
            total[...] = sum(
                dot_nn(piece[:, q * quarter : (q + 1) * quarter], w_o[q][...]) for q in range(4)
            )

    back = total[:, :chans]
    g_ym[...] = back
    g_oa[...] = total[:, chans:].astype(bf16)
    z = pz[...]
    sig = jax.nn.sigmoid(z)
    g_pz[...] = (back * kept[...].astype(f32) * (sig * (1.0 + z * (1.0 - sig)))).astype(bf16)


def mixer_back(token, g_m, w_o, pz, kept):
    rows, width = g_m[0].shape
    length, chans = pz.shape
    cols_o = w_o[0][0].shape[1]
    other = cols_o - chans

    def at(cols):
        return pl.BlockSpec((rows, cols), lambda i, r: (i, 0))

    return pl.pallas_call(
        functools.partial(mixer_back_kernel, chans),
        grid_spec=pltpu.PrefetchScalarGridSpec(
            num_scalar_prefetch=1,
            grid=(4,),
            in_specs=[whole((rows, width))] * 4 + quarter_specs(w_o) + [at(chans)] * 2,
            out_specs=[at(chans), at(other), at(chans)],
            scratch_shapes=[pltpu.VMEM((rows, cols_o), f32)],
        ),
        out_shape=[
            jax.ShapeDtypeStruct((length, chans), f32),
            jax.ShapeDtypeStruct((length, other), bf16),
            jax.ShapeDtypeStruct((length, chans), bf16),
        ],
        cost_estimate=cost(10**9, 9 * 10**6, 10**6),
        name="mixer_back",
    )(token, *g_m, *arrays_of(w_o), pz, kept)


def project_back_kernel(chans, rank, a1, g_pz, g_qkv, g_pxs, g_bc, *refs):
    w_x, w_z, w_bc = refs[:4], refs[4:8], refs[8]
    kept, sent, sums = refs[9:]
    step = pl.program_id(0)
    total = jnp.concatenate(
        [
            dot_nt(g_pz[...], wz[:, :chans])
            + dot_nt(g_qkv[...], wz[:, chans:])
            + dot_nt(g_pxs[...], wx[...])
            for wx, wz in zip(w_x, w_z)
        ],
        axis=1,
    ) + dot_nt(g_bc[...], w_bc[...])

    @pl.when(step == 0)
    def _():
        sums[...] = jnp.zeros_like(sums)

    rows, width = total.shape
    weighed = total * a1[...].astype(f32)
    sums[...] += jnp.sum(weighed.reshape(rows // 8, 8, width), axis=0)

    @pl.when(step % 2 == 0)
    def _():
        kept[...] = total

    @pl.when(step % 2 == 1)
    def _():
        sent[...] = total.astype(bf16)


def project_back(token, a1, g_pz, g_qkv, g_pxs, g_bc, w_x, w_z, w_bc):
    length, width = a1.shape
    chans = g_pz.shape[1]
    rows = length // 4

    def at(cols):
        return pl.BlockSpec((rows, cols), lambda i, r: (i, 0))

    half = pl.BlockSpec((rows, width), lambda i, r: (i // 2, 0))
    parts = (a1, g_pz, g_qkv, g_pxs, g_bc)
    return pl.pallas_call(
        functools.partial(project_back_kernel, chans),
        grid_spec=pltpu.PrefetchScalarGridSpec(
            num_scalar_prefetch=1,
            grid=(4,),
            in_specs=[at(item.shape[1]) for item in parts]
            + quarter_specs(w_x)
            + quarter_specs(w_z)
            + [whole(w_bc.shape)],
            out_specs=[half, half, whole((8, width))],
        ),
        out_shape=[
            jax.ShapeDtypeStruct((2 * rows, width), f32),
            jax.ShapeDtypeStruct((2 * rows, width), bf16),
            jax.ShapeDtypeStruct((8, width), f32),
        ],
        cost_estimate=cost(3 * 10**9, 11 * 10**6, 0),
        name="project_back",
    )(token, *parts, *arrays_of(w_x), *arrays_of(w_z), w_bc)


def rotary_tables(length):
    half = HEAD // 2
    frequency = rotary_base ** (-2.0 * jnp.arange(half, dtype=f32) / HEAD)
    angles = jnp.arange(length, dtype=f32)[:, None] * frequency[None, :]
    cosine, sine = jnp.cos(angles), jnp.sin(angles)
    return (
        jnp.concatenate([cosine] * 4, axis=1),
        jnp.concatenate([-sine, sine, -sine, sine], axis=1),
    )


def swiglu(gate_part, up_part):
    return jax.nn.silu(gate_part) * up_part


def mm(a, b):
    return jnp.dot(a, b, preferred_element_type=f32)


def mm_t(a, b):
    return lax.dot_general(a, b, (((1,), (1,)), ((), ())), preferred_element_type=f32)


def t_mm(a, b):
    return lax.dot_general(a, b, (((0,), (0,)), ((), ())), preferred_element_type=f32)


def body(
    layer_in,
    out_grad,
    lengths,
    mamba_x,
    mamba_z,
    mamba_step,
    query_proj,
    key_proj,
    value_proj,
    mamba_out,
    attend_out,
    mlp_gate,
    mlp_up,
    mlp_down,
    state_proj,
    conv_state,
    norm_gains,
    conv_mamba,
    step_bias,
    decay_log,
    skip_gain,
):
    ranks = lax.axis_size("tensor")
    assert ranks == 4 and layer_in.shape[1] == 1
    rank = lax.axis_index("tensor")
    y, core = rank // 2, rank % 2
    rank_ref = rank.reshape(1)
    peers = lax.axis_size("dp")
    me = lax.axis_index("dp")
    rows, _, width = layer_in.shape
    length = rows * ranks
    chans = mamba_x.shape[1]
    heads = step_bias.shape[0]
    q_cols, k_cols = query_proj.shape[1], key_proj.shape[1]
    ff = mlp_gate.shape[1]
    own_rows, n2 = state_proj.shape

    raw_0 = layer_in[:, 0]
    raw_even = jnp.concatenate([raw_0, flip_y(raw_0)], axis=0)
    raw_odd = flip_core(raw_even)

    pack_x, pack_z = pack_early(
        mamba_x, mamba_step, mamba_z, query_proj, key_proj, value_proj
    )
    first = Gather(pack_x, "dp", False)
    second = Gather(pack_z, "dp", True)
    small = jnp.concatenate([conv_state.reshape(-1), norm_gains.reshape(-1)])
    parts = []
    rest = small
    for _ in range(3):
        parts.append(lax.reduce_precision(rest, 8, 7))
        rest = rest - parts[-1]
    parts = jnp.concatenate(parts)
    small_rows = -(-parts.shape[0] // n2)
    parts = jnp.pad(parts, (0, small_rows * n2 - parts.shape[0])).reshape(small_rows, n2)
    pack_s = jnp.concatenate([state_proj, parts], axis=0).astype(bf16)
    pack_o = jnp.concatenate([mamba_out.T.astype(bf16), attend_out.T.astype(bf16)], axis=1)
    pack_m = jnp.concatenate(
        [mlp_gate.astype(bf16), mlp_up.astype(bf16), mlp_down.T.astype(bf16)], axis=1
    )
    ranked = in_rank_order(pack_s, y, core)
    third = Gather(ranked.reshape(-1, n2), "dp", False)
    sent_x = first.until(2)
    sent_z = second.until(2)
    third.until(2, sent_x, sent_z)
    far_x = first.advance()
    far_z = second.advance()
    third.advance(far_x, far_z)
    gather_m = Gather(after(pack_m, far_x, far_z), "dp", False, True)
    w_x = first.advance()
    gather_o = Gather(after(pack_o, arrays_of(w_x)[2]), "dp", True)
    w_z = second.advance()
    all_s = join_quarters(third.advance()).reshape(peers, ranks, own_rows + small_rows, n2)
    w_bc = all_s[:, :, :own_rows].reshape(width, n2)
    parts = all_s[:, :, own_rows:].reshape(peers, ranks, -1).astype(f32)
    count = small.shape[0]
    small = parts[..., :count] + parts[..., count : 2 * count] + parts[..., 2 * count : 3 * count]
    cut = conv_state.size
    taps_own = conv_state.shape[1]
    gains_own = norm_gains.shape[1]
    taps_rel = small[..., :cut].reshape(peers, ranks, conv_state.shape[0], taps_own)
    taps_rel = jnp.transpose(taps_rel, (2, 0, 1, 3)).reshape(conv_state.shape[0], -1)
    conv_shared = take_blocks(taps_rel, me, peers, True)
    gain_pair = jnp.transpose(
        small[..., cut:].reshape(peers, ranks, 2, gains_own), (2, 0, 1, 3)
    ).reshape(2, width)

    def rho_of(values):
        return lax.rsqrt(jnp.mean(values * values, axis=-1, keepdims=True) + epsilon)

    a1, x02, px, pz, pbc, pdt, qkv = project(
        me.reshape(1), raw_even, raw_odd, gain_pair[0], w_x, w_z, w_bc, chans, peers
    )
    x0, x2 = x02[:rows], x02[rows:]

    limit = lengths[0]

    def masked(block, k):
        place = (rank ^ k) * rows + jnp.arange(rows, dtype=jnp.int32)
        return jnp.where((place < limit)[:, None], block, jnp.zeros_like(block))

    gf0 = masked(move_blocks(after(out_grad, far_x, far_z)[:, 0], me, peers, False), 0)
    gf2 = flip_y(after(gf0, raw_even))

    sent_m = gather_m.until(2, pdt)
    sent_o = gather_o.until(2, pdt)
    cosine, sine = rotary_tables(length)
    oa = attend_fwd(after(rank_ref, sent_o, sent_m), qkv, cosine, sine)
    gf_odd = flip_core(jnp.concatenate([gf0, after(gf2, pdt)], axis=0))
    sent_o = gather_o.advance(oa)
    vec = vec_of(step_bias, decay_log, skip_gain)
    taps, shared_taps = pad_rows(conv_mamba), pad_rows(conv_shared)
    gf_odd = after(gf_odd, oa)
    om, kept, states = mamba_fwd(
        after(rank_ref, sent_o, gf_odd), px, pz, pbc, pdt, taps, shared_taps, vec, heads, ranks
    )
    w_o = gather_o.advance(om)
    gf1, gf3 = gf_odd[:rows], gf_odd[rows:]
    gf_a = jnp.concatenate([gf0, gf1], axis=0)
    gf_b = jnp.concatenate([gf2, gf3], axis=0)
    sent_m = gather_m.advance(om)
    m_kept, m_sent = mixer_out(after(rank_ref, sent_m, gather_m.cross), om, oa, w_o)
    s02 = add_low(m_kept, flip_core(m_sent))
    s0, s2 = s02[:rows], s02[rows:]
    w_m = gather_m.advance()
    m_got = after(flip_y(s2), *arrays_of(w_m))
    w_m = join_quarters(w_m)
    w_gu, w_dn = w_m[:, : 2 * ff], w_m[:, 2 * ff :]

    def second_norm(low_x, m):
        r1 = low_x.astype(f32) + m
        rho = rho_of(r1)
        return r1, rho, (r1 * rho * gain_pair[1]).astype(bf16)

    r1_0, rho_0, a2_0 = second_norm(x0, s0.astype(f32) + m_got.astype(f32))
    a2_1 = flip_core(a2_0)
    a2_a = jnp.concatenate([a2_0, a2_1], axis=0)
    r1_2, rho_2, a2_2 = second_norm(x2, y_sum(s2, s0))
    a2_3 = flip_core(a2_2)
    a2_b = jnp.concatenate([a2_2, a2_3], axis=0)

    def feed(a2, gf, *others):
        gate_up = mm(a2, w_gu)
        gate, up = gate_up[:, :ff], gate_up[:, ff:]
        hidden, glu_back = jax.vjp(swiglu, gate, up)
        hid = hidden.astype(bf16)
        gate_grad, up_grad = glu_back(mm(gf, w_dn))
        g_gu = jnp.concatenate([gate_grad.astype(bf16), up_grad.astype(bf16)], axis=1)
        if others:
            g_gu = after(g_gu, *others)
        return hid, g_gu, mm_t(g_gu, w_gu)

    hid_a, g_gu_a, g_a2_a = feed(a2_a, gf_a)
    t0 = core_sum(g_a2_a[:rows], g_a2_a[rows:])
    hid_b, g_gu_b, g_a2_b = feed(a2_b, gf_b, t0)
    t2 = core_sum(g_a2_b[:rows], g_a2_b[rows:])

    halves = ((0, 0), (0, 1), (1, 0), (1, 1))
    dn_kept, dn_sent = product(
        after(rank_ref, g_a2_b),
        [[(left, [((hid_a, hid_b)[p], b)]) for left, (p, b) in zip((gf0, gf1, gf2, gf3), halves)]],
        True,
    )
    dn = Sum(dn_kept, dn_sent, "dp", True)
    gu_kept, gu_sent = product(
        after(rank_ref, dn_sent),
        [
            [
                (left, [((g_gu_a, g_gu_b)[p], b)])
                for left, (p, b) in zip((a2_0, a2_1, a2_2, a2_3), halves)
            ]
        ],
        False,
    )
    gu = Sum(gu_kept, gu_sent, "dp", False)

    def second_back(g_a2, r1, rho, gf):
        n_two = r1 * rho
        e_two = g_a2 * gain_pair[1]
        inner = jnp.mean(e_two * n_two, axis=-1, keepdims=True)
        return gf.astype(f32) + rho * (e_two - n_two * inner)

    t0_got, t2_got = flip_y(t0), flip_y(t2)
    g_a2_2 = t2.astype(f32) + after(t0_got, t2, gu_sent).astype(f32)
    g_r1_2 = second_back(g_a2_2, r1_2, rho_2, gf2)
    g_m_2 = g_r1_2.astype(bf16)
    g_a2_0 = t0.astype(f32) + after(t2_got, gu_sent).astype(f32)
    g_r1_0 = second_back(g_a2_0, r1_0, rho_0, gf0)
    g_m_0 = g_r1_0.astype(bf16)
    gain_two_grad = jnp.sum(g_a2_0 * (r1_0 * rho_0), axis=0)
    g_m_3, g_m_1 = flip_core(g_m_2), flip_core(g_m_0)
    g_m = (g_m_0, g_m_1, g_m_2, g_m_3)
    g_ym, g_oa, g_pz = mixer_back(after(rank_ref, dn_sent, gu_sent), g_m, w_o, pz, kept)

    sent_dn = dn.advance(g_oa)
    hid_a, hid_b = lax.optimization_barrier((hid_a, hid_b, g_m_0))[:2]
    f_a, f_b = mm_t(hid_a, w_dn), mm_t(hid_b, w_dn)
    f_sent = jnp.concatenate([f_a[rows:], f_b[rows:]], axis=0).astype(bf16)
    f_got = flip_core(f_sent)
    g_qkv = attend_bwd(after(rank_ref, sent_dn, f_sent), qkv, cosine, sine, g_oa)
    sent_dn = dn.advance(g_qkv)
    sent_gu = gu.advance(g_qkv)
    f_kept = jnp.concatenate([f_a[:rows], f_b[:rows]], axis=0)
    f02 = add_low(f_kept, after(f_got, g_qkv))
    f_other = flip_y(f02[rows:])
    z_kept, z_sent = product(
        after(rank_ref, sent_dn, sent_gu, f02),
        [[(g_m[k], [(om, k), (oa, k)]) for k in range(4)], [(a1, [(g_pz, 0), (g_qkv, 0)])]],
        False,
    )
    z = Sum(z_kept, z_sent, "dp", False)
    sent_gu = gu.advance(z_sent)

    g_pxs, g_bc, g_taps, g_shared, g_vec, g_skip = mamba_bwd(
        after(rank_ref, z_sent, sent_gu),
        px, pz, pbc, pdt, taps, shared_taps, vec, states, g_ym, heads, ranks,
    )
    dn_sum, gu_sum = dn.finish(g_pxs), gu.finish(g_pxs)
    x_kept, x_sent = product(
        after(rank_ref, dn_sum, gu_sum), [[(a1, [(g_pxs, 0)])]], False
    )
    x = Sum(x_kept, x_sent, "dp", False)
    sent_z = z.advance(x_sent)
    g_kept, g_sent, g_sums = project_back(
        after(rank_ref, x_sent, sent_z), a1, g_pz, g_qkv, g_pxs, g_bc, w_x, w_z, w_bc
    )
    g_got = flip_core(g_sent)
    sent_x = x.advance(g_sums)
    sent_z = z.advance(g_sums)
    u02 = add_low(g_kept, after(g_got, sent_x, sent_z))
    u_other = flip_y(u02[rows:])
    gain_one_grad = jnp.sum(g_sums, axis=0) / gain_pair[0]
    state_part = t_mm(after(a1, x_sent), g_bc).reshape(peers, 2, 2, own_rows, n2)
    f_other = after(f_other, u02)

    g_taps, g_shared, g_vec, g_skip = lax.optimization_barrier(
        (g_taps, g_shared, g_vec, g_skip, g_sums)
    )[:4]
    conv_taps_grad = g_taps[: conv_mamba.shape[0]]
    conv_shared_grad = g_shared[: conv_state.shape[0]]
    bias_grad = jnp.sum(g_vec[:heads], axis=1)
    decay_grad = jnp.sum(g_vec[8 : 8 + heads], axis=1)
    skip_grad = jnp.sum(g_skip.reshape(8, heads, HEAD), axis=(0, 2))
    gain_grads = take_blocks(jnp.stack([gain_one_grad, gain_two_grad]), me, peers, True)

    def rows_of(items):
        flat = jnp.concatenate([item.reshape(-1) for item in items])
        return jnp.pad(flat, (0, -flat.shape[0] % (8 * n2))).reshape(-1, n2)

    both = rows_of([conv_shared_grad, gain_grads])
    only = rows_of([conv_taps_grad, bias_grad, decay_grad, skip_grad])

    def exchange(kept, sent, shared, axis, mask, *others):
        got = flip(jnp.concatenate([sent.reshape(-1, n2), shared], axis=0), axis, mask)
        got = after(got, *others)
        count = got.shape[0] - shared.shape[0]
        return kept + got[:count].reshape(kept.shape), shared + got[count:]

    by_core = pick(core, state_part[:, :, ::-1], state_part)
    state, both = exchange(by_core[:, :, 0], by_core[:, :, 1], both, "tensor", 1, u02)
    by_y = pick(y, state[:, ::-1], state)
    sent_x = x.advance(by_y)
    state, both = exchange(by_y[:, 0], by_y[:, 1], both, "tensor", 2, sent_x, sent_z)
    state = state.reshape(peers * own_rows, n2)
    shared = jnp.concatenate([both, only], axis=0)
    tie = (u_other,)
    for bit in range(bits_of(peers)):
        half = state.shape[0] // 2
        state, shared = exchange(state[:half], state[half:], shared, "dp", 1 << bit, *tie)
        if bit == 0:
            both_sum = z.finish(state)
            tie = (both_sum,)
        elif bit == 1:
            tie = ()
    state_proj_grad = state
    both_rows = both.shape[0]
    both = shared[:both_rows].reshape(-1)
    only = shared[both_rows:].reshape(-1)

    f_sum = f02[:rows].astype(f32) + f_other.astype(f32)
    layer_out = masked(r1_0 + f_sum, 0).astype(bf16)
    layer_out = move_blocks(layer_out, me, peers, True)[:, None]
    x_sum = x.finish()
    out_sum, z_sum = both_sum[:, : chans + q_cols], both_sum[:, chans + q_cols :]
    in_grad = final_gradient(after(me, both_sum), peers, u02, u_other, gain_pair[0], x02, g_r1_0)[:, None]

    conv_state_sum = both[: conv_state.size * peers * ranks].reshape(conv_shared.shape)
    gain_sum = both[conv_shared.size : conv_shared.size + 2 * width].reshape(2, width)
    member = me * ranks + rank
    conv_state_grad = lax.dynamic_slice_in_dim(conv_state_sum, member * taps_own, taps_own, 1)
    norm_gains_grad = lax.dynamic_slice_in_dim(gain_sum, member * gains_own, gains_own, 1)
    cut = conv_taps_grad.size
    conv_mamba_grad = only[:cut].reshape(conv_taps_grad.shape)
    step_bias_grad = only[cut : cut + heads]
    decay_log_grad = only[cut + heads : cut + 2 * heads]
    skip_gain_grad = only[cut + 2 * heads : cut + 3 * heads]

    return (
        layer_out,
        in_grad,
        x_sum[:, :chans],
        z_sum[:, :chans],
        x_sum[:, chans : chans + heads],
        z_sum[:, chans : chans + q_cols],
        z_sum[:, chans + q_cols : chans + q_cols + k_cols],
        z_sum[:, chans + q_cols + k_cols :],
        out_sum[:, :chans].T,
        out_sum[:, chans:].T,
        gu_sum[:, :ff],
        gu_sum[:, ff:],
        dn_sum.T,
        state_proj_grad,
        conv_state_grad,
        norm_gains_grad,
        conv_mamba_grad,
        step_bias_grad,
        decay_log_grad,
        skip_gain_grad,
    )


def solution(mesh):
    in_specs = (
        P("tensor", "dp", None),
        P("tensor", "dp", None),
        P("dp"),
        P("dp", "tensor"),
        P("dp", "tensor"),
        P("dp", "tensor"),
        P("dp", "tensor"),
        P("dp", "tensor"),
        P("dp", "tensor"),
        P("tensor", "dp"),
        P("tensor", "dp"),
        P("dp", "tensor"),
        P("dp", "tensor"),
        P("tensor", "dp"),
        P(("dp", "tensor"), None),
        P(None, ("dp", "tensor")),
        P(None, ("dp", "tensor")),
        P(None, "tensor"),
        P("tensor"),
        P("tensor"),
        P("tensor"),
    )
    out_specs = (
        P("tensor", "dp", None),
        P("tensor", "dp", None),
        P("dp", "tensor"),
        P("dp", "tensor"),
        P("dp", "tensor"),
        P("dp", "tensor"),
        P("dp", "tensor"),
        P("dp", "tensor"),
        P("tensor", "dp"),
        P("tensor", "dp"),
        P("dp", "tensor"),
        P("dp", "tensor"),
        P("tensor", "dp"),
        P(("dp", "tensor"), None),
        P(None, ("dp", "tensor")),
        P(None, ("dp", "tensor")),
        P(None, "tensor"),
        P("tensor"),
        P("tensor"),
        P("tensor"),
    )
    return jax.shard_map(body, mesh=mesh, in_specs=in_specs, out_specs=out_specs, check_vma=False)
```

```python
import functools

import jax
import jax.numpy as jnp
from jax import lax
from jax.experimental import pallas as pl
from jax.experimental.pallas import tpu as pltpu
from jax.sharding import PartitionSpec as P

epsilon = 1e-05
rotary_base = 100000000000.0
HIGHEST = lax.Precision.HIGHEST
bf16 = jnp.bfloat16
f32 = jnp.float32


def flip(value, axis, mask):
    size = lax.axis_size(axis)
    return lax.ppermute(value, axis, [(i, i ^ mask) for i in range(size)])


def bits_of(size):
    bits = size.bit_length() - 1
    assert size == 1 << bits
    return bits


def relative_order(size):
    order = [0]
    for bit in reversed(range(bits_of(size))):
        order = order + [k | (1 << bit) for k in order]
    return order


def join_quarters(quarters):
    count = quarters[0][0].shape[0]
    return jnp.concatenate(
        [item[k * count : (k + 1) * count] for item, k in quarters], axis=0
    )


def quarter_specs(quarters):
    count, cols = quarters[0][0].shape
    return [
        pl.BlockSpec((count, cols), lambda i, r, block=block: (block, 0)) for _, block in quarters
    ]


def arrays_of(quarters):
    return [array for array, _ in quarters]


class Gather:
    def __init__(self, own, axis, swap, split=False):
        self.axis, self.swap, self.split = axis, swap, split
        order = list(reversed(range(bits_of(lax.axis_size(axis)))))
        if swap:
            order[-2:] = [0, 1]
        self.order, self.held = order, own
        self.send()

    def send(self):
        self.got = flip(self.held, self.axis, 1 << self.order[0])
        if self.split and len(self.order) == 2:
            self.cross = flip(self.held, self.axis, 1 << self.order[1])

    def advance(self, *others):
        got = after(self.got, *others) if others else self.got
        left = len(self.order)
        self.order = self.order[1:]
        if left > 2:
            self.held = jnp.concatenate([self.held, got], axis=0)
            self.send()
            return self.held
        if left == 2:
            self.near = got
            sent = got if self.split else jnp.concatenate([self.held, got], axis=0)
            self.got = flip(sent, self.axis, 1 << self.order[0])
            return sent
        cross, last = ((self.cross, 0), (got, 0)) if self.split else ((got, 0), (got, 1))
        one, two = (cross, (self.near, 0)) if self.swap else ((self.near, 0), cross)
        return [(self.held, 0), one, two, last]

    def until(self, left, *others):
        while len(self.order) > left:
            both = self.advance(*others)
        return both


class Sum:
    def __init__(self, kept, sent, axis, swap):
        order = list(range(bits_of(lax.axis_size(axis))))
        if swap:
            order[:2] = [1, 0]
        self.order, self.kept, self.axis = order, kept, axis
        self.got = flip(sent, axis, 1 << order[0])

    def advance(self, *others):
        got = after(self.got, *others) if others else self.got
        self.order = self.order[1:]
        if not self.order:
            return self.kept + got.astype(f32)
        half = got.shape[0] // 2
        sent = (self.kept[half:] + got[half:].astype(f32)).astype(bf16)
        self.kept = self.kept[:half] + got[:half].astype(f32)
        self.got = flip(sent, self.axis, 1 << self.order[0])
        return sent

    def finish(self, *others):
        while self.order:
            total = self.advance(*others)
        return total


def product_kernel(groups, rank, *refs):
    kept, sent = refs[-2:]
    step = pl.program_id(0)
    first, at = 0, 0
    for pairs, widths in groups:
        per = 1 + len(widths)
        for j, width in enumerate(widths):
            total = 0.0
            for p in range(pairs):
                left, right = refs[first + p * per], refs[first + p * per + 1 + j]
                total = total + dot_tn(left[...], right[...])
            cols = slice(at, at + width)
            at += width

            @pl.when(step < 2)
            def _(total=total, cols=cols):
                sent[:, cols] = total.astype(bf16)

            @pl.when(step >= 2)
            def _(total=total, cols=cols):
                kept[:, cols] = total

        first += pairs * per


def product(token, groups, swap):
    width = groups[0][0][0].shape[1]
    quarter = width // 4

    def place(i):
        return (2 * i + 1) % 5 if swap else (i + 2) % 4

    specs, operands, shapes, total, flops = [], [], [], 0, 0
    for pairs in groups:
        widths = [array.shape[1] for array, _ in pairs[0][1]]
        shapes.append((len(pairs), widths))
        total += sum(widths)
        for left, rights in pairs:
            lines = left.shape[0]
            flops += 2 * lines * width * sum(widths)
            specs.append(pl.BlockSpec((lines, quarter), lambda i, r: (0, place(i))))
            operands.append(left)
            for array, block in rights:
                specs.append(
                    pl.BlockSpec((lines, array.shape[1]), lambda i, r, block=block: (block, 0))
                )
                operands.append(array)
    return pl.pallas_call(
        functools.partial(product_kernel, shapes),
        grid_spec=pltpu.PrefetchScalarGridSpec(
            num_scalar_prefetch=1,
            grid=(4,),
            in_specs=specs,
            out_specs=[
                pl.BlockSpec((quarter, total), lambda i, r: (jnp.maximum(i - 2, 0), 0)),
                pl.BlockSpec((quarter, total), lambda i, r: (jnp.minimum(i, 1), 0)),
            ],
        ),
        out_shape=[
            jax.ShapeDtypeStruct((2 * quarter, total), f32),
            jax.ShapeDtypeStruct((2 * quarter, total), bf16),
        ],
        cost_estimate=cost(flops, 8 * width * total, 0),
        name="weight_product",
    )(token, *operands)


def pack_kernel(chans, x, step, z, q, k, v, pack_x, pack_z, turned):
    pack_x[:, :chans] = x[...].astype(bf16)
    turned[...] = jnp.zeros_like(turned)
    turned[: step.shape[0]] = step[...]
    pack_x[:, chans:] = jnp.transpose(turned[...]).astype(bf16)
    pack_z[:, :chans] = z[...].astype(bf16)
    pack_z[:, chans : chans + q.shape[1]] = q[...].astype(bf16)
    both = jnp.concatenate([k[...], v[...]], axis=0)
    pack_z[:, chans + q.shape[1] :] = jnp.transpose(both).astype(bf16)


def pack_early(x, step, z, q, k, v):
    lines, chans = x.shape
    cols = chans + q.shape[1] + k.shape[0] + v.shape[0]
    return pl.pallas_call(
        functools.partial(pack_kernel, chans),
        out_shape=[
            jax.ShapeDtypeStruct((lines, chans + 128), bf16),
            jax.ShapeDtypeStruct((lines, cols), bf16),
        ],
        scratch_shapes=[pltpu.VMEM((128, lines), f32)],
        cost_estimate=cost(0, lines * 7000, 0),
        name="pack_weights",
    )(x, step, z, q, k, v)


def move_kernel(back, order, me, source, target):
    width = source.shape[1] // len(order)
    for p, k in enumerate(order):
        there = pl.ds(pl.multiple_of((me[0] ^ k) * width, width), width)
        here = slice(p * width, (p + 1) * width)
        if back:
            target[:, there] = source[:, here]
        else:
            target[:, here] = source[:, there]


def final_kernel(order, me, u_own, u_other, gain, source, g_r1, target):
    width = source.shape[1] // len(order)
    step = 32
    for i in range(source.shape[0] // step):
        rows = slice(i * step, (i + 1) * step)
        x = source[rows].astype(f32)
        e = (u_own[rows].astype(f32) + u_other[rows].astype(f32)) * gain[...]
        rho = lax.rsqrt(jnp.mean(x * x, axis=1, keepdims=True) + epsilon)
        n = x * rho
        inner = jnp.mean(e * n, axis=1, keepdims=True)
        out = (g_r1[rows] + rho * (e - n * inner)).astype(bf16)
        for p, k in enumerate(order):
            there = pl.ds(pl.multiple_of((me[0] ^ k) * width, width), width)
            target[rows, there] = out[:, p * width : (p + 1) * width]


def final_gradient(member, size, u02, u_other, gain, x02, g_r1):
    shape = u_other.shape
    moved = shape[1] // size % 128 == 0
    result = pl.pallas_call(
        functools.partial(final_kernel, relative_order(size) if moved else [0]),
        grid_spec=pltpu.PrefetchScalarGridSpec(
            num_scalar_prefetch=1,
            grid=(1,),
            in_specs=[whole(shape), whole(shape), whole((1, shape[1])), whole(shape), whole(shape)],
            out_specs=whole(shape),
        ),
        out_shape=jax.ShapeDtypeStruct(shape, bf16),
        cost_estimate=cost(10**7, 10**7, 0),
        name="input_gradient",
    )(
        member.reshape(1) if moved else jnp.zeros((1,), jnp.int32),
        u02, u_other, gain.reshape(1, -1), x02, g_r1,
    )
    return result if moved else take_blocks(result, member, size, True)


def move_blocks(value, member, size, back):
    width = value.shape[1] // size
    if width % 128 == 0:
        return pl.pallas_call(
            functools.partial(move_kernel, back, relative_order(size)),
            grid_spec=pltpu.PrefetchScalarGridSpec(
                num_scalar_prefetch=1,
                grid=(1,),
                in_specs=[whole(value.shape)],
                out_specs=whole(value.shape),
            ),
            out_shape=jax.ShapeDtypeStruct(value.shape, value.dtype),
            cost_estimate=cost(0, 2 * value.size * value.dtype.itemsize, 0),
            name="move_blocks",
        )(member.reshape(1), value)
    return take_blocks(value, member, size, back)


def take_blocks(value, member, size, back):
    order = relative_order(size)
    where = [0] * size
    for p, k in enumerate(order):
        where[k] = p
    if back:
        index = jnp.array(where, jnp.int32)[member ^ jnp.arange(size, dtype=jnp.int32)]
    else:
        index = member ^ jnp.array(order, jnp.int32)
    cut = value.reshape(value.shape[0], size, -1)
    return jnp.take(cut, index, axis=1).reshape(value.shape)


def pick(bit, one, zero):
    return jnp.where(bit == 1, one, zero)


def after(value, *others):
    return lax.optimization_barrier((value,) + others)[0]


def flip_core(value):
    return flip(value, "tensor", 1)


def flip_y(value):
    return flip(value, "tensor", 2)


def in_rank_order(own, y, core):
    other = flip_y(own)
    pair = jnp.stack([pick(y, other, own), pick(y, own, other)])
    other = flip_core(pair)
    both = jnp.stack([pick(core, other, pair), pick(core, pair, other)], axis=1)
    return both.reshape((4,) + own.shape)


def add_low(kept, got):
    return lax.optimization_barrier((kept.astype(f32) + got.astype(f32)).astype(bf16))


def core_sum(kept, sent):
    return add_low(kept, flip_core(sent.astype(bf16)))


def y_sum(kept, sent):
    return kept.astype(f32) + flip_y(sent).astype(f32)


CHUNK = 128
HEAD = 64
TAPS = 4


def dot_nn(a, b):
    return lax.dot_general(a, b, (((1,), (0,)), ((), ())), preferred_element_type=f32)


def dot_nt(a, b):
    return lax.dot_general(a, b, (((1,), (1,)), ((), ())), preferred_element_type=f32)


def dot_tn(a, b):
    return lax.dot_general(a, b, (((0,), (0,)), ((), ())), preferred_element_type=f32)


def dot_exact(a, b):
    return lax.dot_general(
        a, b, (((1,), (0,)), ((), ())), precision=HIGHEST, preferred_element_type=f32
    )


def iota(shape, axis):
    return lax.broadcasted_iota(jnp.int32, shape, axis)


def earlier(tail, block, back):
    if back == 0:
        return block
    return pltpu.roll(jnp.concatenate([tail, block], axis=0), back, 0)[8:]


def later(block, head, ahead):
    if ahead == 0:
        return block
    both = jnp.concatenate([block, head], axis=0)
    return pltpu.roll(both, both.shape[0] - ahead, 0)[: block.shape[0]]


def conv_rows(tail, block, taps):
    total = block * taps[TAPS - 1 : TAPS] + taps[TAPS : TAPS + 1]
    for j in range(TAPS - 1):
        total = total + earlier(tail, block, TAPS - 1 - j) * taps[j : j + 1]
    return total


def conv_rows_back(grad, head, taps):
    total = grad * taps[TAPS - 1 : TAPS]
    for j in range(TAPS - 1):
        total = total + later(grad, head, TAPS - 1 - j) * taps[j : j + 1]
    return total


def conv_taps_back(tail, block, grad):
    rows = [
        jnp.sum(earlier(tail, block, TAPS - 1 - j) * grad, axis=0, keepdims=True)
        for j in range(TAPS)
    ]
    rows.append(jnp.sum(grad, axis=0, keepdims=True))
    rows.append(jnp.zeros((8 - len(rows), grad.shape[1]), f32))
    return jnp.concatenate(rows, axis=0)


def head_columns(columns, heads):
    rows = columns.shape[0]
    low = iota((rows, 2 * HEAD), 1) < HEAD
    return jnp.concatenate(
        [
            jnp.where(low, columns[:, h : h + 1], columns[:, h + 1 : h + 2])
            for h in range(0, heads, 2)
        ],
        axis=1,
    )


def head_sums(values, heads):
    rows = values.shape[0]
    low = iota((rows, 2 * HEAD), 1) < HEAD
    sums = []
    for pair in range(heads // 2):
        part = values[:, pair * 2 * HEAD : (pair + 1) * 2 * HEAD]
        sums.append(jnp.sum(jnp.where(low, part, 0.0), axis=1, keepdims=True))
        sums.append(jnp.sum(jnp.where(low, 0.0, part), axis=1, keepdims=True))
    return sums


def softplus(value):
    return jnp.maximum(value, 0.0) + jnp.log1p(jnp.exp(-jnp.abs(value)))


def step_rows(pdt, vec):
    size = pdt.shape[1]
    raw = pdt + vec[:, 0:1]
    dt = softplus(raw)
    rate = -jnp.exp(vec[:, 1:2])
    upper = (iota((size, size), 0) <= iota((size, size), 1)).astype(f32)
    logs = dot_exact(dt * rate, upper)
    last = logs[:, size - 1 : size]
    return raw, dt, rate, logs, jnp.exp(logs), jnp.exp(last - logs), jnp.exp(last)


def mamba_fwd_kernel(
    heads,
    rank,
    px,
    px_tail,
    pz,
    pbc,
    pbc_tail,
    pdt,
    taps,
    shared_taps,
    vec,
    om,
    kept,
    states,
    state,
):
    step = pl.program_id(0)

    @pl.when(step == 0)
    def _():
        state[...] = jnp.zeros_like(state)

    started = jnp.where(step == 0, 0.0, 1.0)
    u = conv_rows(px_tail[...] * started, px[...], taps[...])
    u = u * jax.nn.sigmoid(u)
    bc = conv_rows(pbc_tail[...] * started, pbc[...], shared_taps[...])
    bc = (bc * jax.nn.sigmoid(bc)).astype(bf16)
    half = bc.shape[1] // 2
    b_in, c_out = bc[:, :half], bc[:, half:]
    _, dt, _, logs, grow, fade, last = step_rows(pdt[...], vec[...])
    columns = jnp.transpose(jnp.concatenate([logs, grow, fade * dt, dt], axis=0))
    size = u.shape[0]
    causal = iota((size, size), 0) >= iota((size, size), 1)
    mixing = dot_nt(c_out, b_in)
    u_low = u.astype(bf16)
    low = iota((size, 2 * HEAD), 1) < HEAD
    local = []
    for pair in range(heads // 2):
        piece = u_low[:, pair * 2 * HEAD : (pair + 1) * 2 * HEAD]
        outs = []
        for h in (2 * pair, 2 * pair + 1):
            spread = jnp.where(causal, columns[:, h : h + 1] - logs[h : h + 1], -1e30)
            matrix = (mixing * jnp.exp(spread) * dt[h : h + 1]).astype(bf16)
            outs.append(dot_nn(matrix, piece))
        local.append(jnp.where(low, outs[0], outs[1]))
    before = state[...]
    states[0] = before
    carried = dot_nn(c_out, before.astype(bf16)) * head_columns(columns[:, 8:16], heads)
    skip = head_columns(jnp.transpose(jnp.broadcast_to(vec[:, 2:3], (8, size))), heads)
    total = jnp.concatenate(local, axis=1) + carried + skip * u
    z = pz[...]
    om[...] = (total * (z * jax.nn.sigmoid(z))).astype(bf16)
    kept[...] = total.astype(bf16)
    fed = (u * head_columns(columns[:, 16:24], heads)).astype(bf16)
    end = head_columns(jnp.transpose(jnp.broadcast_to(last, (8, 128))), heads)[:1]
    state[...] = before * end + dot_tn(b_in, fed)


def mamba_bwd_kernel(
    heads,
    rank,
    px,
    px_tail,
    pz,
    pbc,
    pbc_tail,
    pdt,
    taps,
    shared_taps,
    vec,
    states,
    gym,
    g_pxs,
    g_pbc,
    g_taps,
    g_shared,
    g_vec,
    g_skip,
    d_state,
    next_px,
    next_bc,
):
    step = pl.program_id(0)
    steps = pl.num_programs(0)

    @pl.when(step == 0)
    def _():
        d_state[...] = jnp.zeros_like(d_state)
        next_px[...] = jnp.zeros_like(next_px)
        next_bc[...] = jnp.zeros_like(next_bc)
        g_taps[...] = jnp.zeros_like(g_taps)
        g_shared[...] = jnp.zeros_like(g_shared)
        g_vec[...] = jnp.zeros_like(g_vec)
        g_skip[...] = jnp.zeros_like(g_skip)

    started = jnp.where(step == steps - 1, 0.0, 1.0)
    size = px.shape[0]
    tail_x = px_tail[...] * started
    block_x = px[...]
    pre_u = conv_rows(tail_x, block_x, taps[...])
    sig_u = jax.nn.sigmoid(pre_u)
    u = pre_u * sig_u
    tail_bc = pbc_tail[...] * started
    block_bc = pbc[...]
    pre_bc = conv_rows(tail_bc, block_bc, shared_taps[...])
    sig_bc = jax.nn.sigmoid(pre_bc)
    bc = (pre_bc * sig_bc).astype(bf16)
    half = bc.shape[1] // 2
    b_in, c_out = bc[:, :half], bc[:, half:]
    raw, dt, rate, logs, grow, fade, last = step_rows(pdt[...], vec[...])
    columns = jnp.transpose(jnp.concatenate([logs, grow, fade, dt], axis=0))
    z = pz[...]
    sig_z = jax.nn.sigmoid(z)
    g = gym[...]
    dy = g * (z * sig_z)
    dy_low = dy.astype(bf16)
    u_low = u.astype(bf16)
    before = states[0]
    before_low = before.astype(bf16)
    d_after = d_state[...]
    d_after_low = d_after.astype(bf16)
    causal = iota((size, size), 0) <= iota((size, size), 1)
    mixing = dot_nt(b_in, c_out)
    low = iota((size, 2 * HEAD), 1) < HEAD
    d_mixing = jnp.zeros((size, size), f32)
    du_local, col_sums, row_sums = [], [], []
    for pair in range(heads // 2):
        lanes = slice(pair * 2 * HEAD, (pair + 1) * 2 * HEAD)
        u_piece, dy_piece = u_low[:, lanes], dy_low[:, lanes]
        outs = []
        for h in (2 * pair, 2 * pair + 1):
            dt_col = columns[:, 24 + h : 25 + h]
            spread = jnp.where(causal, logs[h : h + 1] - columns[:, h : h + 1], -1e30)
            decay = jnp.exp(spread)
            keep = low if h % 2 == 0 else jnp.logical_not(low)
            masked = jnp.where(keep, u_piece, jnp.zeros_like(u_piece))
            product = dot_nt(masked, dy_piece) * decay
            d_mixing = d_mixing + product * dt_col
            product = product * mixing
            col_sums.append(jnp.sum(product, axis=1, keepdims=True))
            row_sums.append(jnp.sum(product * dt_col, axis=0, keepdims=True))
            outs.append(dot_nn((mixing * decay).astype(bf16), dy_piece))
        du_local.append(jnp.where(low, outs[0], outs[1]))
    grow_all = head_columns(columns[:, 8:16], heads)
    fade_all = head_columns(columns[:, 16:24], heads)
    dt_all = head_columns(columns[:, 24:32], heads)
    dy_grown = dy * grow_all
    dy_grown_low = dy_grown.astype(bf16)
    fed_low = (u * fade_all * dt_all).astype(bf16)
    back = dot_nn(b_in, d_after_low) * fade_all
    inter = head_sums(dy_grown * dot_nn(c_out, before_low), heads)
    tails = head_sums(u * back, heads)
    skip = head_columns(jnp.transpose(jnp.broadcast_to(vec[:, 2:3], (8, size))), heads)
    du = (jnp.concatenate(du_local, axis=1) + back) * dt_all + skip * dy
    d_mixing_low = d_mixing.astype(bf16)
    db = dot_nn(d_mixing_low, c_out) + dot_nt(fed_low, d_after_low)
    dc = dot_tn(d_mixing_low, b_in) + dot_nt(dy_grown_low, before_low)
    end = head_columns(jnp.transpose(jnp.broadcast_to(last, (8, 128))), heads)[:1]
    ended = d_after * end
    ends = head_sums(jnp.sum(ended * before, axis=0, keepdims=True), heads)
    d_state[...] = ended + dot_tn(c_out, dy_grown_low)
    lane = iota((size, 128), 1)
    gathered = jnp.zeros((size, 128), f32)
    for h in range(heads):
        gathered = jnp.where(lane == h, col_sums[h] + tails[h], gathered)
        gathered = jnp.where(lane == 8 + h, tails[h], gathered)
        gathered = jnp.where(lane == 16 + h, inter[h], gathered)
    turned = jnp.transpose(gathered)
    direct, tail_row, inter_row = turned[0:8], turned[8:16], turned[16:24]
    pad = [jnp.zeros((1, size), f32)] * (8 - heads)
    row_sum = jnp.concatenate(row_sums + pad, axis=0)
    zero = jnp.zeros((1, 1), f32)
    end_col = jnp.concatenate(ends + [zero] * (8 - heads), axis=0)
    d_logs = row_sum + inter_row - dt * direct
    at_last = end_col + jnp.sum(dt * tail_row, axis=1, keepdims=True)
    lower = (iota((size, size), 0) >= iota((size, size), 1)).astype(f32)
    d_rate = dot_exact(d_logs, lower) + at_last
    d_dt = direct + rate * d_rate
    d_raw = d_dt * jax.nn.sigmoid(raw)
    spread_rows = jnp.concatenate([d_raw, jnp.zeros((120, size), f32)], axis=0)
    g_pxs[:, u.shape[1] :] = jnp.transpose(spread_rows).astype(bf16)
    g_vec[0:8] += d_raw
    g_vec[8:16] += rate * dt * d_rate
    g_skip[...] += jnp.sum((dy * u).reshape(size // 8, 8, u.shape[1]), axis=0)
    d_pre = du * (sig_u * (1.0 + pre_u * (1.0 - sig_u)))
    g_pxs[:, : u.shape[1]] = conv_rows_back(d_pre, next_px[...], taps[...]).astype(bf16)
    g_taps[...] += conv_taps_back(tail_x, block_x, d_pre)
    next_px[...] = d_pre[:8]
    d_bc = jnp.concatenate([db, dc], axis=1) * (sig_bc * (1.0 + pre_bc * (1.0 - sig_bc)))
    g_pbc[...] = conv_rows_back(d_bc, next_bc[...], shared_taps[...]).astype(bf16)
    g_shared[...] += conv_taps_back(tail_bc, block_bc, d_bc)
    next_bc[...] = d_bc[:8]


def pad_rows(value):
    return jnp.pad(value, ((0, -value.shape[0] % 8), (0, 0)))


def vec_of(step_bias, decay_log, skip_gain):
    table = jnp.stack([step_bias, decay_log, skip_gain], axis=1)
    return jnp.pad(table, ((0, 8 - table.shape[0]), (0, 128 - table.shape[1])))


def whole(shape):
    return pl.BlockSpec(shape, lambda i, r: tuple(0 for _ in shape))


def cost(flops, moved, exps):
    return pl.CostEstimate(flops=flops, bytes_accessed=moved, transcendentals=exps)


def chunk_specs(length, ranks, order):
    per_block = length // ranks // CHUNK
    per = CHUNK // 8

    def place(i, r):
        c = order(i)
        return ((c // per_block) ^ r[0]) * per_block + c % per_block

    def at(cols):
        return pl.BlockSpec((CHUNK, cols), lambda i, r: (place(i, r), 0))

    def tail(cols):
        def index(i, r):
            c = jnp.maximum(order(i) - 1, 0)
            return ((((c // per_block) ^ r[0]) * per_block + c % per_block) * per + per - 1, 0)

        return pl.BlockSpec((8, cols), index)

    row = pl.BlockSpec((8, CHUNK), lambda i, r: (0, place(i, r)))
    return at, tail, row


def mamba_fwd(rank, px, pz, pbc, pdt, taps, shared_taps, vec, heads, ranks):
    length, chans = px.shape
    wide = pbc.shape[1]
    steps = length // CHUNK
    at, tail, row = chunk_specs(length, ranks, lambda i: i)
    return pl.pallas_call(
        functools.partial(mamba_fwd_kernel, heads),
        grid_spec=pltpu.PrefetchScalarGridSpec(
            num_scalar_prefetch=1,
            grid=(steps,),
            in_specs=[
                at(chans),
                tail(chans),
                at(chans),
                at(wide),
                tail(wide),
                row,
                whole((8, chans)),
                whole((8, wide)),
                whole((8, 128)),
            ],
            out_specs=[
                at(chans),
                at(chans),
                pl.BlockSpec((1, wide // 2, chans), lambda i, r: (i, 0, 0)),
            ],
            scratch_shapes=[pltpu.VMEM((wide // 2, chans), f32)],
        ),
        out_shape=[
            jax.ShapeDtypeStruct((length, chans), bf16),
            jax.ShapeDtypeStruct((length, chans), bf16),
            jax.ShapeDtypeStruct((steps, wide // 2, chans), f32),
        ],
        cost_estimate=cost(4 * 10**9, 8 * 10**6, 10**6),
        name="mamba_forward",
    )(rank, px, px, pz, pbc, pbc, pdt, taps, shared_taps, vec)


def mamba_bwd(rank, px, pz, pbc, pdt, taps, shared_taps, vec, states, gym, heads, ranks):
    length, chans = px.shape
    wide = pbc.shape[1]
    steps = length // CHUNK
    at, tail, row = chunk_specs(length, ranks, lambda i: steps - 1 - i)
    return pl.pallas_call(
        functools.partial(mamba_bwd_kernel, heads),
        grid_spec=pltpu.PrefetchScalarGridSpec(
            num_scalar_prefetch=1,
            grid=(steps,),
            in_specs=[
                at(chans),
                tail(chans),
                at(chans),
                at(wide),
                tail(wide),
                row,
                whole((8, chans)),
                whole((8, wide)),
                whole((8, 128)),
                pl.BlockSpec((1, wide // 2, chans), lambda i, r: (steps - 1 - i, 0, 0)),
                at(chans),
            ],
            out_specs=[
                at(chans + 128),
                at(wide),
                whole((8, chans)),
                whole((8, wide)),
                whole((16, 128)),
                whole((8, chans)),
            ],
            scratch_shapes=[
                pltpu.VMEM((wide // 2, chans), f32),
                pltpu.VMEM((8, chans), f32),
                pltpu.VMEM((8, wide), f32),
            ],
        ),
        out_shape=[
            jax.ShapeDtypeStruct((length, chans + 128), bf16),
            jax.ShapeDtypeStruct((length, wide), bf16),
            jax.ShapeDtypeStruct((8, chans), f32),
            jax.ShapeDtypeStruct((8, wide), f32),
            jax.ShapeDtypeStruct((16, 128), f32),
            jax.ShapeDtypeStruct((8, chans), f32),
        ],
        cost_estimate=cost(9 * 10**9, 10**7, 10**6),
        name="mamba_backward",
    )(rank, px, px, pz, pbc, pbc, pdt, taps, shared_taps, vec, states, gym)


ROWS = 256


def turn(pre, cosine, sine):
    inner = iota(pre.shape, 1) % HEAD < HEAD // 2
    lanes = pre.shape[1]
    other = jnp.where(
        inner, pltpu.roll(pre, lanes - HEAD // 2, 1), pltpu.roll(pre, HEAD // 2, 1)
    )
    return pre * cosine + other * sine


def attend_fwd_kernel(scale, rank, qkv, cosine, sine, out, q, k, v):
    length, wide = out.shape
    blocks = length // ROWS
    low = iota((ROWS, 2 * HEAD), 1) < HEAD
    load_qkv(rank, qkv, cosine, sine, q, k, v)
    for i in range(blocks):
        seen = (i + 1) * ROWS
        block = q[i * ROWS : (i + 1) * ROWS]
        keys, values = k[:seen], v[:seen]
        allowed = iota((ROWS, seen), 1) <= iota((ROWS, seen), 0) + i * ROWS
        outs = []
        for h in range(2):
            keep = low if h == 0 else jnp.logical_not(low)
            part = jnp.where(keep, block, jnp.zeros_like(block))
            scores = jnp.where(allowed, dot_nt(part, keys) * scale, -1e30)
            expo = jnp.exp(scores - jnp.max(scores, axis=1, keepdims=True))
            chance = expo * (1.0 / jnp.sum(expo, axis=1, keepdims=True))
            outs.append(dot_nn(chance.astype(bf16), values))
        out[relative_rows(rank, i)] = jnp.where(low, outs[0], outs[1]).astype(bf16)


def relative_rows(rank, i):
    return pl.ds(pl.multiple_of((i ^ rank[0]) * ROWS, ROWS), ROWS)


def load_qkv(rank, qkv, cosine, sine, q, k, v):
    wide = q.shape[1]
    for i in range(q.shape[0] // ROWS):
        rows = slice(i * ROWS, (i + 1) * ROWS)
        piece = qkv[relative_rows(rank, i)]
        q[rows] = turn(piece[:, :wide], cosine[rows], sine[rows]).astype(bf16)
        both = piece[:, wide:]
        turned = pltpu.roll(both, HEAD, 1)
        low = iota(both.shape, 1) < HEAD
        k[rows] = turn(jnp.where(low, both, turned), cosine[rows], sine[rows]).astype(bf16)
        v[rows] = jnp.where(low, turned, both).astype(bf16)


def attend_bwd_kernel(scale, rank, qkv, cosine, sine, go, g_qkv, q, k, v, dk, dv):
    length, wide = dk.shape
    blocks = length // ROWS
    low = iota((ROWS, 2 * HEAD), 1) < HEAD
    load_qkv(rank, qkv, cosine, sine, q, k, v)
    dk[...] = jnp.zeros_like(dk)
    dv[...] = jnp.zeros_like(dv)
    for i in range(blocks):
        seen = (i + 1) * ROWS
        rows = slice(i * ROWS, (i + 1) * ROWS)
        block, grads = q[rows], go[relative_rows(rank, i)]
        keys, values = k[:seen], v[:seen]
        allowed = iota((seen, ROWS), 0) <= iota((seen, ROWS), 1) + i * ROWS
        dqs, dks, dvs = [], [], []
        for h in range(2):
            keep = low if h == 0 else jnp.logical_not(low)
            part = jnp.where(keep, block, jnp.zeros_like(block))
            part_g = jnp.where(keep, grads, jnp.zeros_like(grads))
            scores = jnp.where(allowed, dot_nt(keys, part) * scale, -1e30)
            expo = jnp.exp(scores - jnp.max(scores, axis=0, keepdims=True))
            chance = expo * (1.0 / jnp.sum(expo, axis=0, keepdims=True))
            g_chance = dot_nt(values, part_g)
            center = jnp.sum(chance * g_chance, axis=0, keepdims=True)
            g_scores = (chance * (g_chance - center)).astype(bf16)
            dqs.append(dot_tn(g_scores, keys))
            dks.append(dot_nn(g_scores, part))
            dvs.append(dot_nn(chance.astype(bf16), part_g))
        dq = jnp.where(low, dqs[0], dqs[1]) * scale
        g_qkv[relative_rows(rank, i), :wide] = turn(dq, cosine[rows], -sine[rows]).astype(bf16)
        dk[:seen] += (dks[0] + dks[1]) * scale
        dv[:seen] += dvs[0] + dvs[1]
    for i in range(blocks):
        rows = slice(i * ROWS, (i + 1) * ROWS)
        g_k, g_v = dk[rows], dv[rows]
        g_k = turn(g_k + pltpu.roll(g_k, HEAD, 1), cosine[rows], -sine[rows])
        g_v = g_v + pltpu.roll(g_v, HEAD, 1)
        g_qkv[relative_rows(rank, i), wide:] = jnp.where(low, g_k, g_v).astype(bf16)


def attend_specs(length, wide):
    return [
        whole((length, 2 * wide)),
        whole((length, wide)),
        whole((length, wide)),
    ], [pltpu.VMEM((length, wide), bf16)] * 3


def attend_fwd(rank, qkv, cosine, sine):
    length, wide = cosine.shape
    ins, scratch = attend_specs(length, wide)
    return pl.pallas_call(
        functools.partial(attend_fwd_kernel, HEAD**-0.5),
        grid_spec=pltpu.PrefetchScalarGridSpec(
            num_scalar_prefetch=1,
            grid=(1,),
            in_specs=ins,
            out_specs=whole((length, wide)),
            scratch_shapes=scratch,
        ),
        out_shape=jax.ShapeDtypeStruct((length, wide), bf16),
        cost_estimate=cost(2 * 10**9, 4 * 10**6, 10**6),
        name="attend_forward",
    )(rank, qkv, cosine, sine)


def attend_bwd(rank, qkv, cosine, sine, g_oa):
    length, wide = cosine.shape
    ins, scratch = attend_specs(length, wide)
    return pl.pallas_call(
        functools.partial(attend_bwd_kernel, HEAD**-0.5),
        grid_spec=pltpu.PrefetchScalarGridSpec(
            num_scalar_prefetch=1,
            grid=(1,),
            in_specs=ins + [whole((length, wide))],
            out_specs=whole((length, 2 * wide)),
            scratch_shapes=scratch + [pltpu.VMEM((length, wide), f32)] * 2,
        ),
        out_shape=jax.ShapeDtypeStruct((length, 2 * wide), bf16),
        cost_estimate=cost(4 * 10**9, 6 * 10**6, 10**6),
        name="attend_backward",
    )(rank, qkv, cosine, sine, g_oa)


def project_kernel(order, chans, scalars, even, odd, gain, *refs):
    w_x, w_z, w_bc, outs = refs[:4], refs[4:8], refs[8], refs[9:]
    a1, kept, px, pz, pbc, pdt, qkv = outs
    rows, width = even.shape
    block = width // len(order)
    is_even = pl.program_id(0) % 2 == 0
    step = 32

    def norm(source, keep):
        for i in range(rows // step):
            own = slice(i * step, (i + 1) * step)
            value = source[own].astype(f32)
            rho = lax.rsqrt(jnp.mean(value * value, axis=1, keepdims=True) + epsilon)
            for p, k in enumerate(order):
                there = pl.ds(pl.multiple_of((scalars[0] ^ k) * block, block), block)
                here = slice(p * block, (p + 1) * block)
                piece = source[own, there]
                a1[own, here] = (piece.astype(f32) * rho * gain[:, here]).astype(bf16)
                if keep:
                    kept[own, here] = piece

    @pl.when(is_even)
    def _():
        norm(even, True)

    @pl.when(jnp.logical_not(is_even))
    def _():
        norm(odd, False)

    quarter = width // 4
    parts = [a1[:, q * quarter : (q + 1) * quarter] for q in range(4)]
    px[...] = sum(dot_nn(part, w[:, :chans]) for part, w in zip(parts, w_x))
    steps = sum(
        lax.dot_general(
            w[:, chans:], part, (((0,), (1,)), ((), ())), preferred_element_type=f32
        )
        for part, w in zip(parts, w_x)
    )
    pdt[...] = steps[:8]
    pz[...] = sum(dot_nn(part, w[:, :chans]) for part, w in zip(parts, w_z))
    pbc[...] = dot_nn(a1[...], w_bc[...])
    qkv[...] = sum(dot_nn(part, w[:, chans:]) for part, w in zip(parts, w_z))


def project(scalars, even, odd, gain, w_x, w_z, w_bc, chans, size):
    rows, width = even.shape[0] // 2, even.shape[1]
    length = 4 * rows
    if width // size % 128:
        member = scalars[0]
        even = take_blocks(even, member, size, False)
        odd = take_blocks(odd, member, size, False)
        order = [0]
    else:
        order = relative_order(size)
    if len(order) == 1:
        scalars = jnp.zeros_like(scalars)

    def at(cols):
        return pl.BlockSpec((rows, cols), lambda i, r: (i, 0))

    def half(cols):
        return pl.BlockSpec((rows, cols), lambda i, r: (i // 2, 0))

    def shape(cols, kind, count=length):
        return jax.ShapeDtypeStruct((count, cols), kind)

    n2, low = w_bc.shape[1], w_z[0][0].shape[1] - chans
    return pl.pallas_call(
        functools.partial(project_kernel, order, chans),
        grid_spec=pltpu.PrefetchScalarGridSpec(
            num_scalar_prefetch=1,
            grid=(4,),
            in_specs=[half(width), half(width), whole((1, width))]
            + quarter_specs(w_x)
            + quarter_specs(w_z)
            + [whole(w_bc.shape)],
            out_specs=[
                at(width),
                half(width),
                at(chans),
                at(chans),
                at(n2),
                pl.BlockSpec((8, rows), lambda i, r: (0, i)),
                at(low),
            ],
        ),
        out_shape=[
            shape(width, bf16),
            shape(width, bf16, 2 * rows),
            shape(chans, f32),
            shape(chans, f32),
            shape(n2, f32),
            shape(length, f32, 8),
            shape(low, f32),
        ],
        cost_estimate=cost(3 * 10**9, 14 * 10**6, length),
        name="norm_project",
    )(scalars, even, odd, gain.reshape(1, -1), *arrays_of(w_x), *arrays_of(w_z), w_bc)


def mixer_kernel(chans, rank, om, oa, *refs):
    w_o, (kept, sent) = refs[:4], refs[4:]
    total = jnp.concatenate(
        [dot_nt(om[...], w[:, :chans]) + dot_nt(oa[...], w[:, chans:]) for w in w_o], axis=1
    )

    @pl.when(pl.program_id(0) % 2 == 0)
    def _():
        kept[...] = total

    @pl.when(pl.program_id(0) % 2 == 1)
    def _():
        sent[...] = total.astype(bf16)


def mixer_out(token, om, oa, w_o):
    rows, width = om.shape[0] // 4, 4 * w_o[0][0].shape[0]

    def at(cols):
        return pl.BlockSpec((rows, cols), lambda i, r: (i, 0))

    half = pl.BlockSpec((rows, width), lambda i, r: (i // 2, 0))
    return pl.pallas_call(
        functools.partial(mixer_kernel, om.shape[1]),
        grid_spec=pltpu.PrefetchScalarGridSpec(
            num_scalar_prefetch=1,
            grid=(4,),
            in_specs=[at(om.shape[1]), at(oa.shape[1])] + quarter_specs(w_o),
            out_specs=[half, half],
        ),
        out_shape=[
            jax.ShapeDtypeStruct((2 * rows, width), f32),
            jax.ShapeDtypeStruct((2 * rows, width), bf16),
        ],
        cost_estimate=cost(10**9, 7 * 10**6, 0),
        name="mixer_out",
    )(token, om, oa, *arrays_of(w_o))


def mixer_back_kernel(chans, rank, g0, g1, g2, g3, *refs):
    w_o = refs[:4]
    pz, kept, g_ym, g_oa, g_pz, total = refs[4:]
    quarter = g0.shape[1] // 4
    for k, piece in enumerate((g0, g1, g2, g3)):

        @pl.when(pl.program_id(0) == k)
        def _(piece=piece):
            total[...] = sum(
                dot_nn(piece[:, q * quarter : (q + 1) * quarter], w_o[q][...]) for q in range(4)
            )

    back = total[:, :chans]
    g_ym[...] = back
    g_oa[...] = total[:, chans:].astype(bf16)
    z = pz[...]
    sig = jax.nn.sigmoid(z)
    g_pz[...] = (back * kept[...].astype(f32) * (sig * (1.0 + z * (1.0 - sig)))).astype(bf16)


def mixer_back(token, g_m, w_o, pz, kept):
    rows, width = g_m[0].shape
    length, chans = pz.shape
    cols_o = w_o[0][0].shape[1]
    other = cols_o - chans

    def at(cols):
        return pl.BlockSpec((rows, cols), lambda i, r: (i, 0))

    return pl.pallas_call(
        functools.partial(mixer_back_kernel, chans),
        grid_spec=pltpu.PrefetchScalarGridSpec(
            num_scalar_prefetch=1,
            grid=(4,),
            in_specs=[whole((rows, width))] * 4 + quarter_specs(w_o) + [at(chans)] * 2,
            out_specs=[at(chans), at(other), at(chans)],
            scratch_shapes=[pltpu.VMEM((rows, cols_o), f32)],
        ),
        out_shape=[
            jax.ShapeDtypeStruct((length, chans), f32),
            jax.ShapeDtypeStruct((length, other), bf16),
            jax.ShapeDtypeStruct((length, chans), bf16),
        ],
        cost_estimate=cost(10**9, 9 * 10**6, 10**6),
        name="mixer_back",
    )(token, *g_m, *arrays_of(w_o), pz, kept)


def project_back_kernel(chans, rank, a1, g_pz, g_qkv, g_pxs, g_bc, *refs):
    w_x, w_z, w_bc = refs[:4], refs[4:8], refs[8]
    kept, sent, sums = refs[9:]
    step = pl.program_id(0)
    total = jnp.concatenate(
        [
            dot_nt(g_pz[...], wz[:, :chans])
            + dot_nt(g_qkv[...], wz[:, chans:])
            + dot_nt(g_pxs[...], wx[...])
            for wx, wz in zip(w_x, w_z)
        ],
        axis=1,
    ) + dot_nt(g_bc[...], w_bc[...])

    @pl.when(step == 0)
    def _():
        sums[...] = jnp.zeros_like(sums)

    rows, width = total.shape
    weighed = total * a1[...].astype(f32)
    sums[...] += jnp.sum(weighed.reshape(rows // 8, 8, width), axis=0)

    @pl.when(step % 2 == 0)
    def _():
        kept[...] = total

    @pl.when(step % 2 == 1)
    def _():
        sent[...] = total.astype(bf16)


def project_back(token, a1, g_pz, g_qkv, g_pxs, g_bc, w_x, w_z, w_bc):
    length, width = a1.shape
    chans = g_pz.shape[1]
    rows = length // 4

    def at(cols):
        return pl.BlockSpec((rows, cols), lambda i, r: (i, 0))

    half = pl.BlockSpec((rows, width), lambda i, r: (i // 2, 0))
    parts = (a1, g_pz, g_qkv, g_pxs, g_bc)
    return pl.pallas_call(
        functools.partial(project_back_kernel, chans),
        grid_spec=pltpu.PrefetchScalarGridSpec(
            num_scalar_prefetch=1,
            grid=(4,),
            in_specs=[at(item.shape[1]) for item in parts]
            + quarter_specs(w_x)
            + quarter_specs(w_z)
            + [whole(w_bc.shape)],
            out_specs=[half, half, whole((8, width))],
        ),
        out_shape=[
            jax.ShapeDtypeStruct((2 * rows, width), f32),
            jax.ShapeDtypeStruct((2 * rows, width), bf16),
            jax.ShapeDtypeStruct((8, width), f32),
        ],
        cost_estimate=cost(3 * 10**9, 11 * 10**6, 0),
        name="project_back",
    )(token, *parts, *arrays_of(w_x), *arrays_of(w_z), w_bc)


def rotary_tables(length):
    half = HEAD // 2
    frequency = rotary_base ** (-2.0 * jnp.arange(half, dtype=f32) / HEAD)
    angles = jnp.arange(length, dtype=f32)[:, None] * frequency[None, :]
    cosine, sine = jnp.cos(angles), jnp.sin(angles)
    return (
        jnp.concatenate([cosine] * 4, axis=1),
        jnp.concatenate([-sine, sine, -sine, sine], axis=1),
    )


def swiglu(gate_part, up_part):
    return jax.nn.silu(gate_part) * up_part


def mm(a, b):
    return jnp.dot(a, b, preferred_element_type=f32)


def mm_t(a, b):
    return lax.dot_general(a, b, (((1,), (1,)), ((), ())), preferred_element_type=f32)


def t_mm(a, b):
    return lax.dot_general(a, b, (((0,), (0,)), ((), ())), preferred_element_type=f32)


def body(
    layer_in,
    out_grad,
    lengths,
    mamba_x,
    mamba_z,
    mamba_step,
    query_proj,
    key_proj,
    value_proj,
    mamba_out,
    attend_out,
    mlp_gate,
    mlp_up,
    mlp_down,
    state_proj,
    conv_state,
    norm_gains,
    conv_mamba,
    step_bias,
    decay_log,
    skip_gain,
):
    ranks = lax.axis_size("tensor")
    assert ranks == 4 and layer_in.shape[1] == 1
    rank = lax.axis_index("tensor")
    y, core = rank // 2, rank % 2
    rank_ref = rank.reshape(1)
    peers = lax.axis_size("dp")
    me = lax.axis_index("dp")
    rows, _, width = layer_in.shape
    length = rows * ranks
    chans = mamba_x.shape[1]
    heads = step_bias.shape[0]
    q_cols, k_cols = query_proj.shape[1], key_proj.shape[1]
    ff = mlp_gate.shape[1]
    own_rows, n2 = state_proj.shape

    pack_x, pack_z = pack_early(
        mamba_x, mamba_step.T, mamba_z, query_proj, key_proj.T, value_proj.T
    )
    first = Gather(pack_x, "dp", False)
    second = Gather(pack_z, "dp", True)
    layer_in, conv_state, norm_gains, state_proj = lax.optimization_barrier(
        (layer_in, conv_state, norm_gains, state_proj, pack_x, pack_z)
    )[:4]
    raw_0 = layer_in[:, 0]
    raw_even = jnp.concatenate([raw_0, flip_y(raw_0)], axis=0)
    raw_odd = flip_core(raw_even)
    small = jnp.concatenate([conv_state.reshape(-1), norm_gains.reshape(-1)])
    parts = []
    rest = small
    for _ in range(3):
        parts.append(lax.reduce_precision(rest, 8, 7))
        rest = rest - parts[-1]
    parts = jnp.concatenate(parts)
    small_rows = -(-parts.shape[0] // n2)
    parts = jnp.pad(parts, (0, small_rows * n2 - parts.shape[0])).reshape(small_rows, n2)
    pack_s = jnp.concatenate([state_proj, parts], axis=0).astype(bf16)
    pack_o = jnp.concatenate([mamba_out.T.astype(bf16), attend_out.T.astype(bf16)], axis=1)
    pack_m = jnp.concatenate(
        [mlp_gate.astype(bf16), mlp_up.astype(bf16), mlp_down.T.astype(bf16)], axis=1
    )
    ranked = in_rank_order(pack_s, y, core)
    third = Gather(ranked.reshape(-1, n2), "dp", False)
    sent_x = first.until(2)
    sent_z = second.until(2)
    third.until(2, sent_x, sent_z)
    far_x = first.advance()
    far_z = second.advance()
    third.advance(far_x, far_z)
    gather_m = Gather(after(pack_m, far_x, far_z), "dp", False, True)
    w_x = first.advance()
    gather_o = Gather(after(pack_o, arrays_of(w_x)[2]), "dp", True)
    w_z = second.advance()
    all_s = join_quarters(third.advance()).reshape(peers, ranks, own_rows + small_rows, n2)
    w_bc = all_s[:, :, :own_rows].reshape(width, n2)
    parts = all_s[:, :, own_rows:].reshape(peers, ranks, -1).astype(f32)
    count = small.shape[0]
    small = parts[..., :count] + parts[..., count : 2 * count] + parts[..., 2 * count : 3 * count]
    cut = conv_state.size
    taps_own = conv_state.shape[1]
    gains_own = norm_gains.shape[1]
    taps_rel = small[..., :cut].reshape(peers, ranks, conv_state.shape[0], taps_own)
    taps_rel = jnp.transpose(taps_rel, (2, 0, 1, 3)).reshape(conv_state.shape[0], -1)
    conv_shared = take_blocks(taps_rel, me, peers, True)
    gain_pair = jnp.transpose(
        small[..., cut:].reshape(peers, ranks, 2, gains_own), (2, 0, 1, 3)
    ).reshape(2, width)

    def rho_of(values):
        return lax.rsqrt(jnp.mean(values * values, axis=-1, keepdims=True) + epsilon)

    a1, x02, px, pz, pbc, pdt, qkv = project(
        me.reshape(1), raw_even, raw_odd, gain_pair[0], w_x, w_z, w_bc, chans, peers
    )
    x0, x2 = x02[:rows], x02[rows:]

    limit = lengths[0]

    def masked(block, k):
        place = (rank ^ k) * rows + jnp.arange(rows, dtype=jnp.int32)
        return jnp.where((place < limit)[:, None], block, jnp.zeros_like(block))

    gf0 = masked(move_blocks(after(out_grad, far_x, far_z)[:, 0], me, peers, False), 0)
    gf2 = flip_y(after(gf0, raw_even))

    sent_m = gather_m.until(2, pdt)
    sent_o = gather_o.until(2, pdt)
    cosine, sine = rotary_tables(length)
    oa = attend_fwd(after(rank_ref, sent_o, sent_m), qkv, cosine, sine)
    gf_odd = flip_core(jnp.concatenate([gf0, after(gf2, pdt)], axis=0))
    sent_o = gather_o.advance(oa)
    vec = vec_of(step_bias, decay_log, skip_gain)
    taps, shared_taps = pad_rows(conv_mamba), pad_rows(conv_shared)
    gf_odd = after(gf_odd, oa)
    om, kept, states = mamba_fwd(
        after(rank_ref, sent_o, gf_odd), px, pz, pbc, pdt, taps, shared_taps, vec, heads, ranks
    )
    w_o = gather_o.advance(om)
    gf1, gf3 = gf_odd[:rows], gf_odd[rows:]
    gf_a = jnp.concatenate([gf0, gf1], axis=0)
    gf_b = jnp.concatenate([gf2, gf3], axis=0)
    sent_m = gather_m.advance(om)
    m_kept, m_sent = mixer_out(after(rank_ref, sent_m, gather_m.cross), om, oa, w_o)
    s02 = add_low(m_kept, flip_core(m_sent))
    s0, s2 = s02[:rows], s02[rows:]
    w_m = gather_m.advance()
    m_got = after(flip_y(s2), *arrays_of(w_m))
    w_m = join_quarters(w_m)
    w_gu, w_dn = w_m[:, : 2 * ff], w_m[:, 2 * ff :]

    def second_norm(low_x, m):
        r1 = low_x.astype(f32) + m
        rho = rho_of(r1)
        return r1, rho, (r1 * rho * gain_pair[1]).astype(bf16)

    r1_0, rho_0, a2_0 = second_norm(x0, s0.astype(f32) + m_got.astype(f32))
    a2_1 = flip_core(a2_0)
    a2_a = jnp.concatenate([a2_0, a2_1], axis=0)
    m_other = after(flip_y(s0), a2_0)
    r1_2, rho_2, a2_2 = second_norm(x2, s2.astype(f32) + m_other.astype(f32))
    a2_3 = flip_core(a2_2)
    a2_b = jnp.concatenate([a2_2, a2_3], axis=0)

    def feed(a2, gf, *others):
        gate_up = mm(a2, w_gu)
        gate, up = gate_up[:, :ff], gate_up[:, ff:]
        hidden, glu_back = jax.vjp(swiglu, gate, up)
        hid = hidden.astype(bf16)
        gate_grad, up_grad = glu_back(mm(gf, w_dn))
        g_gu = jnp.concatenate([gate_grad.astype(bf16), up_grad.astype(bf16)], axis=1)
        if others:
            g_gu = after(g_gu, *others)
        return hid, g_gu, mm_t(g_gu, w_gu)

    hid_a, g_gu_a, g_a2_a = feed(a2_a, gf_a)
    t0 = core_sum(g_a2_a[:rows], g_a2_a[rows:])
    hid_b, g_gu_b, g_a2_b = feed(a2_b, gf_b, t0)
    t2 = core_sum(g_a2_b[:rows], g_a2_b[rows:])

    halves = ((0, 0), (0, 1), (1, 0), (1, 1))
    dn_kept, dn_sent = product(
        after(rank_ref, g_a2_b),
        [[(left, [((hid_a, hid_b)[p], b)]) for left, (p, b) in zip((gf0, gf1, gf2, gf3), halves)]],
        True,
    )
    dn = Sum(dn_kept, dn_sent, "dp", True)
    gu_kept, gu_sent = product(
        after(rank_ref, dn_sent),
        [
            [
                (left, [((g_gu_a, g_gu_b)[p], b)])
                for left, (p, b) in zip((a2_0, a2_1, a2_2, a2_3), halves)
            ]
        ],
        False,
    )
    gu = Sum(gu_kept, gu_sent, "dp", False)

    def second_back(g_a2, r1, rho, gf):
        n_two = r1 * rho
        e_two = g_a2 * gain_pair[1]
        inner = jnp.mean(e_two * n_two, axis=-1, keepdims=True)
        return gf.astype(f32) + rho * (e_two - n_two * inner)

    t0_got, t2_got = flip_y(t0), flip_y(t2)
    g_a2_2 = t2.astype(f32) + after(t0_got, t2, gu_sent).astype(f32)
    g_r1_2 = second_back(g_a2_2, r1_2, rho_2, gf2)
    g_m_2 = g_r1_2.astype(bf16)
    g_a2_0 = t0.astype(f32) + after(t2_got, gu_sent).astype(f32)
    g_r1_0 = second_back(g_a2_0, r1_0, rho_0, gf0)
    g_m_0 = g_r1_0.astype(bf16)
    gain_two_grad = jnp.sum(g_a2_0 * (r1_0 * rho_0), axis=0)
    g_m_3, g_m_1 = flip_core(g_m_2), flip_core(g_m_0)
    g_m = (g_m_0, g_m_1, g_m_2, g_m_3)
    g_ym, g_oa, g_pz = mixer_back(after(rank_ref, dn_sent, gu_sent), g_m, w_o, pz, kept)

    sent_dn = dn.advance(g_oa)
    hid_a, hid_b = lax.optimization_barrier((hid_a, hid_b, g_m_0))[:2]
    f_a, f_b = mm_t(hid_a, w_dn), mm_t(hid_b, w_dn)
    f_sent = jnp.concatenate([f_a[rows:], f_b[rows:]], axis=0).astype(bf16)
    f_got = flip_core(f_sent)
    g_qkv = attend_bwd(after(rank_ref, sent_dn, f_sent), qkv, cosine, sine, g_oa)
    sent_dn = dn.advance(g_qkv)
    sent_gu = gu.advance(g_qkv)
    f_kept = jnp.concatenate([f_a[:rows], f_b[:rows]], axis=0)
    f02 = add_low(f_kept, after(f_got, g_qkv))
    f_other = flip_y(f02[rows:])
    z_kept, z_sent = product(
        after(rank_ref, sent_dn, sent_gu, f02),
        [[(g_m[k], [(om, k), (oa, k)]) for k in range(4)], [(a1, [(g_pz, 0), (g_qkv, 0)])]],
        False,
    )
    z = Sum(z_kept, z_sent, "dp", False)
    sent_gu = gu.advance(z_sent)

    g_pxs, g_bc, g_taps, g_shared, g_vec, g_skip = mamba_bwd(
        after(rank_ref, z_sent, sent_gu),
        px, pz, pbc, pdt, taps, shared_taps, vec, states, g_ym, heads, ranks,
    )
    dn_sum, gu_sum = dn.finish(g_pxs), gu.finish(g_pxs)
    x_kept, x_sent = product(
        after(rank_ref, dn_sum, gu_sum), [[(a1, [(g_pxs, 0)])]], False
    )
    x = Sum(x_kept, x_sent, "dp", False)
    sent_z = z.advance(x_sent)
    g_kept, g_sent, g_sums = project_back(
        after(rank_ref, x_sent, sent_z), a1, g_pz, g_qkv, g_pxs, g_bc, w_x, w_z, w_bc
    )
    g_got = flip_core(g_sent)
    sent_x = x.advance(g_sums)
    sent_z = z.advance(g_sums)
    u02 = add_low(g_kept, after(g_got, sent_x, sent_z))
    u_other = flip_y(u02[rows:])
    gain_one_grad = jnp.sum(g_sums, axis=0) / gain_pair[0]
    state_part = t_mm(after(a1, x_sent), g_bc).reshape(peers, 2, 2, own_rows, n2)
    f_other = after(f_other, u02)

    g_taps, g_shared, g_vec, g_skip = lax.optimization_barrier(
        (g_taps, g_shared, g_vec, g_skip, g_sums)
    )[:4]
    conv_taps_grad = g_taps[: conv_mamba.shape[0]]
    conv_shared_grad = g_shared[: conv_state.shape[0]]
    bias_grad = jnp.sum(g_vec[:heads], axis=1)
    decay_grad = jnp.sum(g_vec[8 : 8 + heads], axis=1)
    skip_grad = jnp.sum(g_skip.reshape(8, heads, HEAD), axis=(0, 2))
    gain_grads = take_blocks(jnp.stack([gain_one_grad, gain_two_grad]), me, peers, True)

    def rows_of(items):
        flat = jnp.concatenate([item.reshape(-1) for item in items])
        return jnp.pad(flat, (0, -flat.shape[0] % (8 * n2))).reshape(-1, n2)

    both = rows_of([conv_shared_grad, gain_grads])
    only = rows_of([conv_taps_grad, bias_grad, decay_grad, skip_grad])

    def exchange(kept, sent, shared, axis, mask, *others):
        got = flip(jnp.concatenate([sent.reshape(-1, n2), shared], axis=0), axis, mask)
        got = after(got, *others)
        count = got.shape[0] - shared.shape[0]
        return kept + got[:count].reshape(kept.shape), shared + got[count:]

    by_core = pick(core, state_part[:, :, ::-1], state_part)
    state, both = exchange(by_core[:, :, 0], by_core[:, :, 1], both, "tensor", 1, u02)
    by_y = pick(y, state[:, ::-1], state)
    sent_x = x.advance(by_y)
    state, both = exchange(by_y[:, 0], by_y[:, 1], both, "tensor", 2, sent_x, sent_z)
    state = state.reshape(peers * own_rows, n2)
    shared = jnp.concatenate([both, only], axis=0)
    tie = (u_other,)
    for bit in range(bits_of(peers)):
        half = state.shape[0] // 2
        state, shared = exchange(state[:half], state[half:], shared, "dp", 1 << bit, *tie)
        if bit == 0:
            both_sum = z.finish(state)
            tie = (both_sum,)
        elif bit == 1:
            tie = ()
    state_proj_grad = state
    both_rows = both.shape[0]
    both = shared[:both_rows].reshape(-1)
    only = shared[both_rows:].reshape(-1)

    f_sum = f02[:rows].astype(f32) + f_other.astype(f32)
    layer_out = masked(r1_0 + f_sum, 0).astype(bf16)
    layer_out = move_blocks(layer_out, me, peers, True)[:, None]
    x_sum = x.finish()
    out_sum, z_sum = both_sum[:, : chans + q_cols], both_sum[:, chans + q_cols :]
    in_grad = final_gradient(after(me, both_sum), peers, u02, u_other, gain_pair[0], x02, g_r1_0)[:, None]

    conv_state_sum = both[: conv_state.size * peers * ranks].reshape(conv_shared.shape)
    gain_sum = both[conv_shared.size : conv_shared.size + 2 * width].reshape(2, width)
    member = me * ranks + rank
    conv_state_grad = lax.dynamic_slice_in_dim(conv_state_sum, member * taps_own, taps_own, 1)
    norm_gains_grad = lax.dynamic_slice_in_dim(gain_sum, member * gains_own, gains_own, 1)
    cut = conv_taps_grad.size
    conv_mamba_grad = only[:cut].reshape(conv_taps_grad.shape)
    step_bias_grad = only[cut : cut + heads]
    decay_log_grad = only[cut + heads : cut + 2 * heads]
    skip_gain_grad = only[cut + 2 * heads : cut + 3 * heads]

    return (
        layer_out,
        in_grad,
        x_sum[:, :chans],
        z_sum[:, :chans],
        x_sum[:, chans : chans + heads],
        z_sum[:, chans : chans + q_cols],
        z_sum[:, chans + q_cols : chans + q_cols + k_cols],
        z_sum[:, chans + q_cols + k_cols :],
        out_sum[:, :chans].T,
        out_sum[:, chans:].T,
        gu_sum[:, :ff],
        gu_sum[:, ff:],
        dn_sum.T,
        state_proj_grad,
        conv_state_grad,
        norm_gains_grad,
        conv_mamba_grad,
        step_bias_grad,
        decay_log_grad,
        skip_gain_grad,
    )


def solution(mesh):
    in_specs = (
        P("tensor", "dp", None),
        P("tensor", "dp", None),
        P("dp"),
        P("dp", "tensor"),
        P("dp", "tensor"),
        P("dp", "tensor"),
        P("dp", "tensor"),
        P("dp", "tensor"),
        P("dp", "tensor"),
        P("tensor", "dp"),
        P("tensor", "dp"),
        P("dp", "tensor"),
        P("dp", "tensor"),
        P("tensor", "dp"),
        P(("dp", "tensor"), None),
        P(None, ("dp", "tensor")),
        P(None, ("dp", "tensor")),
        P(None, "tensor"),
        P("tensor"),
        P("tensor"),
        P("tensor"),
    )
    out_specs = (
        P("tensor", "dp", None),
        P("tensor", "dp", None),
        P("dp", "tensor"),
        P("dp", "tensor"),
        P("dp", "tensor"),
        P("dp", "tensor"),
        P("dp", "tensor"),
        P("dp", "tensor"),
        P("tensor", "dp"),
        P("tensor", "dp"),
        P("dp", "tensor"),
        P("dp", "tensor"),
        P("tensor", "dp"),
        P(("dp", "tensor"), None),
        P(None, ("dp", "tensor")),
        P(None, ("dp", "tensor")),
        P(None, "tensor"),
        P("tensor"),
        P("tensor"),
        P("tensor"),
    )
    return jax.shard_map(body, mesh=mesh, in_specs=in_specs, out_specs=out_specs, check_vma=False)
```

```python
import functools

import jax
import jax.numpy as jnp
from jax import lax
from jax.experimental import pallas as pl
from jax.experimental.pallas import tpu as pltpu
from jax.sharding import PartitionSpec as P

epsilon = 1e-05
rotary_base = 100000000000.0
HIGHEST = lax.Precision.HIGHEST
bf16 = jnp.bfloat16
f32 = jnp.float32


def flip(value, axis, mask):
    size = lax.axis_size(axis)
    return lax.ppermute(value, axis, [(i, i ^ mask) for i in range(size)])


def bits_of(size):
    bits = size.bit_length() - 1
    assert size == 1 << bits
    return bits


def relative_order(size):
    order = [0]
    for bit in reversed(range(bits_of(size))):
        order = order + [k | (1 << bit) for k in order]
    return order


def join_quarters(quarters):
    count = quarters[0][0].shape[0]
    return jnp.concatenate(
        [item[k * count : (k + 1) * count] for item, k in quarters], axis=0
    )


def quarter_specs(quarters):
    count, cols = quarters[0][0].shape
    return [
        pl.BlockSpec((count, cols), lambda i, r, block=block: (block, 0)) for _, block in quarters
    ]


def arrays_of(quarters):
    return [array for array, _ in quarters]


class Gather:
    def __init__(self, own, axis, swap, split=False):
        self.axis, self.swap, self.split = axis, swap, split
        order = list(reversed(range(bits_of(lax.axis_size(axis)))))
        if swap:
            order[-2:] = [0, 1]
        self.order, self.held = order, own
        self.send()

    def send(self):
        self.got = flip(self.held, self.axis, 1 << self.order[0])
        if self.split and len(self.order) == 2:
            self.cross = flip(self.held, self.axis, 1 << self.order[1])

    def advance(self, *others):
        got = after(self.got, *others) if others else self.got
        left = len(self.order)
        self.order = self.order[1:]
        if left > 2:
            self.held = jnp.concatenate([self.held, got], axis=0)
            self.send()
            return self.held
        if left == 2:
            self.near = got
            sent = got if self.split else jnp.concatenate([self.held, got], axis=0)
            self.got = flip(sent, self.axis, 1 << self.order[0])
            return sent
        cross, last = ((self.cross, 0), (got, 0)) if self.split else ((got, 0), (got, 1))
        one, two = (cross, (self.near, 0)) if self.swap else ((self.near, 0), cross)
        return [(self.held, 0), one, two, last]

    def until(self, left, *others):
        while len(self.order) > left:
            both = self.advance(*others)
        return both


class Sum:
    def __init__(self, kept, sent, axis, swap):
        order = list(range(bits_of(lax.axis_size(axis))))
        if swap:
            order[:2] = [1, 0]
        self.order, self.kept, self.axis = order, kept, axis
        self.got = flip(sent, axis, 1 << order[0])

    def advance(self, *others):
        got = after(self.got, *others) if others else self.got
        self.order = self.order[1:]
        if not self.order:
            return self.kept + got.astype(f32)
        half = got.shape[0] // 2
        sent = (self.kept[half:] + got[half:].astype(f32)).astype(bf16)
        self.kept = self.kept[:half] + got[:half].astype(f32)
        self.got = flip(sent, self.axis, 1 << self.order[0])
        return sent

    def finish(self, *others):
        while self.order:
            total = self.advance(*others)
        return total


def product_kernel(groups, rank, *refs):
    kept, sent = refs[-2:]
    step = pl.program_id(0)
    first, at = 0, 0
    for pairs, widths in groups:
        per = 1 + len(widths)
        for j, width in enumerate(widths):
            total = 0.0
            for p in range(pairs):
                left, right = refs[first + p * per], refs[first + p * per + 1 + j]
                total = total + dot_tn(left[...], right[...])
            cols = slice(at, at + width)
            at += width

            @pl.when(step < 2)
            def _(total=total, cols=cols):
                sent[:, cols] = total.astype(bf16)

            @pl.when(step >= 2)
            def _(total=total, cols=cols):
                kept[:, cols] = total

        first += pairs * per


def product(token, groups, swap):
    width = groups[0][0][0].shape[1]
    quarter = width // 4

    def place(i):
        return (2 * i + 1) % 5 if swap else (i + 2) % 4

    specs, operands, shapes, total, flops = [], [], [], 0, 0
    for pairs in groups:
        widths = [array.shape[1] for array, _ in pairs[0][1]]
        shapes.append((len(pairs), widths))
        total += sum(widths)
        for left, rights in pairs:
            lines = left.shape[0]
            flops += 2 * lines * width * sum(widths)
            specs.append(pl.BlockSpec((lines, quarter), lambda i, r: (0, place(i))))
            operands.append(left)
            for array, block in rights:
                specs.append(
                    pl.BlockSpec((lines, array.shape[1]), lambda i, r, block=block: (block, 0))
                )
                operands.append(array)
    return pl.pallas_call(
        functools.partial(product_kernel, shapes),
        grid_spec=pltpu.PrefetchScalarGridSpec(
            num_scalar_prefetch=1,
            grid=(4,),
            in_specs=specs,
            out_specs=[
                pl.BlockSpec((quarter, total), lambda i, r: (jnp.maximum(i - 2, 0), 0)),
                pl.BlockSpec((quarter, total), lambda i, r: (jnp.minimum(i, 1), 0)),
            ],
        ),
        out_shape=[
            jax.ShapeDtypeStruct((2 * quarter, total), f32),
            jax.ShapeDtypeStruct((2 * quarter, total), bf16),
        ],
        cost_estimate=cost(flops, 8 * width * total, 0),
        name="weight_product",
    )(token, *operands)


def pack_kernel(chans, x, step, z, q, k, v, pack_x, pack_z, turned):
    pack_x[:, :chans] = x[...].astype(bf16)
    turned[...] = jnp.zeros_like(turned)
    turned[: step.shape[0]] = step[...]
    pack_x[:, chans:] = jnp.transpose(turned[...]).astype(bf16)
    pack_z[:, :chans] = z[...].astype(bf16)
    pack_z[:, chans : chans + q.shape[1]] = q[...].astype(bf16)
    both = jnp.concatenate([k[...], v[...]], axis=0)
    pack_z[:, chans + q.shape[1] :] = jnp.transpose(both).astype(bf16)


def pack_early(x, step, z, q, k, v):
    lines, chans = x.shape
    cols = chans + q.shape[1] + k.shape[0] + v.shape[0]
    return pl.pallas_call(
        functools.partial(pack_kernel, chans),
        out_shape=[
            jax.ShapeDtypeStruct((lines, chans + 128), bf16),
            jax.ShapeDtypeStruct((lines, cols), bf16),
        ],
        scratch_shapes=[pltpu.VMEM((128, lines), f32)],
        cost_estimate=cost(0, lines * 7000, 0),
        name="pack_weights",
    )(x, step, z, q, k, v)


def move_kernel(back, order, me, source, target):
    width = source.shape[1] // len(order)
    for p, k in enumerate(order):
        there = pl.ds(pl.multiple_of((me[0] ^ k) * width, width), width)
        here = slice(p * width, (p + 1) * width)
        if back:
            target[:, there] = source[:, here]
        else:
            target[:, here] = source[:, there]


def final_kernel(order, me, u_own, u_other, gain, source, g_r1, target):
    width = source.shape[1] // len(order)
    step = 32
    for i in range(source.shape[0] // step):
        rows = slice(i * step, (i + 1) * step)
        x = source[rows].astype(f32)
        e = (u_own[rows].astype(f32) + u_other[rows].astype(f32)) * gain[...]
        rho = lax.rsqrt(jnp.mean(x * x, axis=1, keepdims=True) + epsilon)
        n = x * rho
        inner = jnp.mean(e * n, axis=1, keepdims=True)
        out = (g_r1[rows] + rho * (e - n * inner)).astype(bf16)
        for p, k in enumerate(order):
            there = pl.ds(pl.multiple_of((me[0] ^ k) * width, width), width)
            target[rows, there] = out[:, p * width : (p + 1) * width]


def final_gradient(member, size, u02, u_other, gain, x02, g_r1):
    shape = u_other.shape
    moved = shape[1] // size % 128 == 0
    result = pl.pallas_call(
        functools.partial(final_kernel, relative_order(size) if moved else [0]),
        grid_spec=pltpu.PrefetchScalarGridSpec(
            num_scalar_prefetch=1,
            grid=(1,),
            in_specs=[whole(shape), whole(shape), whole((1, shape[1])), whole(shape), whole(shape)],
            out_specs=whole(shape),
        ),
        out_shape=jax.ShapeDtypeStruct(shape, bf16),
        cost_estimate=cost(10**7, 10**7, 0),
        name="input_gradient",
    )(
        member.reshape(1) if moved else jnp.zeros((1,), jnp.int32),
        u02, u_other, gain.reshape(1, -1), x02, g_r1,
    )
    return result if moved else take_blocks(result, member, size, True)


def move_blocks(value, member, size, back):
    width = value.shape[1] // size
    if width % 128 == 0:
        return pl.pallas_call(
            functools.partial(move_kernel, back, relative_order(size)),
            grid_spec=pltpu.PrefetchScalarGridSpec(
                num_scalar_prefetch=1,
                grid=(1,),
                in_specs=[whole(value.shape)],
                out_specs=whole(value.shape),
            ),
            out_shape=jax.ShapeDtypeStruct(value.shape, value.dtype),
            cost_estimate=cost(0, 2 * value.size * value.dtype.itemsize, 0),
            name="move_blocks",
        )(member.reshape(1), value)
    return take_blocks(value, member, size, back)


def take_blocks(value, member, size, back):
    order = relative_order(size)
    where = [0] * size
    for p, k in enumerate(order):
        where[k] = p
    if back:
        index = jnp.array(where, jnp.int32)[member ^ jnp.arange(size, dtype=jnp.int32)]
    else:
        index = member ^ jnp.array(order, jnp.int32)
    cut = value.reshape(value.shape[0], size, -1)
    return jnp.take(cut, index, axis=1).reshape(value.shape)


def pick(bit, one, zero):
    return jnp.where(bit == 1, one, zero)


def after(value, *others):
    return lax.optimization_barrier((value,) + others)[0]


def flip_core(value):
    return flip(value, "tensor", 1)


def flip_y(value):
    return flip(value, "tensor", 2)


def in_rank_order(own, y, core):
    other = flip_y(own)
    pair = jnp.stack([pick(y, other, own), pick(y, own, other)])
    other = flip_core(pair)
    both = jnp.stack([pick(core, other, pair), pick(core, pair, other)], axis=1)
    return both.reshape((4,) + own.shape)


def add_low(kept, got):
    return lax.optimization_barrier((kept.astype(f32) + got.astype(f32)).astype(bf16))


def core_sum(kept, sent):
    return add_low(kept, flip_core(sent.astype(bf16)))


def y_sum(kept, sent):
    return kept.astype(f32) + flip_y(sent).astype(f32)


CHUNK = 128
HEAD = 64
TAPS = 4


def dot_nn(a, b):
    return lax.dot_general(a, b, (((1,), (0,)), ((), ())), preferred_element_type=f32)


def dot_nt(a, b):
    return lax.dot_general(a, b, (((1,), (1,)), ((), ())), preferred_element_type=f32)


def dot_tn(a, b):
    return lax.dot_general(a, b, (((0,), (0,)), ((), ())), preferred_element_type=f32)


def dot_exact(a, b):
    return lax.dot_general(
        a, b, (((1,), (0,)), ((), ())), precision=HIGHEST, preferred_element_type=f32
    )


def iota(shape, axis):
    return lax.broadcasted_iota(jnp.int32, shape, axis)


def earlier(tail, block, back):
    if back == 0:
        return block
    return pltpu.roll(jnp.concatenate([tail, block], axis=0), back, 0)[8:]


def later(block, head, ahead):
    if ahead == 0:
        return block
    both = jnp.concatenate([block, head], axis=0)
    return pltpu.roll(both, both.shape[0] - ahead, 0)[: block.shape[0]]


def conv_rows(tail, block, taps):
    total = block * taps[TAPS - 1 : TAPS] + taps[TAPS : TAPS + 1]
    for j in range(TAPS - 1):
        total = total + earlier(tail, block, TAPS - 1 - j) * taps[j : j + 1]
    return total


def conv_rows_back(grad, head, taps):
    total = grad * taps[TAPS - 1 : TAPS]
    for j in range(TAPS - 1):
        total = total + later(grad, head, TAPS - 1 - j) * taps[j : j + 1]
    return total


def conv_taps_back(tail, block, grad):
    rows = [
        jnp.sum(earlier(tail, block, TAPS - 1 - j) * grad, axis=0, keepdims=True)
        for j in range(TAPS)
    ]
    rows.append(jnp.sum(grad, axis=0, keepdims=True))
    rows.append(jnp.zeros((8 - len(rows), grad.shape[1]), f32))
    return jnp.concatenate(rows, axis=0)


def head_columns(columns, heads):
    rows = columns.shape[0]
    low = iota((rows, 2 * HEAD), 1) < HEAD
    return jnp.concatenate(
        [
            jnp.where(low, columns[:, h : h + 1], columns[:, h + 1 : h + 2])
            for h in range(0, heads, 2)
        ],
        axis=1,
    )


def head_sums(values, heads):
    rows = values.shape[0]
    low = iota((rows, 2 * HEAD), 1) < HEAD
    sums = []
    for pair in range(heads // 2):
        part = values[:, pair * 2 * HEAD : (pair + 1) * 2 * HEAD]
        sums.append(jnp.sum(jnp.where(low, part, 0.0), axis=1, keepdims=True))
        sums.append(jnp.sum(jnp.where(low, 0.0, part), axis=1, keepdims=True))
    return sums


def softplus(value):
    return jnp.maximum(value, 0.0) + jnp.log1p(jnp.exp(-jnp.abs(value)))


def step_rows(pdt, vec):
    size = pdt.shape[1]
    raw = pdt + vec[:, 0:1]
    dt = softplus(raw)
    rate = -jnp.exp(vec[:, 1:2])
    upper = (iota((size, size), 0) <= iota((size, size), 1)).astype(f32)
    logs = dot_exact(dt * rate, upper)
    last = logs[:, size - 1 : size]
    return raw, dt, rate, logs, jnp.exp(logs), jnp.exp(last - logs), jnp.exp(last)


def mamba_fwd_kernel(
    heads,
    rank,
    px,
    px_tail,
    pz,
    pbc,
    pbc_tail,
    pdt,
    taps,
    shared_taps,
    vec,
    om,
    kept,
    states,
    state,
):
    step = pl.program_id(0)

    @pl.when(step == 0)
    def _():
        state[...] = jnp.zeros_like(state)

    started = jnp.where(step == 0, 0.0, 1.0)
    u = conv_rows(px_tail[...] * started, px[...], taps[...])
    u = u * jax.nn.sigmoid(u)
    bc = conv_rows(pbc_tail[...] * started, pbc[...], shared_taps[...])
    bc = (bc * jax.nn.sigmoid(bc)).astype(bf16)
    half = bc.shape[1] // 2
    b_in, c_out = bc[:, :half], bc[:, half:]
    _, dt, _, logs, grow, fade, last = step_rows(pdt[...], vec[...])
    columns = jnp.transpose(jnp.concatenate([logs, grow, fade * dt, dt], axis=0))
    size = u.shape[0]
    causal = iota((size, size), 0) >= iota((size, size), 1)
    mixing = dot_nt(c_out, b_in)
    u_low = u.astype(bf16)
    low = iota((size, 2 * HEAD), 1) < HEAD
    local = []
    for pair in range(heads // 2):
        piece = u_low[:, pair * 2 * HEAD : (pair + 1) * 2 * HEAD]
        outs = []
        for h in (2 * pair, 2 * pair + 1):
            spread = jnp.where(causal, columns[:, h : h + 1] - logs[h : h + 1], -1e30)
            matrix = (mixing * jnp.exp(spread) * dt[h : h + 1]).astype(bf16)
            outs.append(dot_nn(matrix, piece))
        local.append(jnp.where(low, outs[0], outs[1]))
    before = state[...]
    states[0] = before
    carried = dot_nn(c_out, before.astype(bf16)) * head_columns(columns[:, 8:16], heads)
    skip = head_columns(jnp.transpose(jnp.broadcast_to(vec[:, 2:3], (8, size))), heads)
    total = jnp.concatenate(local, axis=1) + carried + skip * u
    z = pz[...]
    om[...] = (total * (z * jax.nn.sigmoid(z))).astype(bf16)
    kept[...] = total.astype(bf16)
    fed = (u * head_columns(columns[:, 16:24], heads)).astype(bf16)
    end = head_columns(jnp.transpose(jnp.broadcast_to(last, (8, 128))), heads)[:1]
    state[...] = before * end + dot_tn(b_in, fed)


def mamba_bwd_kernel(
    heads,
    rank,
    px,
    px_tail,
    pz,
    pbc,
    pbc_tail,
    pdt,
    taps,
    shared_taps,
    vec,
    states,
    gym,
    g_pxs,
    g_pbc,
    g_taps,
    g_shared,
    g_vec,
    g_skip,
    d_state,
    next_px,
    next_bc,
):
    step = pl.program_id(0)
    steps = pl.num_programs(0)

    @pl.when(step == 0)
    def _():
        d_state[...] = jnp.zeros_like(d_state)
        next_px[...] = jnp.zeros_like(next_px)
        next_bc[...] = jnp.zeros_like(next_bc)
        g_taps[...] = jnp.zeros_like(g_taps)
        g_shared[...] = jnp.zeros_like(g_shared)
        g_vec[...] = jnp.zeros_like(g_vec)
        g_skip[...] = jnp.zeros_like(g_skip)

    started = jnp.where(step == steps - 1, 0.0, 1.0)
    size = px.shape[0]
    tail_x = px_tail[...] * started
    block_x = px[...]
    pre_u = conv_rows(tail_x, block_x, taps[...])
    sig_u = jax.nn.sigmoid(pre_u)
    u = pre_u * sig_u
    tail_bc = pbc_tail[...] * started
    block_bc = pbc[...]
    pre_bc = conv_rows(tail_bc, block_bc, shared_taps[...])
    sig_bc = jax.nn.sigmoid(pre_bc)
    bc = (pre_bc * sig_bc).astype(bf16)
    half = bc.shape[1] // 2
    b_in, c_out = bc[:, :half], bc[:, half:]
    raw, dt, rate, logs, grow, fade, last = step_rows(pdt[...], vec[...])
    columns = jnp.transpose(jnp.concatenate([logs, grow, fade, dt], axis=0))
    z = pz[...]
    sig_z = jax.nn.sigmoid(z)
    g = gym[...]
    dy = g * (z * sig_z)
    dy_low = dy.astype(bf16)
    u_low = u.astype(bf16)
    before = states[0]
    before_low = before.astype(bf16)
    d_after = d_state[...]
    d_after_low = d_after.astype(bf16)
    causal = iota((size, size), 0) <= iota((size, size), 1)
    mixing = dot_nt(b_in, c_out)
    low = iota((size, 2 * HEAD), 1) < HEAD
    d_mixing = jnp.zeros((size, size), f32)
    du_local, col_sums, row_sums = [], [], []
    for pair in range(heads // 2):
        lanes = slice(pair * 2 * HEAD, (pair + 1) * 2 * HEAD)
        u_piece, dy_piece = u_low[:, lanes], dy_low[:, lanes]
        outs = []
        for h in (2 * pair, 2 * pair + 1):
            dt_col = columns[:, 24 + h : 25 + h]
            spread = jnp.where(causal, logs[h : h + 1] - columns[:, h : h + 1], -1e30)
            decay = jnp.exp(spread)
            keep = low if h % 2 == 0 else jnp.logical_not(low)
            masked = jnp.where(keep, u_piece, jnp.zeros_like(u_piece))
            product = dot_nt(masked, dy_piece) * decay
            d_mixing = d_mixing + product * dt_col
            product = product * mixing
            col_sums.append(jnp.sum(product, axis=1, keepdims=True))
            row_sums.append(jnp.sum(product * dt_col, axis=0, keepdims=True))
            outs.append(dot_nn((mixing * decay).astype(bf16), dy_piece))
        du_local.append(jnp.where(low, outs[0], outs[1]))
    grow_all = head_columns(columns[:, 8:16], heads)
    fade_all = head_columns(columns[:, 16:24], heads)
    dt_all = head_columns(columns[:, 24:32], heads)
    dy_grown = dy * grow_all
    dy_grown_low = dy_grown.astype(bf16)
    fed_low = (u * fade_all * dt_all).astype(bf16)
    back = dot_nn(b_in, d_after_low) * fade_all
    inter = head_sums(dy_grown * dot_nn(c_out, before_low), heads)
    tails = head_sums(u * back, heads)
    skip = head_columns(jnp.transpose(jnp.broadcast_to(vec[:, 2:3], (8, size))), heads)
    du = (jnp.concatenate(du_local, axis=1) + back) * dt_all + skip * dy
    d_mixing_low = d_mixing.astype(bf16)
    db = dot_nn(d_mixing_low, c_out) + dot_nt(fed_low, d_after_low)
    dc = dot_tn(d_mixing_low, b_in) + dot_nt(dy_grown_low, before_low)
    end = head_columns(jnp.transpose(jnp.broadcast_to(last, (8, 128))), heads)[:1]
    ended = d_after * end
    ends = head_sums(jnp.sum(ended * before, axis=0, keepdims=True), heads)
    d_state[...] = ended + dot_tn(c_out, dy_grown_low)
    lane = iota((size, 128), 1)
    gathered = jnp.zeros((size, 128), f32)
    for h in range(heads):
        gathered = jnp.where(lane == h, col_sums[h] + tails[h], gathered)
        gathered = jnp.where(lane == 8 + h, tails[h], gathered)
        gathered = jnp.where(lane == 16 + h, inter[h], gathered)
    turned = jnp.transpose(gathered)
    direct, tail_row, inter_row = turned[0:8], turned[8:16], turned[16:24]
    pad = [jnp.zeros((1, size), f32)] * (8 - heads)
    row_sum = jnp.concatenate(row_sums + pad, axis=0)
    zero = jnp.zeros((1, 1), f32)
    end_col = jnp.concatenate(ends + [zero] * (8 - heads), axis=0)
    d_logs = row_sum + inter_row - dt * direct
    at_last = end_col + jnp.sum(dt * tail_row, axis=1, keepdims=True)
    lower = (iota((size, size), 0) >= iota((size, size), 1)).astype(f32)
    d_rate = dot_exact(d_logs, lower) + at_last
    d_dt = direct + rate * d_rate
    d_raw = d_dt * jax.nn.sigmoid(raw)
    spread_rows = jnp.concatenate([d_raw, jnp.zeros((120, size), f32)], axis=0)
    g_pxs[:, u.shape[1] :] = jnp.transpose(spread_rows).astype(bf16)
    g_vec[0:8] += d_raw
    g_vec[8:16] += rate * dt * d_rate
    g_skip[...] += jnp.sum((dy * u).reshape(size // 8, 8, u.shape[1]), axis=0)
    d_pre = du * (sig_u * (1.0 + pre_u * (1.0 - sig_u)))
    g_pxs[:, : u.shape[1]] = conv_rows_back(d_pre, next_px[...], taps[...]).astype(bf16)
    g_taps[...] += conv_taps_back(tail_x, block_x, d_pre)
    next_px[...] = d_pre[:8]
    d_bc = jnp.concatenate([db, dc], axis=1) * (sig_bc * (1.0 + pre_bc * (1.0 - sig_bc)))
    g_pbc[...] = conv_rows_back(d_bc, next_bc[...], shared_taps[...]).astype(bf16)
    g_shared[...] += conv_taps_back(tail_bc, block_bc, d_bc)
    next_bc[...] = d_bc[:8]


def pad_rows(value):
    return jnp.pad(value, ((0, -value.shape[0] % 8), (0, 0)))


def vec_of(step_bias, decay_log, skip_gain):
    table = jnp.stack([step_bias, decay_log, skip_gain], axis=1)
    return jnp.pad(table, ((0, 8 - table.shape[0]), (0, 128 - table.shape[1])))


def whole(shape):
    return pl.BlockSpec(shape, lambda i, r: tuple(0 for _ in shape))


def cost(flops, moved, exps):
    return pl.CostEstimate(flops=flops, bytes_accessed=moved, transcendentals=exps)


def chunk_specs(length, ranks, order):
    per_block = length // ranks // CHUNK
    per = CHUNK // 8

    def place(i, r):
        c = order(i)
        return ((c // per_block) ^ r[0]) * per_block + c % per_block

    def at(cols):
        return pl.BlockSpec((CHUNK, cols), lambda i, r: (place(i, r), 0))

    def tail(cols):
        def index(i, r):
            c = jnp.maximum(order(i) - 1, 0)
            return ((((c // per_block) ^ r[0]) * per_block + c % per_block) * per + per - 1, 0)

        return pl.BlockSpec((8, cols), index)

    row = pl.BlockSpec((8, CHUNK), lambda i, r: (0, place(i, r)))
    return at, tail, row


def mamba_fwd(rank, px, pz, pbc, pdt, taps, shared_taps, vec, heads, ranks):
    length, chans = px.shape
    wide = pbc.shape[1]
    steps = length // CHUNK
    at, tail, row = chunk_specs(length, ranks, lambda i: i)
    return pl.pallas_call(
        functools.partial(mamba_fwd_kernel, heads),
        grid_spec=pltpu.PrefetchScalarGridSpec(
            num_scalar_prefetch=1,
            grid=(steps,),
            in_specs=[
                at(chans),
                tail(chans),
                at(chans),
                at(wide),
                tail(wide),
                row,
                whole((8, chans)),
                whole((8, wide)),
                whole((8, 128)),
            ],
            out_specs=[
                at(chans),
                at(chans),
                pl.BlockSpec((1, wide // 2, chans), lambda i, r: (i, 0, 0)),
            ],
            scratch_shapes=[pltpu.VMEM((wide // 2, chans), f32)],
        ),
        out_shape=[
            jax.ShapeDtypeStruct((length, chans), bf16),
            jax.ShapeDtypeStruct((length, chans), bf16),
            jax.ShapeDtypeStruct((steps, wide // 2, chans), f32),
        ],
        cost_estimate=cost(4 * 10**9, 8 * 10**6, 10**6),
        name="mamba_forward",
    )(rank, px, px, pz, pbc, pbc, pdt, taps, shared_taps, vec)


def mamba_bwd(rank, px, pz, pbc, pdt, taps, shared_taps, vec, states, gym, heads, ranks):
    length, chans = px.shape
    wide = pbc.shape[1]
    steps = length // CHUNK
    at, tail, row = chunk_specs(length, ranks, lambda i: steps - 1 - i)
    return pl.pallas_call(
        functools.partial(mamba_bwd_kernel, heads),
        grid_spec=pltpu.PrefetchScalarGridSpec(
            num_scalar_prefetch=1,
            grid=(steps,),
            in_specs=[
                at(chans),
                tail(chans),
                at(chans),
                at(wide),
                tail(wide),
                row,
                whole((8, chans)),
                whole((8, wide)),
                whole((8, 128)),
                pl.BlockSpec((1, wide // 2, chans), lambda i, r: (steps - 1 - i, 0, 0)),
                at(chans),
            ],
            out_specs=[
                at(chans + 128),
                at(wide),
                whole((8, chans)),
                whole((8, wide)),
                whole((16, 128)),
                whole((8, chans)),
            ],
            scratch_shapes=[
                pltpu.VMEM((wide // 2, chans), f32),
                pltpu.VMEM((8, chans), f32),
                pltpu.VMEM((8, wide), f32),
            ],
        ),
        out_shape=[
            jax.ShapeDtypeStruct((length, chans + 128), bf16),
            jax.ShapeDtypeStruct((length, wide), bf16),
            jax.ShapeDtypeStruct((8, chans), f32),
            jax.ShapeDtypeStruct((8, wide), f32),
            jax.ShapeDtypeStruct((16, 128), f32),
            jax.ShapeDtypeStruct((8, chans), f32),
        ],
        cost_estimate=cost(9 * 10**9, 10**7, 10**6),
        name="mamba_backward",
    )(rank, px, px, pz, pbc, pbc, pdt, taps, shared_taps, vec, states, gym)


ROWS = 256


def turn(pre, cosine, sine):
    inner = iota(pre.shape, 1) % HEAD < HEAD // 2
    lanes = pre.shape[1]
    other = jnp.where(
        inner, pltpu.roll(pre, lanes - HEAD // 2, 1), pltpu.roll(pre, HEAD // 2, 1)
    )
    return pre * cosine + other * sine


def attend_fwd_kernel(scale, rank, qkv, cosine, sine, out, q, k, v):
    length, wide = out.shape
    blocks = length // ROWS
    low = iota((ROWS, 2 * HEAD), 1) < HEAD
    load_qkv(rank, qkv, cosine, sine, q, k, v)
    for i in range(blocks):
        seen = (i + 1) * ROWS
        block = q[i * ROWS : (i + 1) * ROWS]
        keys, values = k[:seen], v[:seen]
        allowed = iota((ROWS, seen), 1) <= iota((ROWS, seen), 0) + i * ROWS
        outs = []
        for h in range(2):
            keep = low if h == 0 else jnp.logical_not(low)
            part = jnp.where(keep, block, jnp.zeros_like(block))
            scores = jnp.where(allowed, dot_nt(part, keys) * scale, -1e30)
            expo = jnp.exp(scores - jnp.max(scores, axis=1, keepdims=True))
            chance = expo * (1.0 / jnp.sum(expo, axis=1, keepdims=True))
            outs.append(dot_nn(chance.astype(bf16), values))
        out[relative_rows(rank, i)] = jnp.where(low, outs[0], outs[1]).astype(bf16)


def relative_rows(rank, i):
    return pl.ds(pl.multiple_of((i ^ rank[0]) * ROWS, ROWS), ROWS)


def load_qkv(rank, qkv, cosine, sine, q, k, v):
    wide = q.shape[1]
    for i in range(q.shape[0] // ROWS):
        rows = slice(i * ROWS, (i + 1) * ROWS)
        piece = qkv[relative_rows(rank, i)]
        q[rows] = turn(piece[:, :wide], cosine[rows], sine[rows]).astype(bf16)
        both = piece[:, wide:]
        turned = pltpu.roll(both, HEAD, 1)
        low = iota(both.shape, 1) < HEAD
        k[rows] = turn(jnp.where(low, both, turned), cosine[rows], sine[rows]).astype(bf16)
        v[rows] = jnp.where(low, turned, both).astype(bf16)


def attend_bwd_kernel(scale, rank, qkv, cosine, sine, go, g_qkv, q, k, v, dk, dv):
    length, wide = dk.shape
    blocks = length // ROWS
    low = iota((ROWS, 2 * HEAD), 1) < HEAD
    load_qkv(rank, qkv, cosine, sine, q, k, v)
    dk[...] = jnp.zeros_like(dk)
    dv[...] = jnp.zeros_like(dv)
    for i in range(blocks):
        seen = (i + 1) * ROWS
        rows = slice(i * ROWS, (i + 1) * ROWS)
        block, grads = q[rows], go[relative_rows(rank, i)]
        keys, values = k[:seen], v[:seen]
        allowed = iota((seen, ROWS), 0) <= iota((seen, ROWS), 1) + i * ROWS
        dqs, dks, dvs = [], [], []
        for h in range(2):
            keep = low if h == 0 else jnp.logical_not(low)
            part = jnp.where(keep, block, jnp.zeros_like(block))
            part_g = jnp.where(keep, grads, jnp.zeros_like(grads))
            scores = jnp.where(allowed, dot_nt(keys, part) * scale, -1e30)
            expo = jnp.exp(scores - jnp.max(scores, axis=0, keepdims=True))
            chance = expo * (1.0 / jnp.sum(expo, axis=0, keepdims=True))
            g_chance = dot_nt(values, part_g)
            center = jnp.sum(chance * g_chance, axis=0, keepdims=True)
            g_scores = (chance * (g_chance - center)).astype(bf16)
            dqs.append(dot_tn(g_scores, keys))
            dks.append(dot_nn(g_scores, part))
            dvs.append(dot_nn(chance.astype(bf16), part_g))
        dq = jnp.where(low, dqs[0], dqs[1]) * scale
        g_qkv[relative_rows(rank, i), :wide] = turn(dq, cosine[rows], -sine[rows]).astype(bf16)
        dk[:seen] += (dks[0] + dks[1]) * scale
        dv[:seen] += dvs[0] + dvs[1]
    for i in range(blocks):
        rows = slice(i * ROWS, (i + 1) * ROWS)
        g_k, g_v = dk[rows], dv[rows]
        g_k = turn(g_k + pltpu.roll(g_k, HEAD, 1), cosine[rows], -sine[rows])
        g_v = g_v + pltpu.roll(g_v, HEAD, 1)
        g_qkv[relative_rows(rank, i), wide:] = jnp.where(low, g_k, g_v).astype(bf16)


def attend_specs(length, wide):
    return [
        whole((length, 2 * wide)),
        whole((length, wide)),
        whole((length, wide)),
    ], [pltpu.VMEM((length, wide), bf16)] * 3


def attend_fwd(rank, qkv, cosine, sine):
    length, wide = cosine.shape
    ins, scratch = attend_specs(length, wide)
    return pl.pallas_call(
        functools.partial(attend_fwd_kernel, HEAD**-0.5),
        grid_spec=pltpu.PrefetchScalarGridSpec(
            num_scalar_prefetch=1,
            grid=(1,),
            in_specs=ins,
            out_specs=whole((length, wide)),
            scratch_shapes=scratch,
        ),
        out_shape=jax.ShapeDtypeStruct((length, wide), bf16),
        cost_estimate=cost(2 * 10**9, 4 * 10**6, 10**6),
        name="attend_forward",
    )(rank, qkv, cosine, sine)


def attend_bwd(rank, qkv, cosine, sine, g_oa):
    length, wide = cosine.shape
    ins, scratch = attend_specs(length, wide)
    return pl.pallas_call(
        functools.partial(attend_bwd_kernel, HEAD**-0.5),
        grid_spec=pltpu.PrefetchScalarGridSpec(
            num_scalar_prefetch=1,
            grid=(1,),
            in_specs=ins + [whole((length, wide))],
            out_specs=whole((length, 2 * wide)),
            scratch_shapes=scratch + [pltpu.VMEM((length, wide), f32)] * 2,
        ),
        out_shape=jax.ShapeDtypeStruct((length, 2 * wide), bf16),
        cost_estimate=cost(4 * 10**9, 6 * 10**6, 10**6),
        name="attend_backward",
    )(rank, qkv, cosine, sine, g_oa)


def project_kernel(order, chans, scalars, even, odd, gain, *refs):
    w_x, w_z, w_bc, outs = refs[:4], refs[4:8], refs[8], refs[9:]
    a1, kept, px, pz, pbc, pdt, qkv = outs
    rows, width = even.shape
    block = width // len(order)
    is_even = pl.program_id(0) % 2 == 0
    step = 32

    def norm(source, keep):
        for i in range(rows // step):
            own = slice(i * step, (i + 1) * step)
            value = source[own].astype(f32)
            rho = lax.rsqrt(jnp.mean(value * value, axis=1, keepdims=True) + epsilon)
            for p, k in enumerate(order):
                there = pl.ds(pl.multiple_of((scalars[0] ^ k) * block, block), block)
                here = slice(p * block, (p + 1) * block)
                piece = source[own, there]
                a1[own, here] = (piece.astype(f32) * rho * gain[:, here]).astype(bf16)
                if keep:
                    kept[own, here] = piece

    @pl.when(is_even)
    def _():
        norm(even, True)

    @pl.when(jnp.logical_not(is_even))
    def _():
        norm(odd, False)

    quarter = width // 4
    parts = [a1[:, q * quarter : (q + 1) * quarter] for q in range(4)]
    px[...] = sum(dot_nn(part, w[:, :chans]) for part, w in zip(parts, w_x))
    steps = sum(
        lax.dot_general(
            w[:, chans:], part, (((0,), (1,)), ((), ())), preferred_element_type=f32
        )
        for part, w in zip(parts, w_x)
    )
    pdt[...] = steps[:8]
    pz[...] = sum(dot_nn(part, w[:, :chans]) for part, w in zip(parts, w_z))
    pbc[...] = dot_nn(a1[...], w_bc[...])
    qkv[...] = sum(dot_nn(part, w[:, chans:]) for part, w in zip(parts, w_z))


def project(scalars, even, odd, gain, w_x, w_z, w_bc, chans, size):
    rows, width = even.shape[0] // 2, even.shape[1]
    length = 4 * rows
    if width // size % 128:
        member = scalars[0]
        even = take_blocks(even, member, size, False)
        odd = take_blocks(odd, member, size, False)
        order = [0]
    else:
        order = relative_order(size)
    if len(order) == 1:
        scalars = jnp.zeros_like(scalars)

    def at(cols):
        return pl.BlockSpec((rows, cols), lambda i, r: (i, 0))

    def half(cols):
        return pl.BlockSpec((rows, cols), lambda i, r: (i // 2, 0))

    def shape(cols, kind, count=length):
        return jax.ShapeDtypeStruct((count, cols), kind)

    n2, low = w_bc.shape[1], w_z[0][0].shape[1] - chans
    return pl.pallas_call(
        functools.partial(project_kernel, order, chans),
        grid_spec=pltpu.PrefetchScalarGridSpec(
            num_scalar_prefetch=1,
            grid=(4,),
            in_specs=[half(width), half(width), whole((1, width))]
            + quarter_specs(w_x)
            + quarter_specs(w_z)
            + [whole(w_bc.shape)],
            out_specs=[
                at(width),
                half(width),
                at(chans),
                at(chans),
                at(n2),
                pl.BlockSpec((8, rows), lambda i, r: (0, i)),
                at(low),
            ],
        ),
        out_shape=[
            shape(width, bf16),
            shape(width, bf16, 2 * rows),
            shape(chans, f32),
            shape(chans, f32),
            shape(n2, f32),
            shape(length, f32, 8),
            shape(low, f32),
        ],
        cost_estimate=cost(3 * 10**9, 14 * 10**6, length),
        name="norm_project",
    )(scalars, even, odd, gain.reshape(1, -1), *arrays_of(w_x), *arrays_of(w_z), w_bc)


def mixer_kernel(chans, rank, om, oa, *refs):
    w_o, (kept, sent) = refs[:4], refs[4:]
    total = jnp.concatenate(
        [dot_nt(om[...], w[:, :chans]) + dot_nt(oa[...], w[:, chans:]) for w in w_o], axis=1
    )

    @pl.when(pl.program_id(0) % 2 == 0)
    def _():
        kept[...] = total

    @pl.when(pl.program_id(0) % 2 == 1)
    def _():
        sent[...] = total.astype(bf16)


def mixer_out(token, om, oa, w_o):
    rows, width = om.shape[0] // 4, 4 * w_o[0][0].shape[0]

    def at(cols):
        return pl.BlockSpec((rows, cols), lambda i, r: (i, 0))

    half = pl.BlockSpec((rows, width), lambda i, r: (i // 2, 0))
    return pl.pallas_call(
        functools.partial(mixer_kernel, om.shape[1]),
        grid_spec=pltpu.PrefetchScalarGridSpec(
            num_scalar_prefetch=1,
            grid=(4,),
            in_specs=[at(om.shape[1]), at(oa.shape[1])] + quarter_specs(w_o),
            out_specs=[half, half],
        ),
        out_shape=[
            jax.ShapeDtypeStruct((2 * rows, width), f32),
            jax.ShapeDtypeStruct((2 * rows, width), bf16),
        ],
        cost_estimate=cost(10**9, 7 * 10**6, 0),
        name="mixer_out",
    )(token, om, oa, *arrays_of(w_o))


def mixer_back_kernel(chans, rank, g0, g1, g2, g3, *refs):
    w_o = refs[:4]
    pz, kept, g_ym, g_oa, g_pz, total = refs[4:]
    quarter = g0.shape[1] // 4
    for k, piece in enumerate((g0, g1, g2, g3)):

        @pl.when(pl.program_id(0) == k)
        def _(piece=piece):
            total[...] = sum(
                dot_nn(piece[:, q * quarter : (q + 1) * quarter], w_o[q][...]) for q in range(4)
            )

    back = total[:, :chans]
    g_ym[...] = back
    g_oa[...] = total[:, chans:].astype(bf16)
    z = pz[...]
    sig = jax.nn.sigmoid(z)
    g_pz[...] = (back * kept[...].astype(f32) * (sig * (1.0 + z * (1.0 - sig)))).astype(bf16)


def mixer_back(token, g_m, w_o, pz, kept):
    rows, width = g_m[0].shape
    length, chans = pz.shape
    cols_o = w_o[0][0].shape[1]
    other = cols_o - chans

    def at(cols):
        return pl.BlockSpec((rows, cols), lambda i, r: (i, 0))

    return pl.pallas_call(
        functools.partial(mixer_back_kernel, chans),
        grid_spec=pltpu.PrefetchScalarGridSpec(
            num_scalar_prefetch=1,
            grid=(4,),
            in_specs=[whole((rows, width))] * 4 + quarter_specs(w_o) + [at(chans)] * 2,
            out_specs=[at(chans), at(other), at(chans)],
            scratch_shapes=[pltpu.VMEM((rows, cols_o), f32)],
        ),
        out_shape=[
            jax.ShapeDtypeStruct((length, chans), f32),
            jax.ShapeDtypeStruct((length, other), bf16),
            jax.ShapeDtypeStruct((length, chans), bf16),
        ],
        cost_estimate=cost(10**9, 9 * 10**6, 10**6),
        name="mixer_back",
    )(token, *g_m, *arrays_of(w_o), pz, kept)


def project_back_kernel(chans, rank, a1, g_pz, g_qkv, g_pxs, g_bc, *refs):
    w_x, w_z, w_bc = refs[:4], refs[4:8], refs[8]
    kept, sent, sums = refs[9:]
    step = pl.program_id(0)
    total = jnp.concatenate(
        [
            dot_nt(g_pz[...], wz[:, :chans])
            + dot_nt(g_qkv[...], wz[:, chans:])
            + dot_nt(g_pxs[...], wx[...])
            for wx, wz in zip(w_x, w_z)
        ],
        axis=1,
    ) + dot_nt(g_bc[...], w_bc[...])

    @pl.when(step == 0)
    def _():
        sums[...] = jnp.zeros_like(sums)

    rows, width = total.shape
    weighed = total * a1[...].astype(f32)
    sums[...] += jnp.sum(weighed.reshape(rows // 8, 8, width), axis=0)

    @pl.when(step % 2 == 0)
    def _():
        kept[...] = total

    @pl.when(step % 2 == 1)
    def _():
        sent[...] = total.astype(bf16)


def project_back(token, a1, g_pz, g_qkv, g_pxs, g_bc, w_x, w_z, w_bc):
    length, width = a1.shape
    chans = g_pz.shape[1]
    rows = length // 4

    def at(cols):
        return pl.BlockSpec((rows, cols), lambda i, r: (i, 0))

    half = pl.BlockSpec((rows, width), lambda i, r: (i // 2, 0))
    parts = (a1, g_pz, g_qkv, g_pxs, g_bc)
    return pl.pallas_call(
        functools.partial(project_back_kernel, chans),
        grid_spec=pltpu.PrefetchScalarGridSpec(
            num_scalar_prefetch=1,
            grid=(4,),
            in_specs=[at(item.shape[1]) for item in parts]
            + quarter_specs(w_x)
            + quarter_specs(w_z)
            + [whole(w_bc.shape)],
            out_specs=[half, half, whole((8, width))],
        ),
        out_shape=[
            jax.ShapeDtypeStruct((2 * rows, width), f32),
            jax.ShapeDtypeStruct((2 * rows, width), bf16),
            jax.ShapeDtypeStruct((8, width), f32),
        ],
        cost_estimate=cost(3 * 10**9, 11 * 10**6, 0),
        name="project_back",
    )(token, *parts, *arrays_of(w_x), *arrays_of(w_z), w_bc)


def rotary_tables(length):
    half = HEAD // 2
    frequency = rotary_base ** (-2.0 * jnp.arange(half, dtype=f32) / HEAD)
    angles = jnp.arange(length, dtype=f32)[:, None] * frequency[None, :]
    cosine, sine = jnp.cos(angles), jnp.sin(angles)
    return (
        jnp.concatenate([cosine] * 4, axis=1),
        jnp.concatenate([-sine, sine, -sine, sine], axis=1),
    )


def swiglu(gate_part, up_part):
    return jax.nn.silu(gate_part) * up_part


def mm(a, b):
    return jnp.dot(a, b, preferred_element_type=f32)


def mm_t(a, b):
    return lax.dot_general(a, b, (((1,), (1,)), ((), ())), preferred_element_type=f32)


def t_mm(a, b):
    return lax.dot_general(a, b, (((0,), (0,)), ((), ())), preferred_element_type=f32)


def body(
    layer_in,
    out_grad,
    lengths,
    mamba_x,
    mamba_z,
    mamba_step,
    query_proj,
    key_proj,
    value_proj,
    mamba_out,
    attend_out,
    mlp_gate,
    mlp_up,
    mlp_down,
    state_proj,
    conv_state,
    norm_gains,
    conv_mamba,
    step_bias,
    decay_log,
    skip_gain,
):
    ranks = lax.axis_size("tensor")
    assert ranks == 4 and layer_in.shape[1] == 1
    rank = lax.axis_index("tensor")
    y, core = rank // 2, rank % 2
    rank_ref = rank.reshape(1)
    peers = lax.axis_size("dp")
    me = lax.axis_index("dp")
    rows, _, width = layer_in.shape
    length = rows * ranks
    chans = mamba_x.shape[1]
    heads = step_bias.shape[0]
    q_cols, k_cols = query_proj.shape[1], key_proj.shape[1]
    ff = mlp_gate.shape[1]
    own_rows, n2 = state_proj.shape

    pack_x, pack_z = pack_early(
        mamba_x, mamba_step.T, mamba_z, query_proj, key_proj.T, value_proj.T
    )
    first = Gather(pack_x, "dp", False)
    second = Gather(pack_z, "dp", True)
    layer_in, conv_state, norm_gains, state_proj = lax.optimization_barrier(
        (layer_in, conv_state, norm_gains, state_proj, pack_x, pack_z)
    )[:4]
    raw_0 = layer_in[:, 0]
    raw_even = jnp.concatenate([raw_0, flip_y(raw_0)], axis=0)
    raw_odd = flip_core(raw_even)
    small = jnp.concatenate([conv_state.reshape(-1), norm_gains.reshape(-1)])
    parts = []
    rest = small
    for _ in range(3):
        parts.append(lax.reduce_precision(rest, 8, 7))
        rest = rest - parts[-1]
    parts = jnp.concatenate(parts)
    small_rows = -(-parts.shape[0] // n2)
    parts = jnp.pad(parts, (0, small_rows * n2 - parts.shape[0])).reshape(small_rows, n2)
    pack_s = jnp.concatenate([state_proj, parts], axis=0).astype(bf16)
    ranked = in_rank_order(pack_s, y, core)
    third = Gather(ranked.reshape(-1, n2), "dp", False)
    sent_x = first.until(2)
    sent_z = second.until(2)
    third.until(2, sent_x, sent_z)
    late = (mamba_out, attend_out, mlp_gate, mlp_up, mlp_down, conv_mamba)
    late = late + (step_bias, decay_log, skip_gain)
    late = lax.optimization_barrier(late + (sent_x, sent_z))[: len(late)]
    mamba_out, attend_out, mlp_gate, mlp_up, mlp_down, conv_mamba = late[:6]
    step_bias, decay_log, skip_gain = late[6:]
    pack_o = jnp.concatenate([mamba_out.T.astype(bf16), attend_out.T.astype(bf16)], axis=1)
    pack_m = jnp.concatenate(
        [mlp_gate.astype(bf16), mlp_up.astype(bf16), mlp_down.T.astype(bf16)], axis=1
    )
    far_x = first.advance()
    far_z = second.advance()
    third.advance(far_x, far_z)
    gather_m = Gather(after(pack_m, far_x, far_z), "dp", False, True)
    w_x = first.advance()
    gather_o = Gather(after(pack_o, arrays_of(w_x)[2]), "dp", True)
    w_z = second.advance()
    all_s = join_quarters(third.advance()).reshape(peers, ranks, own_rows + small_rows, n2)
    w_bc = all_s[:, :, :own_rows].reshape(width, n2)
    parts = all_s[:, :, own_rows:].reshape(peers, ranks, -1).astype(f32)
    count = small.shape[0]
    small = parts[..., :count] + parts[..., count : 2 * count] + parts[..., 2 * count : 3 * count]
    cut = conv_state.size
    taps_own = conv_state.shape[1]
    gains_own = norm_gains.shape[1]
    taps_rel = small[..., :cut].reshape(peers, ranks, conv_state.shape[0], taps_own)
    taps_rel = jnp.transpose(taps_rel, (2, 0, 1, 3)).reshape(conv_state.shape[0], -1)
    conv_shared = take_blocks(taps_rel, me, peers, True)
    gain_pair = jnp.transpose(
        small[..., cut:].reshape(peers, ranks, 2, gains_own), (2, 0, 1, 3)
    ).reshape(2, width)

    def rho_of(values):
        return lax.rsqrt(jnp.mean(values * values, axis=-1, keepdims=True) + epsilon)

    a1, x02, px, pz, pbc, pdt, qkv = project(
        me.reshape(1), raw_even, raw_odd, gain_pair[0], w_x, w_z, w_bc, chans, peers
    )
    x0, x2 = x02[:rows], x02[rows:]

    limit = lengths[0]

    def masked(block, k):
        place = (rank ^ k) * rows + jnp.arange(rows, dtype=jnp.int32)
        return jnp.where((place < limit)[:, None], block, jnp.zeros_like(block))

    gf0 = masked(move_blocks(after(out_grad, far_x, far_z)[:, 0], me, peers, False), 0)
    gf2 = flip_y(after(gf0, raw_even))

    sent_m = gather_m.until(2, pdt)
    sent_o = gather_o.until(2, pdt)
    cosine, sine = rotary_tables(length)
    oa = attend_fwd(after(rank_ref, sent_o, sent_m), qkv, cosine, sine)
    gf_odd = flip_core(jnp.concatenate([gf0, after(gf2, pdt)], axis=0))
    sent_o = gather_o.advance(oa)
    vec = vec_of(step_bias, decay_log, skip_gain)
    taps, shared_taps = pad_rows(conv_mamba), pad_rows(conv_shared)
    gf_odd = after(gf_odd, oa)
    om, kept, states = mamba_fwd(
        after(rank_ref, sent_o, gf_odd), px, pz, pbc, pdt, taps, shared_taps, vec, heads, ranks
    )
    w_o = gather_o.advance(om)
    gf1, gf3 = gf_odd[:rows], gf_odd[rows:]
    gf_a = jnp.concatenate([gf0, gf1], axis=0)
    gf_b = jnp.concatenate([gf2, gf3], axis=0)
    sent_m = gather_m.advance(om)
    m_kept, m_sent = mixer_out(after(rank_ref, sent_m, gather_m.cross), om, oa, w_o)
    s02 = add_low(m_kept, flip_core(m_sent))
    s0, s2 = s02[:rows], s02[rows:]
    w_m = gather_m.advance()
    m_got = after(flip_y(s2), *arrays_of(w_m))
    w_m = join_quarters(w_m)
    w_gu, w_dn = w_m[:, : 2 * ff], w_m[:, 2 * ff :]

    def second_norm(low_x, m):
        r1 = low_x.astype(f32) + m
        rho = rho_of(r1)
        return r1, rho, (r1 * rho * gain_pair[1]).astype(bf16)

    r1_0, rho_0, a2_0 = second_norm(x0, s0.astype(f32) + m_got.astype(f32))
    a2_1 = flip_core(a2_0)
    a2_a = jnp.concatenate([a2_0, a2_1], axis=0)
    m_other = after(flip_y(s0), a2_0)
    r1_2, rho_2, a2_2 = second_norm(x2, s2.astype(f32) + m_other.astype(f32))
    a2_3 = flip_core(a2_2)
    a2_b = jnp.concatenate([a2_2, a2_3], axis=0)

    def feed(a2, gf, *others):
        gate_up = mm(a2, w_gu)
        gate, up = gate_up[:, :ff], gate_up[:, ff:]
        hidden, glu_back = jax.vjp(swiglu, gate, up)
        hid = hidden.astype(bf16)
        gate_grad, up_grad = glu_back(mm(gf, w_dn))
        g_gu = jnp.concatenate([gate_grad.astype(bf16), up_grad.astype(bf16)], axis=1)
        if others:
            g_gu = after(g_gu, *others)
        return hid, g_gu, mm_t(g_gu, w_gu)

    hid_a, g_gu_a, g_a2_a = feed(a2_a, gf_a)
    t0 = core_sum(g_a2_a[:rows], g_a2_a[rows:])
    hid_b, g_gu_b, g_a2_b = feed(a2_b, gf_b, t0)
    t2 = core_sum(g_a2_b[:rows], g_a2_b[rows:])

    halves = ((0, 0), (0, 1), (1, 0), (1, 1))
    dn_kept, dn_sent = product(
        after(rank_ref, g_a2_b),
        [[(left, [((hid_a, hid_b)[p], b)]) for left, (p, b) in zip((gf0, gf1, gf2, gf3), halves)]],
        True,
    )
    dn = Sum(dn_kept, dn_sent, "dp", True)
    gu_kept, gu_sent = product(
        after(rank_ref, dn_sent),
        [
            [
                (left, [((g_gu_a, g_gu_b)[p], b)])
                for left, (p, b) in zip((a2_0, a2_1, a2_2, a2_3), halves)
            ]
        ],
        False,
    )
    gu = Sum(gu_kept, gu_sent, "dp", False)

    def second_back(g_a2, r1, rho, gf):
        n_two = r1 * rho
        e_two = g_a2 * gain_pair[1]
        inner = jnp.mean(e_two * n_two, axis=-1, keepdims=True)
        return gf.astype(f32) + rho * (e_two - n_two * inner)

    t0_got, t2_got = flip_y(t0), flip_y(t2)
    g_a2_2 = t2.astype(f32) + after(t0_got, t2, gu_sent).astype(f32)
    g_r1_2 = second_back(g_a2_2, r1_2, rho_2, gf2)
    g_m_2 = g_r1_2.astype(bf16)
    g_a2_0 = t0.astype(f32) + after(t2_got, gu_sent).astype(f32)
    g_r1_0 = second_back(g_a2_0, r1_0, rho_0, gf0)
    g_m_0 = g_r1_0.astype(bf16)
    gain_two_grad = jnp.sum(g_a2_0 * (r1_0 * rho_0), axis=0)
    g_m_3, g_m_1 = flip_core(g_m_2), flip_core(g_m_0)
    g_m = (g_m_0, g_m_1, g_m_2, g_m_3)
    g_ym, g_oa, g_pz = mixer_back(after(rank_ref, dn_sent, gu_sent), g_m, w_o, pz, kept)

    sent_dn = dn.advance(g_oa)
    hid_a, hid_b = lax.optimization_barrier((hid_a, hid_b, g_m_0))[:2]
    f_a, f_b = mm_t(hid_a, w_dn), mm_t(hid_b, w_dn)
    f_sent = jnp.concatenate([f_a[rows:], f_b[rows:]], axis=0).astype(bf16)
    f_got = flip_core(f_sent)
    g_qkv = attend_bwd(after(rank_ref, sent_dn, f_sent), qkv, cosine, sine, g_oa)
    sent_dn = dn.advance(g_qkv)
    sent_gu = gu.advance(g_qkv)
    f_kept = jnp.concatenate([f_a[:rows], f_b[:rows]], axis=0)
    f02 = add_low(f_kept, after(f_got, g_qkv))
    f_other = flip_y(f02[rows:])
    z_kept, z_sent = product(
        after(rank_ref, sent_dn, sent_gu, f02),
        [[(g_m[k], [(om, k), (oa, k)]) for k in range(4)], [(a1, [(g_pz, 0), (g_qkv, 0)])]],
        False,
    )
    z = Sum(z_kept, z_sent, "dp", False)
    sent_gu = gu.advance(z_sent)

    g_pxs, g_bc, g_taps, g_shared, g_vec, g_skip = mamba_bwd(
        after(rank_ref, z_sent, sent_gu),
        px, pz, pbc, pdt, taps, shared_taps, vec, states, g_ym, heads, ranks,
    )
    dn_sum, gu_sum = dn.finish(g_pxs), gu.finish(g_pxs)
    x_kept, x_sent = product(
        after(rank_ref, dn_sum, gu_sum), [[(a1, [(g_pxs, 0)])]], False
    )
    x = Sum(x_kept, x_sent, "dp", False)
    sent_z = z.advance(x_sent)
    g_kept, g_sent, g_sums = project_back(
        after(rank_ref, x_sent, sent_z), a1, g_pz, g_qkv, g_pxs, g_bc, w_x, w_z, w_bc
    )
    g_got = flip_core(g_sent)
    sent_x = x.advance(g_sums)
    sent_z = z.advance(g_sums)
    u02 = add_low(g_kept, after(g_got, sent_x, sent_z))
    u_other = flip_y(u02[rows:])
    gain_one_grad = jnp.sum(g_sums, axis=0) / gain_pair[0]
    state_part = t_mm(after(a1, x_sent), g_bc).reshape(peers, 2, 2, own_rows, n2)
    f_other = after(f_other, u02)

    g_taps, g_shared, g_vec, g_skip = lax.optimization_barrier(
        (g_taps, g_shared, g_vec, g_skip, g_sums)
    )[:4]
    conv_taps_grad = g_taps[: conv_mamba.shape[0]]
    conv_shared_grad = g_shared[: conv_state.shape[0]]
    bias_grad = jnp.sum(g_vec[:heads], axis=1)
    decay_grad = jnp.sum(g_vec[8 : 8 + heads], axis=1)
    skip_grad = jnp.sum(g_skip.reshape(8, heads, HEAD), axis=(0, 2))
    gain_grads = take_blocks(jnp.stack([gain_one_grad, gain_two_grad]), me, peers, True)

    def rows_of(items):
        flat = jnp.concatenate([item.reshape(-1) for item in items])
        return jnp.pad(flat, (0, -flat.shape[0] % (8 * n2))).reshape(-1, n2)

    both = rows_of([conv_shared_grad, gain_grads])
    only = rows_of([conv_taps_grad, bias_grad, decay_grad, skip_grad])

    def exchange(kept, sent, shared, axis, mask, *others):
        got = flip(jnp.concatenate([sent.reshape(-1, n2), shared], axis=0), axis, mask)
        got = after(got, *others)
        count = got.shape[0] - shared.shape[0]
        return kept + got[:count].reshape(kept.shape), shared + got[count:]

    by_core = pick(core, state_part[:, :, ::-1], state_part)
    state, both = exchange(by_core[:, :, 0], by_core[:, :, 1], both, "tensor", 1, u02)
    by_y = pick(y, state[:, ::-1], state)
    sent_x = x.advance(by_y)
    state, both = exchange(by_y[:, 0], by_y[:, 1], both, "tensor", 2, sent_x, sent_z)
    state = state.reshape(peers * own_rows, n2)
    shared = jnp.concatenate([both, only], axis=0)
    tie = (u_other,)
    for bit in range(bits_of(peers)):
        half = state.shape[0] // 2
        state, shared = exchange(state[:half], state[half:], shared, "dp", 1 << bit, *tie)
        if bit == 0:
            both_sum = z.finish(state)
            tie = (both_sum,)
        elif bit == 1:
            tie = ()
    state_proj_grad = state
    both_rows = both.shape[0]
    both = shared[:both_rows].reshape(-1)
    only = shared[both_rows:].reshape(-1)

    f_sum = f02[:rows].astype(f32) + f_other.astype(f32)
    layer_out = masked(r1_0 + f_sum, 0).astype(bf16)
    layer_out = move_blocks(layer_out, me, peers, True)[:, None]
    x_sum = x.finish()
    out_sum, z_sum = both_sum[:, : chans + q_cols], both_sum[:, chans + q_cols :]
    in_grad = final_gradient(after(me, both_sum), peers, u02, u_other, gain_pair[0], x02, g_r1_0)[:, None]

    conv_state_sum = both[: conv_state.size * peers * ranks].reshape(conv_shared.shape)
    gain_sum = both[conv_shared.size : conv_shared.size + 2 * width].reshape(2, width)
    member = me * ranks + rank
    conv_state_grad = lax.dynamic_slice_in_dim(conv_state_sum, member * taps_own, taps_own, 1)
    norm_gains_grad = lax.dynamic_slice_in_dim(gain_sum, member * gains_own, gains_own, 1)
    cut = conv_taps_grad.size
    conv_mamba_grad = only[:cut].reshape(conv_taps_grad.shape)
    step_bias_grad = only[cut : cut + heads]
    decay_log_grad = only[cut + heads : cut + 2 * heads]
    skip_gain_grad = only[cut + 2 * heads : cut + 3 * heads]

    return (
        layer_out,
        in_grad,
        x_sum[:, :chans],
        z_sum[:, :chans],
        x_sum[:, chans : chans + heads],
        z_sum[:, chans : chans + q_cols],
        z_sum[:, chans + q_cols : chans + q_cols + k_cols],
        z_sum[:, chans + q_cols + k_cols :],
        out_sum[:, :chans].T,
        out_sum[:, chans:].T,
        gu_sum[:, :ff],
        gu_sum[:, ff:],
        dn_sum.T,
        state_proj_grad,
        conv_state_grad,
        norm_gains_grad,
        conv_mamba_grad,
        step_bias_grad,
        decay_log_grad,
        skip_gain_grad,
    )


def solution(mesh):
    in_specs = (
        P("tensor", "dp", None),
        P("tensor", "dp", None),
        P("dp"),
        P("dp", "tensor"),
        P("dp", "tensor"),
        P("dp", "tensor"),
        P("dp", "tensor"),
        P("dp", "tensor"),
        P("dp", "tensor"),
        P("tensor", "dp"),
        P("tensor", "dp"),
        P("dp", "tensor"),
        P("dp", "tensor"),
        P("tensor", "dp"),
        P(("dp", "tensor"), None),
        P(None, ("dp", "tensor")),
        P(None, ("dp", "tensor")),
        P(None, "tensor"),
        P("tensor"),
        P("tensor"),
        P("tensor"),
    )
    out_specs = (
        P("tensor", "dp", None),
        P("tensor", "dp", None),
        P("dp", "tensor"),
        P("dp", "tensor"),
        P("dp", "tensor"),
        P("dp", "tensor"),
        P("dp", "tensor"),
        P("dp", "tensor"),
        P("tensor", "dp"),
        P("tensor", "dp"),
        P("dp", "tensor"),
        P("dp", "tensor"),
        P("tensor", "dp"),
        P(("dp", "tensor"), None),
        P(None, ("dp", "tensor")),
        P(None, ("dp", "tensor")),
        P(None, "tensor"),
        P("tensor"),
        P("tensor"),
        P("tensor"),
    )
    return jax.shard_map(body, mesh=mesh, in_specs=in_specs, out_specs=out_specs, check_vma=False)
```
